512 devices in a mesh: slab: 32 (over y, z_hi, x), shots: 16 (over z_lo, core).
Axes of the slice: x: 4, y: 4, z: 16 (z_hi: 2, z_lo: 8; z = z_hi * 8 + z_lo), core: 2. Of those that a mesh axis runs over, the one named last changes fastest.
Arguments:
- src_prev: float32 [32, 256, 64, 128], P('shots', 'slab'), may hold values from -6 to 6
- src_cur: float32 [32, 256, 64, 128], P('shots', 'slab'), may hold values from -6 to 6
- rcv_prev: float32 [32, 256, 64, 128], P('shots', 'slab'), may hold values from -6 to 6
- rcv_cur: float32 [32, 256, 64, 128], P('shots', 'slab'), may hold values from -6 to 6
- velocity: float32 [256, 64, 128], P('slab'), may hold values from 0.05 to 0.18
- wavelet: float32 [2, 32], P(None, 'shots'), may hold values from -6 to 6
- residual_traces: float32 [2, 32, 256], P(None, 'shots'), may hold values from -6 to 6
- source_depth: int32 [32], P('shots'), may hold values from 0 to 255
- source_y: int32 [32], P('shots'), may hold values from 21 to 42
- source_x: int32 [32], P('shots'), may hold values from 42 to 85
- half_y: int32 [32], P('shots'), may hold values from 10 to 21
- half_x: int32 [32], P('shots'), may hold values from 21 to 42
- receiver_cell: int32 [32, 256], P('shots'), may hold values from 0 to 2097151
Outputs:
- src_last: float32 [32, 256, 64, 128], P('shots', 'slab')
- rcv_last: float32 [32, 256, 64, 128], P('shots', 'slab')
- image: float32 [256, 64, 128], P('slab')
The draws below stay inside these ranges and needn't reach their ends.
All inputs are finite; a program needn't handle non-finite values.
Results may differ from the reference program's by a relative error of at most 0.0003.
Values sent between devices are 32-bit elements; how exact they have to be, the bound alone decides.
A program may use at most 64 MiB of HBM per device.

```python
import jax
import jax.numpy as jnp
from jax import lax

NY = 64
NX = 128
RCV = 256
STEPS = 2
NZ = 256
SHOTS = 32


def with_ends(entries, rng, low, high):
    longest = entries.shape.index(max(entries.shape))
    spots = []
    for shift in (0, 1):
        where = [jax.random.randint(jax.random.fold_in(rng, axis), (), 0, length) for axis, length in enumerate(entries.shape)]
        where[longest] = (where[longest] + shift) % entries.shape[longest]
        spots.append(tuple(where))
    return entries.at[spots[0]].set(low).at[spots[1]].set(high)


def block_scale(own_key, extent, shards, low, top_value):
    def one(dim, parts):
        heights = jax.random.uniform(jax.random.fold_in(jax.random.fold_in(own_key, 6), dim), (parts,), jnp.float32, low / len(shards), top_value / len(shards))
        return jnp.repeat(jnp.exp(heights), extent[dim] // parts).reshape((-1,) + (1,) * (len(extent) - dim - 1))

    level = one(*shards[0])
    for cut in shards[1:]:
        level = level * one(*cut)
    return level


def normal_values(stream_key, shape, spread, reach, pieces=(), kind=jnp.bfloat16):
    result = jax.random.normal(stream_key, shape, jnp.float32) * spread
    if len(pieces) > 0:
        result = block_scale(stream_key, shape, pieces, -0.22, 0.18) * result
    return jnp.clip(result, min=-reach, max=reach).astype(kind)


def setup_inputs(seed: int = 0) -> dict:
    streams_of = jax.random.split(jax.random.key(seed), 14)
    src_prev = normal_values(streams_of[0], (SHOTS, NZ, NY, NX), 1.0, 6.0, ((0, 16), (1, 32)), jnp.float32)
    src_cur = normal_values(streams_of[1], (SHOTS, NZ, NY, NX), 1.0, 6.0, ((0, 16), (1, 32)), jnp.float32)
    rcv_prev = normal_values(streams_of[2], (SHOTS, NZ, NY, NX), 1.0, 6.0, ((0, 16), (1, 32)), jnp.float32)
    rcv_cur = normal_values(streams_of[3], (SHOTS, NZ, NY, NX), 1.0, 6.0, ((0, 16), (1, 32)), jnp.float32)
    velocity = jnp.clip(0.05 + 0.13000001 * jax.random.uniform(streams_of[4], (NZ, NY, NX), jnp.float32) ** block_scale(streams_of[4], (NZ, NY, NX), ((0, 32),), -0.2, 0.2), 0.05, 0.18)
    wavelet = normal_values(streams_of[5], (STEPS, SHOTS), 1.0, 6.0, ((1, 16),), jnp.float32)
    residual_traces = normal_values(streams_of[6], (STEPS, SHOTS, RCV), 1.0, 6.0, ((1, 16),), jnp.float32)
    source_depth = with_ends(jax.random.randint(streams_of[7], (SHOTS,), 0, NZ), jax.random.fold_in(streams_of[7], 1), 0, NZ - 1).astype(jnp.int32)
    source_y = with_ends(jax.random.randint(streams_of[8], (SHOTS,), NY // 3, NY - NY // 3), jax.random.fold_in(streams_of[8], 1), NY // 3, (NY - NY // 3) - 1).astype(jnp.int32)
    source_x = with_ends(jax.random.randint(streams_of[9], (SHOTS,), NX // 3, NX - NX // 3), jax.random.fold_in(streams_of[9], 1), NX // 3, (NX - NX // 3) - 1).astype(jnp.int32)
    half_y = with_ends(jax.random.randint(streams_of[10], (SHOTS,), NY // 6, NY // 3 + 1), jax.random.fold_in(streams_of[10], 1), NY // 6, (NY // 3 + 1) - 1).astype(jnp.int32)
    half_x = with_ends(jax.random.randint(streams_of[11], (SHOTS,), NX // 6, NX // 3 + 1), jax.random.fold_in(streams_of[11], 1), NX // 6, (NX // 3 + 1) - 1).astype(jnp.int32)
    receiver_cell = with_ends(jax.random.randint(streams_of[12], (SHOTS, RCV), 0, NZ * NY * NX), jax.random.fold_in(streams_of[12], 1), 0, (NZ * NY * NX) - 1).astype(jnp.int32)
    return dict(src_prev=src_prev, src_cur=src_cur, rcv_prev=rcv_prev, rcv_cur=rcv_cur, velocity=velocity, wavelet=wavelet, residual_traces=residual_traces, source_depth=source_depth, source_y=source_y, source_x=source_x, half_y=half_y, half_x=half_x, receiver_cell=receiver_cell)


COEF = (-205.0 / 72.0, 8.0 / 5.0, -1.0 / 5.0, 8.0 / 315.0, -1.0 / 560.0)


def laplace(padded):
    axis_z = padded.ndim - 3
    length = padded.shape[axis_z] - 8
    center = lax.slice_in_dim(padded, 4, 4 + length, axis=axis_z)
    total = 3.0 * COEF[0] * center
    for shift_k in range(1, 5):
        upper = lax.slice_in_dim(padded, 4 + shift_k, 4 + shift_k + length, axis=axis_z)
        lower = lax.slice_in_dim(padded, 4 - shift_k, 4 - shift_k + length, axis=axis_z)
        total = total + COEF[shift_k] * (upper + lower)
    widths = [(0, 0)] * (center.ndim - 2) + [(4, 4), (4, 4)]
    plane = jnp.pad(center, widths)
    rows_y = center.shape[-2]
    cols_x = center.shape[-1]
    for shift_k in range(1, 5):
        side_y = plane[..., 4 + shift_k:4 + shift_k + rows_y, 4:4 + cols_x] + plane[..., 4 - shift_k:4 - shift_k + rows_y, 4:4 + cols_x]
        side_x = plane[..., 4:4 + rows_y, 4 + shift_k:4 + shift_k + cols_x] + plane[..., 4:4 + rows_y, 4 - shift_k:4 - shift_k + cols_x]
        total = total + COEF[shift_k] * (side_y + side_x)
    return total


def band_mask(source_y, source_x, half_y, half_x, rows_y, cols_x):
    grid_y = jnp.arange(rows_y, dtype=jnp.int32)
    grid_x = jnp.arange(cols_x, dtype=jnp.int32)
    inside_y = jnp.abs(grid_y[None, :, None] - source_y[:, None, None]) <= half_y[:, None, None]
    inside_x = jnp.abs(grid_x[None, None, :] - source_x[:, None, None]) <= half_x[:, None, None]
    return (inside_y & inside_x).astype(jnp.float32)


def inject(cells, values, begin, length, rows_y, cols_x):
    plane = rows_y * cols_x
    depth = cells // plane
    rest = cells - depth * plane
    local = depth - begin
    valid = (local >= 0) & (local < length)
    flat = jnp.where(valid, local * plane + rest, 0).astype(jnp.int32)
    amounts = jnp.where(valid, values, jnp.zeros_like(values))
    count = cells.shape[0]
    rows = jnp.broadcast_to(jnp.arange(count, dtype=jnp.int32)[:, None], flat.shape)
    field = jnp.zeros((count, length * plane), jnp.float32).at[rows, flat].add(amounts)
    return field.reshape(count, length, rows_y, cols_x)


def one_shot(items, velocity):
    up, u, vp, v, wave, traces, sdepth, sy, sx, hy, hx, rcells = items
    up, u, vp, v = up[None], u[None], vp[None], v[None]
    depth_all, rows_y, cols_x = velocity.shape
    mask = band_mask(sy[None], sx[None], hy[None], hx[None], rows_y, cols_x)[:, None]
    scell = (sdepth * rows_y * cols_x + sy * cols_x + sx)[None, None]
    image = jnp.zeros(velocity.shape, jnp.float32)
    for step in range(STEPS):
        both = jnp.pad(jnp.stack([u, v]), [(0, 0), (0, 0), (4, 4), (0, 0), (0, 0)])
        lap = laplace(both)
        sdelta = inject(scell, wave[step][None, None], 0, depth_all, rows_y, cols_x)
        rdelta = inject(rcells[None], traces[step][None], 0, depth_all, rows_y, cols_x)
        unew = mask * (2.0 * u - up + velocity * lap[0] + sdelta)
        vnew = mask * (2.0 * v - vp + velocity * lap[1] + rdelta)
        image = image + jnp.sum((unew - 2.0 * u + up) * vnew, axis=0)
        up, u, vp, v = u, unew, v, vnew
    return u[0], v[0], image


def reference(src_prev, src_cur, rcv_prev, rcv_cur, velocity, wavelet, residual_traces, source_depth, source_y, source_x, half_y, half_x, receiver_cell):
    items = (src_prev, src_cur, rcv_prev, rcv_cur, jnp.swapaxes(wavelet, 0, 1), jnp.swapaxes(residual_traces, 0, 1), source_depth, source_y, source_x, half_y, half_x, receiver_cell)
    src_last, rcv_last, images = lax.map(lambda item: one_shot(item, velocity), items)
    return src_last, rcv_last, jnp.sum(images, axis=0)
```

```python
import jax
import jax.numpy as jnp
from jax import lax
from jax.sharding import PartitionSpec as P

STEPS = 2


COEF = (-205.0 / 72.0, 8.0 / 5.0, -1.0 / 5.0, 8.0 / 315.0, -1.0 / 560.0)


def extended(block, sides, width):
    for axis, dim in sides:
        count = lax.axis_size(axis)
        forward = [(i, i + 1) for i in range(count - 1)]
        backward = [(target, source) for source, target in forward]
        low = lax.ppermute(
            lax.slice_in_dim(block, block.shape[dim] - width, None, axis=dim), axis, forward
        )
        high = lax.ppermute(lax.slice_in_dim(block, 0, width, axis=dim), axis, backward)
        block = jnp.concatenate([low, block, high], axis=dim)
    return block


def laplace(padded):
    axis_z = padded.ndim - 3
    length = padded.shape[axis_z] - 8
    center = lax.slice_in_dim(padded, 4, 4 + length, axis=axis_z)
    total = 3.0 * COEF[0] * center
    for shift_k in range(1, 5):
        upper = lax.slice_in_dim(padded, 4 + shift_k, 4 + shift_k + length, axis=axis_z)
        lower = lax.slice_in_dim(padded, 4 - shift_k, 4 - shift_k + length, axis=axis_z)
        total = total + COEF[shift_k] * (upper + lower)
    widths = [(0, 0)] * (center.ndim - 2) + [(4, 4), (4, 4)]
    plane = jnp.pad(center, widths)
    rows_y = center.shape[-2]
    cols_x = center.shape[-1]
    for shift_k in range(1, 5):
        side_y = (
            plane[..., 4 + shift_k : 4 + shift_k + rows_y, 4 : 4 + cols_x]
            + plane[..., 4 - shift_k : 4 - shift_k + rows_y, 4 : 4 + cols_x]
        )
        side_x = (
            plane[..., 4 : 4 + rows_y, 4 + shift_k : 4 + shift_k + cols_x]
            + plane[..., 4 : 4 + rows_y, 4 - shift_k : 4 - shift_k + cols_x]
        )
        total = total + COEF[shift_k] * (side_y + side_x)
    return total


def band_mask(source_y, source_x, half_y, half_x, rows_y, cols_x):
    grid_y = jnp.arange(rows_y, dtype=jnp.int32)
    grid_x = jnp.arange(cols_x, dtype=jnp.int32)
    inside_y = jnp.abs(grid_y[None, :, None] - source_y[:, None, None]) <= half_y[:, None, None]
    inside_x = jnp.abs(grid_x[None, None, :] - source_x[:, None, None]) <= half_x[:, None, None]
    return (inside_y & inside_x).astype(jnp.float32)


def point_field(depth_local, row, col, values, length, rows_y, cols_x):
    grid_z = jnp.arange(length, dtype=jnp.int32)[None, :, None, None]
    grid_y = jnp.arange(rows_y, dtype=jnp.int32)[None, None, :, None]
    grid_x = jnp.arange(cols_x, dtype=jnp.int32)[None, None, None, :]
    hit = (
        (grid_z == depth_local[:, None, None, None])
        & (grid_y == row[:, None, None, None])
        & (grid_x == col[:, None, None, None])
    )
    return jnp.where(hit, values[:, None, None, None], 0.0)


def receiver_field(cells, traces, begin, length, rows_y, cols_x):
    plane = rows_y * cols_x
    depth = cells // plane
    rest = cells - depth * plane
    row = rest // cols_x
    col = rest - row * cols_x
    local = depth - begin
    slab_rows = jnp.arange(length * rows_y, dtype=jnp.int32)
    key = local * rows_y + row
    left = jnp.where(slab_rows[None, :, None] == key[:, None, :], traces[:, None, :], 0.0)
    right = (col[:, :, None] == jnp.arange(cols_x, dtype=jnp.int32)[None, None, :]).astype(
        jnp.float32
    )
    field = jnp.einsum(
        "szr,srx->szx",
        left,
        right,
        precision=lax.Precision.HIGHEST,
        preferred_element_type=jnp.float32,
    )
    return field.reshape(cells.shape[0], length, rows_y, cols_x)


def butterfly_sum(value, axis):
    count = lax.axis_size(axis)
    stride = 1
    while stride < count:
        pairs = [(i, i ^ stride) for i in range(count)]
        value = value + lax.ppermute(value, axis, pairs)
        stride *= 2
    return value


def per_device(
    src_prev,
    src_cur,
    rcv_prev,
    rcv_cur,
    velocity,
    wavelet,
    residual_traces,
    source_depth,
    source_y,
    source_x,
    half_y,
    half_x,
    receiver_cell,
):
    shot_count, depth, rows_y, cols_x = src_cur.shape
    start = lax.axis_index("slab") * depth
    mask = band_mask(source_y, source_x, half_y, half_x, rows_y, cols_x)[:, None]
    terms = []
    up, u, vp, v = (src_prev, src_cur, rcv_prev, rcv_cur)
    for step in range(STEPS):
        stacked = jnp.stack([u, v])
        padded = extended(stacked, (("slab", 2),), 4)
        lap = laplace(padded)
        sdelta = point_field(
            source_depth - start, source_y, source_x, wavelet[step], depth, rows_y, cols_x
        )
        rdelta = receiver_field(receiver_cell, residual_traces[step], start, depth, rows_y, cols_x)
        unew = mask * (2.0 * u - up + velocity * lap[0] + sdelta)
        vnew = mask * (2.0 * v - vp + velocity * lap[1] + rdelta)
        terms.append(jnp.sum((unew - 2.0 * u + up) * vnew, axis=0))
        up, u, vp, v = (u, unew, v, vnew)
    src_last, rcv_last = (u, v)
    local_sum = terms[0]
    for extra in terms[1:]:
        local_sum = local_sum + extra
    image = butterfly_sum(local_sum, "shots")
    return (src_last, rcv_last, image)


def solution(mesh):
    return jax.shard_map(
        per_device,
        mesh=mesh,
        in_specs=(
            P("shots", "slab", None, None),
            P("shots", "slab", None, None),
            P("shots", "slab", None, None),
            P("shots", "slab", None, None),
            P("slab", None, None),
            P(None, "shots"),
            P(None, "shots", None),
            P("shots"),
            P("shots"),
            P("shots"),
            P("shots"),
            P("shots"),
            P("shots", None),
        ),
        out_specs=(
            P("shots", "slab", None, None),
            P("shots", "slab", None, None),
            P("slab", None, None),
        ),
        check_vma=False,
    )
```

```python
import jax
import jax.numpy as jnp
from jax import lax
from jax.sharding import PartitionSpec as P

STEPS = 2


COEF = (-205.0 / 72.0, 8.0 / 5.0, -1.0 / 5.0, 8.0 / 315.0, -1.0 / 560.0)


WIN_Y = 44
WIN_X = 88


def band_corner(source_y, source_x, half_y, half_x, rows_y, cols_x):
    row0 = jnp.clip(source_y - half_y, 0, rows_y - WIN_Y)
    col0 = jnp.clip(source_x - half_x, 0, cols_x - WIN_X)
    return row0, col0


def cut_windows(layers, row0, col0):
    fields, shots, width = layers.shape[:3]
    pieces = []
    for s in range(shots):
        piece = lax.dynamic_slice(
            layers[:, s], (0, 0, row0[s], col0[s]), (fields, width, WIN_Y, WIN_X)
        )
        pieces.append(piece.reshape(fields, -1, 128))
    return jnp.stack(pieces, axis=1)


def paste_windows(flat, row0, col0, width, rows_y, cols_x):
    fields, shots = flat.shape[:2]
    pieces = []
    for s in range(shots):
        piece = flat[:, s].reshape(fields, width, WIN_Y, WIN_X)
        empty = jnp.zeros((fields, width, rows_y, cols_x), flat.dtype)
        pieces.append(lax.dynamic_update_slice(empty, piece, (0, 0, row0[s], col0[s])))
    return jnp.stack(pieces, axis=1)


def extended(block, row0, col0, width):
    count = lax.axis_size("slab")
    forward = [(i, i + 1) for i in range(count - 1)]
    backward = [(target, source) for source, target in forward]
    dim = 2
    rows_y, cols_x = block.shape[-2:]
    low = lax.ppermute(
        cut_windows(lax.slice_in_dim(block, block.shape[dim] - width, None, axis=dim), row0, col0),
        "slab",
        forward,
    )
    high = lax.ppermute(
        cut_windows(lax.slice_in_dim(block, 0, width, axis=dim), row0, col0), "slab", backward
    )
    low = paste_windows(low, row0, col0, width, rows_y, cols_x)
    high = paste_windows(high, row0, col0, width, rows_y, cols_x)
    return jnp.concatenate([low, block, high], axis=dim)


def laplace(padded):
    axis_z = padded.ndim - 3
    length = padded.shape[axis_z] - 8
    center = lax.slice_in_dim(padded, 4, 4 + length, axis=axis_z)
    total = 3.0 * COEF[0] * center
    for shift_k in range(1, 5):
        upper = lax.slice_in_dim(padded, 4 + shift_k, 4 + shift_k + length, axis=axis_z)
        lower = lax.slice_in_dim(padded, 4 - shift_k, 4 - shift_k + length, axis=axis_z)
        total = total + COEF[shift_k] * (upper + lower)
    widths = [(0, 0)] * (center.ndim - 2) + [(4, 4), (4, 4)]
    plane = jnp.pad(center, widths)
    rows_y = center.shape[-2]
    cols_x = center.shape[-1]
    for shift_k in range(1, 5):
        side_y = (
            plane[..., 4 + shift_k : 4 + shift_k + rows_y, 4 : 4 + cols_x]
            + plane[..., 4 - shift_k : 4 - shift_k + rows_y, 4 : 4 + cols_x]
        )
        side_x = (
            plane[..., 4 : 4 + rows_y, 4 + shift_k : 4 + shift_k + cols_x]
            + plane[..., 4 : 4 + rows_y, 4 - shift_k : 4 - shift_k + cols_x]
        )
        total = total + COEF[shift_k] * (side_y + side_x)
    return total


def band_mask(source_y, source_x, half_y, half_x, rows_y, cols_x):
    grid_y = jnp.arange(rows_y, dtype=jnp.int32)
    grid_x = jnp.arange(cols_x, dtype=jnp.int32)
    inside_y = jnp.abs(grid_y[None, :, None] - source_y[:, None, None]) <= half_y[:, None, None]
    inside_x = jnp.abs(grid_x[None, None, :] - source_x[:, None, None]) <= half_x[:, None, None]
    return (inside_y & inside_x).astype(jnp.float32)


def point_field(depth_local, row, col, values, length, rows_y, cols_x):
    grid_z = jnp.arange(length, dtype=jnp.int32)[None, :, None, None]
    grid_y = jnp.arange(rows_y, dtype=jnp.int32)[None, None, :, None]
    grid_x = jnp.arange(cols_x, dtype=jnp.int32)[None, None, None, :]
    hit = (
        (grid_z == depth_local[:, None, None, None])
        & (grid_y == row[:, None, None, None])
        & (grid_x == col[:, None, None, None])
    )
    return jnp.where(hit, values[:, None, None, None], 0.0)


def receiver_field(cells, traces, begin, length, rows_y, cols_x):
    plane = rows_y * cols_x
    depth = cells // plane
    rest = cells - depth * plane
    row = rest // cols_x
    col = rest - row * cols_x
    local = depth - begin
    slab_rows = jnp.arange(length * rows_y, dtype=jnp.int32)
    key = local * rows_y + row
    left = jnp.where(slab_rows[None, :, None] == key[:, None, :], traces[:, None, :], 0.0)
    right = (col[:, :, None] == jnp.arange(cols_x, dtype=jnp.int32)[None, None, :]).astype(
        jnp.float32
    )
    field = jnp.einsum(
        "szr,srx->szx",
        left,
        right,
        precision=lax.Precision.HIGHEST,
        preferred_element_type=jnp.float32,
    )
    return field.reshape(cells.shape[0], length, rows_y, cols_x)


def tree_sum(value, axis):
    count = lax.axis_size(axis)
    me = lax.axis_index(axis)
    shape = value.shape
    piece = value.reshape(-1)
    bits = []
    stride = 1
    while stride < count:
        bits.append(stride)
        stride *= 2
    for stride in bits:
        upper = (me // stride) % 2 == 1
        halves = piece.reshape(2, -1)
        send = jnp.where(upper, halves[0], halves[1])
        keep = jnp.where(upper, halves[1], halves[0])
        pairs = [(i, i ^ stride) for i in range(count)]
        piece = keep + lax.ppermute(send, axis, pairs)
    for stride in reversed(bits):
        upper = (me // stride) % 2 == 1
        pairs = [(i, i ^ stride) for i in range(count)]
        other = lax.ppermute(piece, axis, pairs)
        piece = jnp.where(upper, jnp.concatenate([other, piece]), jnp.concatenate([piece, other]))
    return piece.reshape(shape)


def per_device(
    src_prev,
    src_cur,
    rcv_prev,
    rcv_cur,
    velocity,
    wavelet,
    residual_traces,
    source_depth,
    source_y,
    source_x,
    half_y,
    half_x,
    receiver_cell,
):
    shot_count, depth, rows_y, cols_x = src_cur.shape
    start = lax.axis_index("slab") * depth
    mask = band_mask(source_y, source_x, half_y, half_x, rows_y, cols_x)[:, None]
    row0, col0 = band_corner(source_y, source_x, half_y, half_x, rows_y, cols_x)
    terms = []
    up, u, vp, v = (src_prev, src_cur, rcv_prev, rcv_cur)
    for step in range(STEPS):
        stacked = jnp.stack([u, v])
        padded = extended(stacked, row0, col0, 4)
        lap = laplace(padded)
        sdelta = point_field(
            source_depth - start, source_y, source_x, wavelet[step], depth, rows_y, cols_x
        )
        rdelta = receiver_field(receiver_cell, residual_traces[step], start, depth, rows_y, cols_x)
        unew = mask * (2.0 * u - up + velocity * lap[0] + sdelta)
        vnew = mask * (2.0 * v - vp + velocity * lap[1] + rdelta)
        terms.append(jnp.sum((unew - 2.0 * u + up) * vnew, axis=0))
        up, u, vp, v = (u, unew, v, vnew)
    src_last, rcv_last = (u, v)
    local_sum = terms[0]
    for extra in terms[1:]:
        local_sum = local_sum + extra
    image = tree_sum(local_sum, "shots")
    return (src_last, rcv_last, image)


def solution(mesh):
    return jax.shard_map(
        per_device,
        mesh=mesh,
        in_specs=(
            P("shots", "slab", None, None),
            P("shots", "slab", None, None),
            P("shots", "slab", None, None),
            P("shots", "slab", None, None),
            P("slab", None, None),
            P(None, "shots"),
            P(None, "shots", None),
            P("shots"),
            P("shots"),
            P("shots"),
            P("shots"),
            P("shots"),
            P("shots", None),
        ),
        out_specs=(
            P("shots", "slab", None, None),
            P("shots", "slab", None, None),
            P("slab", None, None),
        ),
        check_vma=False,
    )
```

```python
import jax
import jax.numpy as jnp
from jax import lax
from jax.sharding import PartitionSpec as P
from jax.experimental import pallas as pl
from jax.experimental.pallas import tpu as pltpu
import functools

STEPS = 2


COEF = (-205.0 / 72.0, 8.0 / 5.0, -1.0 / 5.0, 8.0 / 315.0, -1.0 / 560.0)


WIN_Y = 44
WIN_X = 88


def band_corner(source_y, source_x, half_y, half_x, rows_y, cols_x):
    row0 = jnp.clip(source_y - half_y, 0, rows_y - WIN_Y)
    col0 = jnp.clip(source_x - half_x, 0, cols_x - WIN_X)
    return row0, col0


def cut_windows(layers, row0, col0):
    fields, shots, width = layers.shape[:3]
    pieces = []
    for s in range(shots):
        piece = lax.dynamic_slice(
            layers[:, s], (0, 0, row0[s], col0[s]), (fields, width, WIN_Y, WIN_X)
        )
        pieces.append(piece.reshape(fields, -1, 128))
    return jnp.stack(pieces, axis=1)


def paste_windows(flat, row0, col0, width, rows_y, cols_x):
    fields, shots = flat.shape[:2]
    pieces = []
    for s in range(shots):
        piece = flat[:, s].reshape(fields, width, WIN_Y, WIN_X)
        empty = jnp.zeros((fields, width, rows_y, cols_x), flat.dtype)
        pieces.append(lax.dynamic_update_slice(empty, piece, (0, 0, row0[s], col0[s])))
    return jnp.stack(pieces, axis=1)


def extended(block, row0, col0, width):
    count = lax.axis_size("slab")
    forward = [(i, i + 1) for i in range(count - 1)]
    backward = [(target, source) for source, target in forward]
    dim = 2
    rows_y, cols_x = block.shape[-2:]
    low = lax.ppermute(
        cut_windows(lax.slice_in_dim(block, block.shape[dim] - width, None, axis=dim), row0, col0),
        "slab",
        forward,
    )
    high = lax.ppermute(
        cut_windows(lax.slice_in_dim(block, 0, width, axis=dim), row0, col0), "slab", backward
    )
    low = paste_windows(low, row0, col0, width, rows_y, cols_x)
    high = paste_windows(high, row0, col0, width, rows_y, cols_x)
    return jnp.concatenate([low, block, high], axis=dim)


def laplace(padded):
    axis_z = padded.ndim - 3
    length = padded.shape[axis_z] - 8
    center = lax.slice_in_dim(padded, 4, 4 + length, axis=axis_z)
    total = 3.0 * COEF[0] * center
    for shift_k in range(1, 5):
        upper = lax.slice_in_dim(padded, 4 + shift_k, 4 + shift_k + length, axis=axis_z)
        lower = lax.slice_in_dim(padded, 4 - shift_k, 4 - shift_k + length, axis=axis_z)
        total = total + COEF[shift_k] * (upper + lower)
    widths = [(0, 0)] * (center.ndim - 2) + [(4, 4), (4, 4)]
    plane = jnp.pad(center, widths)
    rows_y = center.shape[-2]
    cols_x = center.shape[-1]
    for shift_k in range(1, 5):
        side_y = (
            plane[..., 4 + shift_k : 4 + shift_k + rows_y, 4 : 4 + cols_x]
            + plane[..., 4 - shift_k : 4 - shift_k + rows_y, 4 : 4 + cols_x]
        )
        side_x = (
            plane[..., 4 : 4 + rows_y, 4 + shift_k : 4 + shift_k + cols_x]
            + plane[..., 4 : 4 + rows_y, 4 - shift_k : 4 - shift_k + cols_x]
        )
        total = total + COEF[shift_k] * (side_y + side_x)
    return total


def band_mask(source_y, source_x, half_y, half_x, rows_y, cols_x):
    grid_y = jnp.arange(rows_y, dtype=jnp.int32)
    grid_x = jnp.arange(cols_x, dtype=jnp.int32)
    inside_y = jnp.abs(grid_y[None, :, None] - source_y[:, None, None]) <= half_y[:, None, None]
    inside_x = jnp.abs(grid_x[None, None, :] - source_x[:, None, None]) <= half_x[:, None, None]
    return (inside_y & inside_x).astype(jnp.float32)


def point_field(depth_local, row, col, values, length, rows_y, cols_x):
    grid_z = jnp.arange(length, dtype=jnp.int32)[None, :, None, None]
    grid_y = jnp.arange(rows_y, dtype=jnp.int32)[None, None, :, None]
    grid_x = jnp.arange(cols_x, dtype=jnp.int32)[None, None, None, :]
    hit = (
        (grid_z == depth_local[:, None, None, None])
        & (grid_y == row[:, None, None, None])
        & (grid_x == col[:, None, None, None])
    )
    return jnp.where(hit, values[:, None, None, None], 0.0)


def receiver_field(cells, traces, begin, length, rows_y, cols_x):
    plane = rows_y * cols_x
    depth = cells // plane
    rest = cells - depth * plane
    row = rest // cols_x
    col = rest - row * cols_x
    local = depth - begin
    slab_rows = jnp.arange(length * rows_y, dtype=jnp.int32)
    key = local * rows_y + row
    left = jnp.where(slab_rows[None, :, None] == key[:, None, :], traces[:, None, :], 0.0)
    right = (col[:, :, None] == jnp.arange(cols_x, dtype=jnp.int32)[None, None, :]).astype(
        jnp.float32
    )
    field = jnp.einsum(
        "szr,srx->szx",
        left,
        right,
        precision=lax.Precision.HIGHEST,
        preferred_element_type=jnp.float32,
    )
    return field.reshape(cells.shape[0], length, rows_y, cols_x)


def tree_sum(value, axis):
    count = lax.axis_size(axis)
    me = lax.axis_index(axis)
    shape = value.shape
    piece = value.reshape(-1)
    bits = []
    stride = 1
    while stride < count:
        bits.append(stride)
        stride *= 2
    for stride in bits:
        upper = (me // stride) % 2 == 1
        halves = piece.reshape(2, -1)
        send = jnp.where(upper, halves[0], halves[1])
        keep = jnp.where(upper, halves[1], halves[0])
        pairs = [(i, i ^ stride) for i in range(count)]
        piece = keep + lax.ppermute(send, axis, pairs)
    for stride in reversed(bits):
        upper = (me // stride) % 2 == 1
        pairs = [(i, i ^ stride) for i in range(count)]
        other = lax.ppermute(piece, axis, pairs)
        piece = jnp.where(upper, jnp.concatenate([other, piece]), jnp.concatenate([piece, other]))
    return piece.reshape(shape)


def allreduce_kernel(count, local_ref, out_ref, gathered, reduced, spread, send1, recv1, send2, recv2):
    me = lax.axis_index("shots")
    slab = lax.axis_index("slab")
    barrier = pltpu.get_barrier_semaphore()
    for k in range(1, count):
        peer = lax.rem(me + k, count)
        pl.semaphore_signal(
            barrier, inc=1, device_id=(slab, peer), device_id_type=pl.DeviceIdType.MESH
        )
    pl.semaphore_wait(barrier, count - 1)
    copies = []
    for k in range(1, count):
        peer = lax.rem(me + k, count)
        copy = pltpu.make_async_remote_copy(
            src_ref=local_ref.at[peer],
            dst_ref=gathered.at[k],
            send_sem=send1.at[k],
            recv_sem=recv1.at[k],
            device_id=(slab, peer),
            device_id_type=pl.DeviceIdType.MESH,
        )
        copy.start()
        copies.append(copy)
    for copy in copies:
        copy.wait()
    total = local_ref[me]
    for k in range(1, count):
        total = total + gathered[k]
    reduced[...] = total
    copies = []
    for k in range(1, count):
        peer = lax.rem(me + k, count)
        copy = pltpu.make_async_remote_copy(
            src_ref=reduced,
            dst_ref=spread.at[k],
            send_sem=send2.at[k],
            recv_sem=recv2.at[k],
            device_id=(slab, peer),
            device_id_type=pl.DeviceIdType.MESH,
        )
        copy.start()
        copies.append(copy)
    out_ref[me] = total
    for copy in copies:
        copy.wait()
    for k in range(1, count):
        out_ref[lax.rem(me + count - k, count)] = spread[k]


def shots_sum(value):
    count = lax.axis_size("shots")
    shape = value.shape
    chunks = value.reshape(count, -1, 128)
    rows = chunks.shape[1]
    out = pl.pallas_call(
        functools.partial(allreduce_kernel, count),
        out_shape=jax.ShapeDtypeStruct(chunks.shape, jnp.float32),
        in_specs=[pl.BlockSpec(memory_space=pltpu.VMEM)],
        out_specs=pl.BlockSpec(memory_space=pltpu.VMEM),
        scratch_shapes=[
            pltpu.VMEM((count, rows, 128), jnp.float32),
            pltpu.VMEM((rows, 128), jnp.float32),
            pltpu.VMEM((count, rows, 128), jnp.float32),
            pltpu.SemaphoreType.DMA((count,)),
            pltpu.SemaphoreType.DMA((count,)),
            pltpu.SemaphoreType.DMA((count,)),
            pltpu.SemaphoreType.DMA((count,)),
        ],
        compiler_params=pltpu.CompilerParams(collective_id=0, has_side_effects=True),
    )(chunks)
    return out.reshape(shape)


def per_device(
    src_prev,
    src_cur,
    rcv_prev,
    rcv_cur,
    velocity,
    wavelet,
    residual_traces,
    source_depth,
    source_y,
    source_x,
    half_y,
    half_x,
    receiver_cell,
):
    shot_count, depth, rows_y, cols_x = src_cur.shape
    start = lax.axis_index("slab") * depth
    mask = band_mask(source_y, source_x, half_y, half_x, rows_y, cols_x)[:, None]
    row0, col0 = band_corner(source_y, source_x, half_y, half_x, rows_y, cols_x)
    terms = []
    up, u, vp, v = (src_prev, src_cur, rcv_prev, rcv_cur)
    for step in range(STEPS):
        stacked = jnp.stack([u, v])
        padded = extended(stacked, row0, col0, 4)
        lap = laplace(padded)
        sdelta = point_field(
            source_depth - start, source_y, source_x, wavelet[step], depth, rows_y, cols_x
        )
        rdelta = receiver_field(receiver_cell, residual_traces[step], start, depth, rows_y, cols_x)
        unew = mask * (2.0 * u - up + velocity * lap[0] + sdelta)
        vnew = mask * (2.0 * v - vp + velocity * lap[1] + rdelta)
        terms.append(jnp.sum((unew - 2.0 * u + up) * vnew, axis=0))
        up, u, vp, v = (u, unew, v, vnew)
    src_last, rcv_last = (u, v)
    local_sum = terms[0]
    for extra in terms[1:]:
        local_sum = local_sum + extra
    image = shots_sum(local_sum)
    return (src_last, rcv_last, image)


def solution(mesh):
    return jax.shard_map(
        per_device,
        mesh=mesh,
        in_specs=(
            P("shots", "slab", None, None),
            P("shots", "slab", None, None),
            P("shots", "slab", None, None),
            P("shots", "slab", None, None),
            P("slab", None, None),
            P(None, "shots"),
            P(None, "shots", None),
            P("shots"),
            P("shots"),
            P("shots"),
            P("shots"),
            P("shots"),
            P("shots", None),
        ),
        out_specs=(
            P("shots", "slab", None, None),
            P("shots", "slab", None, None),
            P("slab", None, None),
        ),
        check_vma=False,
    )
```

```python
import jax
import jax.numpy as jnp
from jax import lax
from jax.sharding import PartitionSpec as P
from jax.experimental import pallas as pl
from jax.experimental.pallas import tpu as pltpu
import functools

STEPS = 2


COEF = (-205.0 / 72.0, 8.0 / 5.0, -1.0 / 5.0, 8.0 / 315.0, -1.0 / 560.0)


WIN_Y = 44
WIN_X = 88


def band_corner(source_y, source_x, half_y, half_x, rows_y, cols_x):
    row0 = jnp.clip(source_y - half_y, 0, rows_y - WIN_Y)
    col0 = jnp.clip(source_x - half_x, 0, cols_x - WIN_X)
    return row0, col0


def selectors(row0, col0, rows_y, cols_x):
    pick_y = (
        jnp.arange(rows_y, dtype=jnp.int32)[None, :, None]
        == row0[:, None, None] + jnp.arange(WIN_Y, dtype=jnp.int32)[None, None, :]
    ).astype(jnp.float32)
    pick_x = (
        jnp.arange(cols_x, dtype=jnp.int32)[None, None, :]
        == col0[:, None, None] + jnp.arange(WIN_X, dtype=jnp.int32)[None, :, None]
    ).astype(jnp.float32)
    return pick_y, pick_x


def exact_einsum(spec, a, b):
    return jnp.einsum(
        spec, a, b, precision=lax.Precision.HIGHEST, preferred_element_type=jnp.float32
    )


def cut_windows(layers, pick_y, pick_x):
    fields, shots, width = layers.shape[:3]
    part = exact_einsum("fsjyx,sbx->fsjyb", layers, pick_x)
    part = exact_einsum("sya,fsjyb->fsjab", pick_y, part)
    return part.reshape(fields, shots, -1, 128)


def paste_windows(flat, pick_y, pick_x, width):
    fields, shots = flat.shape[:2]
    part = flat.reshape(fields, shots, width, WIN_Y, WIN_X)
    part = exact_einsum("fsjab,sbx->fsjax", part, pick_x)
    return exact_einsum("sya,fsjax->fsjyx", pick_y, part)


def extended(block, pick_y, pick_x, width):
    count = lax.axis_size("slab")
    forward = [(i, i + 1) for i in range(count - 1)]
    backward = [(target, source) for source, target in forward]
    dim = 2
    rows_y, cols_x = block.shape[-2:]
    low = lax.ppermute(
        cut_windows(lax.slice_in_dim(block, block.shape[dim] - width, None, axis=dim), pick_y, pick_x),
        "slab",
        forward,
    )
    high = lax.ppermute(
        cut_windows(lax.slice_in_dim(block, 0, width, axis=dim), pick_y, pick_x), "slab", backward
    )
    low = paste_windows(low, pick_y, pick_x, width)
    high = paste_windows(high, pick_y, pick_x, width)
    return jnp.concatenate([low, block, high], axis=dim)


def laplace(padded):
    axis_z = padded.ndim - 3
    length = padded.shape[axis_z] - 8
    center = lax.slice_in_dim(padded, 4, 4 + length, axis=axis_z)
    total = 3.0 * COEF[0] * center
    for shift_k in range(1, 5):
        upper = lax.slice_in_dim(padded, 4 + shift_k, 4 + shift_k + length, axis=axis_z)
        lower = lax.slice_in_dim(padded, 4 - shift_k, 4 - shift_k + length, axis=axis_z)
        total = total + COEF[shift_k] * (upper + lower)
    widths = [(0, 0)] * (center.ndim - 2) + [(4, 4), (4, 4)]
    plane = jnp.pad(center, widths)
    rows_y = center.shape[-2]
    cols_x = center.shape[-1]
    for shift_k in range(1, 5):
        side_y = (
            plane[..., 4 + shift_k : 4 + shift_k + rows_y, 4 : 4 + cols_x]
            + plane[..., 4 - shift_k : 4 - shift_k + rows_y, 4 : 4 + cols_x]
        )
        side_x = (
            plane[..., 4 : 4 + rows_y, 4 + shift_k : 4 + shift_k + cols_x]
            + plane[..., 4 : 4 + rows_y, 4 - shift_k : 4 - shift_k + cols_x]
        )
        total = total + COEF[shift_k] * (side_y + side_x)
    return total


def band_mask(source_y, source_x, half_y, half_x, rows_y, cols_x):
    grid_y = jnp.arange(rows_y, dtype=jnp.int32)
    grid_x = jnp.arange(cols_x, dtype=jnp.int32)
    inside_y = jnp.abs(grid_y[None, :, None] - source_y[:, None, None]) <= half_y[:, None, None]
    inside_x = jnp.abs(grid_x[None, None, :] - source_x[:, None, None]) <= half_x[:, None, None]
    return (inside_y & inside_x).astype(jnp.float32)


def point_field(depth_local, row, col, values, length, rows_y, cols_x):
    grid_z = jnp.arange(length, dtype=jnp.int32)[None, :, None, None]
    grid_y = jnp.arange(rows_y, dtype=jnp.int32)[None, None, :, None]
    grid_x = jnp.arange(cols_x, dtype=jnp.int32)[None, None, None, :]
    hit = (
        (grid_z == depth_local[:, None, None, None])
        & (grid_y == row[:, None, None, None])
        & (grid_x == col[:, None, None, None])
    )
    return jnp.where(hit, values[:, None, None, None], 0.0)


def receiver_field(cells, traces, begin, length, rows_y, cols_x):
    plane = rows_y * cols_x
    depth = cells // plane
    rest = cells - depth * plane
    row = rest // cols_x
    col = rest - row * cols_x
    local = depth - begin
    slab_rows = jnp.arange(length * rows_y, dtype=jnp.int32)
    key = local * rows_y + row
    left = jnp.where(slab_rows[None, :, None] == key[:, None, :], traces[:, None, :], 0.0)
    right = (col[:, :, None] == jnp.arange(cols_x, dtype=jnp.int32)[None, None, :]).astype(
        jnp.float32
    )
    field = jnp.einsum(
        "szr,srx->szx",
        left,
        right,
        precision=lax.Precision.HIGHEST,
        preferred_element_type=jnp.float32,
    )
    return field.reshape(cells.shape[0], length, rows_y, cols_x)


def tree_sum(value, axis):
    count = lax.axis_size(axis)
    me = lax.axis_index(axis)
    shape = value.shape
    piece = value.reshape(-1)
    bits = []
    stride = 1
    while stride < count:
        bits.append(stride)
        stride *= 2
    for stride in bits:
        upper = (me // stride) % 2 == 1
        halves = piece.reshape(2, -1)
        send = jnp.where(upper, halves[0], halves[1])
        keep = jnp.where(upper, halves[1], halves[0])
        pairs = [(i, i ^ stride) for i in range(count)]
        piece = keep + lax.ppermute(send, axis, pairs)
    for stride in reversed(bits):
        upper = (me // stride) % 2 == 1
        pairs = [(i, i ^ stride) for i in range(count)]
        other = lax.ppermute(piece, axis, pairs)
        piece = jnp.where(upper, jnp.concatenate([other, piece]), jnp.concatenate([piece, other]))
    return piece.reshape(shape)


def allreduce_kernel(count, local_ref, out_ref, gathered, reduced, spread, send1, recv1, send2, recv2):
    me = lax.axis_index("shots")
    slab = lax.axis_index("slab")
    barrier = pltpu.get_barrier_semaphore()
    for k in range(1, count):
        peer = lax.rem(me + k, count)
        pl.semaphore_signal(
            barrier, inc=1, device_id=(slab, peer), device_id_type=pl.DeviceIdType.MESH
        )
    pl.semaphore_wait(barrier, count - 1)
    copies = []
    for k in range(1, count):
        peer = lax.rem(me + k, count)
        copy = pltpu.make_async_remote_copy(
            src_ref=local_ref.at[peer],
            dst_ref=gathered.at[k],
            send_sem=send1.at[k],
            recv_sem=recv1.at[k],
            device_id=(slab, peer),
            device_id_type=pl.DeviceIdType.MESH,
        )
        copy.start()
        copies.append(copy)
    for copy in copies:
        copy.wait()
    total = local_ref[me]
    for k in range(1, count):
        total = total + gathered[k]
    reduced[...] = total
    copies = []
    for k in range(1, count):
        peer = lax.rem(me + k, count)
        copy = pltpu.make_async_remote_copy(
            src_ref=reduced,
            dst_ref=spread.at[k],
            send_sem=send2.at[k],
            recv_sem=recv2.at[k],
            device_id=(slab, peer),
            device_id_type=pl.DeviceIdType.MESH,
        )
        copy.start()
        copies.append(copy)
    out_ref[me] = total
    for copy in copies:
        copy.wait()
    for k in range(1, count):
        out_ref[lax.rem(me + count - k, count)] = spread[k]


def shots_sum(value):
    count = lax.axis_size("shots")
    shape = value.shape
    chunks = value.reshape(count, -1, 128)
    rows = chunks.shape[1]
    out = pl.pallas_call(
        functools.partial(allreduce_kernel, count),
        out_shape=jax.ShapeDtypeStruct(chunks.shape, jnp.float32),
        in_specs=[pl.BlockSpec(memory_space=pltpu.VMEM)],
        out_specs=pl.BlockSpec(memory_space=pltpu.VMEM),
        scratch_shapes=[
            pltpu.VMEM((count, rows, 128), jnp.float32),
            pltpu.VMEM((rows, 128), jnp.float32),
            pltpu.VMEM((count, rows, 128), jnp.float32),
            pltpu.SemaphoreType.DMA((count,)),
            pltpu.SemaphoreType.DMA((count,)),
            pltpu.SemaphoreType.DMA((count,)),
            pltpu.SemaphoreType.DMA((count,)),
        ],
        compiler_params=pltpu.CompilerParams(collective_id=0, has_side_effects=True),
    )(chunks)
    return out.reshape(shape)


def per_device(
    src_prev,
    src_cur,
    rcv_prev,
    rcv_cur,
    velocity,
    wavelet,
    residual_traces,
    source_depth,
    source_y,
    source_x,
    half_y,
    half_x,
    receiver_cell,
):
    shot_count, depth, rows_y, cols_x = src_cur.shape
    start = lax.axis_index("slab") * depth
    mask = band_mask(source_y, source_x, half_y, half_x, rows_y, cols_x)[:, None]
    row0, col0 = band_corner(source_y, source_x, half_y, half_x, rows_y, cols_x)
    pick_y, pick_x = selectors(row0, col0, rows_y, cols_x)
    terms = []
    up, u, vp, v = (src_prev, src_cur, rcv_prev, rcv_cur)
    for step in range(STEPS):
        stacked = jnp.stack([u, v])
        padded = extended(stacked, pick_y, pick_x, 4)
        lap = laplace(padded)
        sdelta = point_field(
            source_depth - start, source_y, source_x, wavelet[step], depth, rows_y, cols_x
        )
        rdelta = receiver_field(receiver_cell, residual_traces[step], start, depth, rows_y, cols_x)
        unew = mask * (2.0 * u - up + velocity * lap[0] + sdelta)
        vnew = mask * (2.0 * v - vp + velocity * lap[1] + rdelta)
        terms.append(jnp.sum((unew - 2.0 * u + up) * vnew, axis=0))
        up, u, vp, v = (u, unew, v, vnew)
    src_last, rcv_last = (u, v)
    local_sum = terms[0]
    for extra in terms[1:]:
        local_sum = local_sum + extra
    image = shots_sum(local_sum)
    return (src_last, rcv_last, image)


def solution(mesh):
    return jax.shard_map(
        per_device,
        mesh=mesh,
        in_specs=(
            P("shots", "slab", None, None),
            P("shots", "slab", None, None),
            P("shots", "slab", None, None),
            P("shots", "slab", None, None),
            P("slab", None, None),
            P(None, "shots"),
            P(None, "shots", None),
            P("shots"),
            P("shots"),
            P("shots"),
            P("shots"),
            P("shots"),
            P("shots", None),
        ),
        out_specs=(
            P("shots", "slab", None, None),
            P("shots", "slab", None, None),
            P("slab", None, None),
        ),
        check_vma=False,
    )
```

```python
import jax
import jax.numpy as jnp
from jax import lax
from jax.sharding import PartitionSpec as P
from jax.experimental import pallas as pl
from jax.experimental.pallas import tpu as pltpu
import functools

STEPS = 2


COEF = (-205.0 / 72.0, 8.0 / 5.0, -1.0 / 5.0, 8.0 / 315.0, -1.0 / 560.0)


WIN_Y = 44
WIN_X = 88


def band_corner(source_y, source_x, half_y, half_x, rows_y, cols_x):
    row0 = jnp.clip(source_y - half_y, 0, rows_y - WIN_Y)
    col0 = jnp.clip(source_x - half_x, 0, cols_x - WIN_X)
    return row0, col0


def selectors(row0, col0, rows_y, cols_x):
    pick_y = (
        jnp.arange(rows_y, dtype=jnp.int32)[None, :, None]
        == row0[:, None, None] + jnp.arange(WIN_Y, dtype=jnp.int32)[None, None, :]
    ).astype(jnp.float32)
    pick_x = (
        jnp.arange(cols_x, dtype=jnp.int32)[None, None, :]
        == col0[:, None, None] + jnp.arange(WIN_X, dtype=jnp.int32)[None, :, None]
    ).astype(jnp.float32)
    return pick_y, pick_x


def exact_einsum(spec, a, b):
    return jnp.einsum(
        spec, a, b, precision=lax.Precision.HIGHEST, preferred_element_type=jnp.float32
    )


def cut_windows(layers, pick_y, pick_x):
    fields, shots, width = layers.shape[:3]
    part = exact_einsum("fsjyx,sbx->fsjyb", layers, pick_x)
    part = exact_einsum("sya,fsjyb->fsjab", pick_y, part)
    return part.reshape(fields, shots, -1, 128)


def paste_windows(flat, pick_y, pick_x, width):
    fields, shots = flat.shape[:2]
    part = flat.reshape(fields, shots, width, WIN_Y, WIN_X)
    part = exact_einsum("fsjab,sbx->fsjax", part, pick_x)
    return exact_einsum("sya,fsjax->fsjyx", pick_y, part)


def extended(block, pick_y, pick_x, width):
    count = lax.axis_size("slab")
    forward = [(i, i + 1) for i in range(count - 1)]
    backward = [(target, source) for source, target in forward]
    dim = 2
    rows_y, cols_x = block.shape[-2:]
    low = lax.ppermute(
        cut_windows(lax.slice_in_dim(block, block.shape[dim] - width, None, axis=dim), pick_y, pick_x),
        "slab",
        forward,
    )
    high = lax.ppermute(
        cut_windows(lax.slice_in_dim(block, 0, width, axis=dim), pick_y, pick_x), "slab", backward
    )
    low = paste_windows(low, pick_y, pick_x, width)
    high = paste_windows(high, pick_y, pick_x, width)
    return jnp.concatenate([low, block, high], axis=dim)


def laplace(padded):
    axis_z = padded.ndim - 3
    length = padded.shape[axis_z] - 8
    center = lax.slice_in_dim(padded, 4, 4 + length, axis=axis_z)
    total = 3.0 * COEF[0] * center
    for shift_k in range(1, 5):
        upper = lax.slice_in_dim(padded, 4 + shift_k, 4 + shift_k + length, axis=axis_z)
        lower = lax.slice_in_dim(padded, 4 - shift_k, 4 - shift_k + length, axis=axis_z)
        total = total + COEF[shift_k] * (upper + lower)
    widths = [(0, 0)] * (center.ndim - 2) + [(4, 4), (4, 4)]
    plane = jnp.pad(center, widths)
    rows_y = center.shape[-2]
    cols_x = center.shape[-1]
    for shift_k in range(1, 5):
        side_y = (
            plane[..., 4 + shift_k : 4 + shift_k + rows_y, 4 : 4 + cols_x]
            + plane[..., 4 - shift_k : 4 - shift_k + rows_y, 4 : 4 + cols_x]
        )
        side_x = (
            plane[..., 4 : 4 + rows_y, 4 + shift_k : 4 + shift_k + cols_x]
            + plane[..., 4 : 4 + rows_y, 4 - shift_k : 4 - shift_k + cols_x]
        )
        total = total + COEF[shift_k] * (side_y + side_x)
    return total


def band_mask(source_y, source_x, half_y, half_x, rows_y, cols_x):
    grid_y = jnp.arange(rows_y, dtype=jnp.int32)
    grid_x = jnp.arange(cols_x, dtype=jnp.int32)
    inside_y = jnp.abs(grid_y[None, :, None] - source_y[:, None, None]) <= half_y[:, None, None]
    inside_x = jnp.abs(grid_x[None, None, :] - source_x[:, None, None]) <= half_x[:, None, None]
    return (inside_y & inside_x).astype(jnp.float32)


def point_field(depth_local, row, col, values, length, rows_y, cols_x):
    grid_z = jnp.arange(length, dtype=jnp.int32)[None, :, None, None]
    grid_y = jnp.arange(rows_y, dtype=jnp.int32)[None, None, :, None]
    grid_x = jnp.arange(cols_x, dtype=jnp.int32)[None, None, None, :]
    hit = (
        (grid_z == depth_local[:, None, None, None])
        & (grid_y == row[:, None, None, None])
        & (grid_x == col[:, None, None, None])
    )
    return jnp.where(hit, values[:, None, None, None], 0.0)


def receiver_field(cells, traces, begin, length, rows_y, cols_x):
    plane = rows_y * cols_x
    depth = cells // plane
    rest = cells - depth * plane
    row = rest // cols_x
    col = rest - row * cols_x
    local = depth - begin
    slab_rows = jnp.arange(length * rows_y, dtype=jnp.int32)
    key = local * rows_y + row
    left = jnp.where(slab_rows[None, :, None] == key[:, None, :], traces[:, None, :], 0.0)
    right = (col[:, :, None] == jnp.arange(cols_x, dtype=jnp.int32)[None, None, :]).astype(
        jnp.float32
    )
    field = jnp.einsum(
        "szr,srx->szx",
        left,
        right,
        precision=lax.Precision.HIGHEST,
        preferred_element_type=jnp.float32,
    )
    return field.reshape(cells.shape[0], length, rows_y, cols_x)


def tree_sum(value, axis):
    count = lax.axis_size(axis)
    me = lax.axis_index(axis)
    shape = value.shape
    piece = value.reshape(-1)
    bits = []
    stride = 1
    while stride < count:
        bits.append(stride)
        stride *= 2
    for stride in bits:
        upper = (me // stride) % 2 == 1
        halves = piece.reshape(2, -1)
        send = jnp.where(upper, halves[0], halves[1])
        keep = jnp.where(upper, halves[1], halves[0])
        pairs = [(i, i ^ stride) for i in range(count)]
        piece = keep + lax.ppermute(send, axis, pairs)
    for stride in reversed(bits):
        upper = (me // stride) % 2 == 1
        pairs = [(i, i ^ stride) for i in range(count)]
        other = lax.ppermute(piece, axis, pairs)
        piece = jnp.where(upper, jnp.concatenate([other, piece]), jnp.concatenate([piece, other]))
    return piece.reshape(shape)


def allreduce_kernel(strides, local_ref, out_ref, *scratch):
    rounds = len(strides)
    halves = scratch[:rounds]
    sums = scratch[rounds : 2 * rounds]
    send_sems, recv_sems = scratch[2 * rounds], scratch[2 * rounds + 1]
    me = lax.axis_index("shots")
    slab = lax.axis_index("slab")
    mesh_id = pl.DeviceIdType.MESH
    barrier = pltpu.get_barrier_semaphore()
    for stride in strides:
        partner = me + stride - 2 * stride * ((me // stride) % 2)
        pl.semaphore_signal(barrier, inc=1, device_id=(slab, partner), device_id_type=mesh_id)
    pl.semaphore_wait(barrier, rounds)
    source = local_ref
    start = 0
    rows = local_ref.shape[0]
    for k, stride in enumerate(strides):
        upper = (me // stride) % 2
        partner = me + stride - 2 * stride * upper
        rows //= 2
        copy = pltpu.make_async_remote_copy(
            src_ref=source.at[pl.ds(pl.multiple_of((1 - upper) * rows, 8), rows)],
            dst_ref=halves[k],
            send_sem=send_sems.at[k],
            recv_sem=recv_sems.at[k],
            device_id=(slab, partner),
            device_id_type=mesh_id,
        )
        copy.start()
        copy.wait()
        kept = source[pl.ds(pl.multiple_of(upper * rows, 8), rows)]
        sums[k][...] = kept + halves[k][...]
        source = sums[k]
        start = start + upper * rows
    out_ref[pl.ds(pl.multiple_of(start, 8), rows)] = sums[rounds - 1][...]
    for k in reversed(range(rounds)):
        stride = strides[k]
        upper = (me // stride) % 2
        partner = me + stride - 2 * stride * upper
        mine = out_ref.at[pl.ds(pl.multiple_of(start, 8), rows)]
        copy = pltpu.make_async_remote_copy(
            src_ref=mine,
            dst_ref=mine,
            send_sem=send_sems.at[rounds + k],
            recv_sem=recv_sems.at[rounds + k],
            device_id=(slab, partner),
            device_id_type=mesh_id,
        )
        copy.start()
        copy.wait()
        start = start - upper * rows
        rows *= 2


def shots_sum(value):
    count = lax.axis_size("shots")
    strides = []
    stride = 1
    while stride < count:
        strides.append(stride)
        stride *= 2
    shape = value.shape
    chunks = value.reshape(-1, 128)
    rows = chunks.shape[0]
    scratch = []
    for k in range(len(strides)):
        scratch.append(pltpu.VMEM((rows >> (k + 1), 128), jnp.float32))
    for k in range(len(strides)):
        scratch.append(pltpu.VMEM((rows >> (k + 1), 128), jnp.float32))
    scratch.append(pltpu.SemaphoreType.DMA((2 * len(strides),)))
    scratch.append(pltpu.SemaphoreType.DMA((2 * len(strides),)))
    out = pl.pallas_call(
        functools.partial(allreduce_kernel, tuple(strides)),
        out_shape=jax.ShapeDtypeStruct(chunks.shape, jnp.float32),
        in_specs=[pl.BlockSpec(memory_space=pltpu.VMEM)],
        out_specs=pl.BlockSpec(memory_space=pltpu.VMEM),
        scratch_shapes=scratch,
        compiler_params=pltpu.CompilerParams(collective_id=0, has_side_effects=True),
    )(chunks)
    return out.reshape(shape)


def per_device(
    src_prev,
    src_cur,
    rcv_prev,
    rcv_cur,
    velocity,
    wavelet,
    residual_traces,
    source_depth,
    source_y,
    source_x,
    half_y,
    half_x,
    receiver_cell,
):
    shot_count, depth, rows_y, cols_x = src_cur.shape
    start = lax.axis_index("slab") * depth
    mask = band_mask(source_y, source_x, half_y, half_x, rows_y, cols_x)[:, None]
    row0, col0 = band_corner(source_y, source_x, half_y, half_x, rows_y, cols_x)
    pick_y, pick_x = selectors(row0, col0, rows_y, cols_x)
    terms = []
    up, u, vp, v = (src_prev, src_cur, rcv_prev, rcv_cur)
    for step in range(STEPS):
        stacked = jnp.stack([u, v])
        padded = extended(stacked, pick_y, pick_x, 4)
        lap = laplace(padded)
        sdelta = point_field(
            source_depth - start, source_y, source_x, wavelet[step], depth, rows_y, cols_x
        )
        rdelta = receiver_field(receiver_cell, residual_traces[step], start, depth, rows_y, cols_x)
        unew = mask * (2.0 * u - up + velocity * lap[0] + sdelta)
        vnew = mask * (2.0 * v - vp + velocity * lap[1] + rdelta)
        terms.append(jnp.sum((unew - 2.0 * u + up) * vnew, axis=0))
        up, u, vp, v = (u, unew, v, vnew)
    src_last, rcv_last = (u, v)
    local_sum = terms[0]
    for extra in terms[1:]:
        local_sum = local_sum + extra
    image = shots_sum(local_sum)
    return (src_last, rcv_last, image)


def solution(mesh):
    return jax.shard_map(
        per_device,
        mesh=mesh,
        in_specs=(
            P("shots", "slab", None, None),
            P("shots", "slab", None, None),
            P("shots", "slab", None, None),
            P("shots", "slab", None, None),
            P("slab", None, None),
            P(None, "shots"),
            P(None, "shots", None),
            P("shots"),
            P("shots"),
            P("shots"),
            P("shots"),
            P("shots"),
            P("shots", None),
        ),
        out_specs=(
            P("shots", "slab", None, None),
            P("shots", "slab", None, None),
            P("slab", None, None),
        ),
        check_vma=False,
    )
```

```python
import jax
import jax.numpy as jnp
from jax import lax
from jax.sharding import PartitionSpec as P
from jax.experimental import pallas as pl
from jax.experimental.pallas import tpu as pltpu
import functools

STEPS = 2


COEF = (-205.0 / 72.0, 8.0 / 5.0, -1.0 / 5.0, 8.0 / 315.0, -1.0 / 560.0)


WIN_Y = 44
WIN_X = 88


def band_corner(source_y, source_x, half_y, half_x, rows_y, cols_x):
    row0 = jnp.clip(source_y - half_y, 0, rows_y - WIN_Y)
    col0 = jnp.clip(source_x - half_x, 0, cols_x - WIN_X)
    return row0, col0


def selectors(row0, col0, rows_y, cols_x):
    pick_y = (
        jnp.arange(rows_y, dtype=jnp.int32)[None, :, None]
        == row0[:, None, None] + jnp.arange(WIN_Y, dtype=jnp.int32)[None, None, :]
    ).astype(jnp.float32)
    pick_x = (
        jnp.arange(cols_x, dtype=jnp.int32)[None, None, :]
        == col0[:, None, None] + jnp.arange(WIN_X, dtype=jnp.int32)[None, :, None]
    ).astype(jnp.float32)
    return pick_y, pick_x


def exact_einsum(spec, a, b):
    return jnp.einsum(
        spec, a, b, precision=lax.Precision.HIGHEST, preferred_element_type=jnp.float32
    )


def cut_windows(layers, pick_y, pick_x):
    fields, shots, width = layers.shape[:3]
    part = exact_einsum("fsjyx,sbx->fsjyb", layers, pick_x)
    part = exact_einsum("sya,fsjyb->fsjab", pick_y, part)
    return part.reshape(fields, shots, -1, 128)


def paste_windows(flat, pick_y, pick_x, width):
    fields, shots = flat.shape[:2]
    part = flat.reshape(fields, shots, width, WIN_Y, WIN_X)
    part = exact_einsum("fsjab,sbx->fsjax", part, pick_x)
    return exact_einsum("sya,fsjax->fsjyx", pick_y, part)


def halo_kernel(n, lo_send, hi_send, lo_recv, hi_recv, relay_f, relay_b, sems):
    i = lax.axis_index("slab")
    shot = lax.axis_index("shots")
    x = i % 4
    part = lo_send.shape[0] // 3
    mesh_id = pl.DeviceIdType.MESH
    barrier = pltpu.get_barrier_semaphore()
    greeted = 0
    for d in (-3, -2, -1, 1, 2, 3):
        ok = (i + d >= 0) & (i + d < n)

        @pl.when(ok)
        def _():
            pl.semaphore_signal(barrier, inc=1, device_id=(i + d, shot), device_id_type=mesh_id)

        greeted = greeted + ok.astype(jnp.int32)
    pl.semaphore_wait(barrier, greeted)

    def rows(p):
        return pl.ds(p * part, part)

    def remote(src, dst, send, recv, target):
        return pltpu.make_async_remote_copy(
            src_ref=src,
            dst_ref=dst,
            send_sem=sems.at[send],
            recv_sem=sems.at[recv],
            device_id=(target, shot),
            device_id_type=mesh_id,
        )

    has_up = i + 1 < n
    has_down = i >= 1
    up_far = x == 3
    down_far = x == 0
    for p in range(3):
        direct_up = has_up if p == 0 else has_up & jnp.logical_not(up_far)

        @pl.when(direct_up)
        def _():
            remote(lo_send.at[rows(p)], lo_recv.at[rows(p)], p, 8 + p, i + 1).start()

        direct_down = has_down if p == 0 else has_down & jnp.logical_not(down_far)

        @pl.when(direct_down)
        def _():
            remote(hi_send.at[rows(p)], hi_recv.at[rows(p)], 3 + p, 11 + p, i - 1).start()

        if p > 0:

            @pl.when(has_up & up_far)
            def _():
                remote(lo_send.at[rows(p)], relay_f, p, 14, i + 1 + p).start()

            @pl.when(has_down & down_far)
            def _():
                remote(hi_send.at[rows(p)], relay_b, 3 + p, 15, i - 4 + p).start()

    for p in (1, 2):
        fwd = (x == p) & (i - 1 - p >= 0)

        @pl.when(fwd)
        def _():
            remote(lo_send.at[rows(p)], relay_f, p, 14, i).wait_recv()
            copy = remote(relay_f, lo_recv.at[rows(p)], 6, 8 + p, i - p)
            copy.start()
            copy.wait_send()

        bwd = (x == p) & (i + 4 - p < n)

        @pl.when(bwd)
        def _():
            remote(hi_send.at[rows(p)], relay_b, 3 + p, 15, i).wait_recv()
            copy = remote(relay_b, hi_recv.at[rows(p)], 7, 11 + p, i + 3 - p)
            copy.start()
            copy.wait_send()

    for p in range(3):

        @pl.when(has_up)
        def _():
            remote(lo_send.at[rows(p)], lo_recv.at[rows(p)], p, 8 + p, i + 1).wait_send()

        @pl.when(has_down)
        def _():
            remote(hi_send.at[rows(p)], hi_recv.at[rows(p)], 3 + p, 11 + p, i - 1).wait_send()

        @pl.when(has_down)
        def _():
            remote(lo_send.at[rows(p)], lo_recv.at[rows(p)], p, 8 + p, i).wait_recv()

        @pl.when(has_up)
        def _():
            remote(hi_send.at[rows(p)], hi_recv.at[rows(p)], 3 + p, 11 + p, i).wait_recv()


def exchange(lo_flat, hi_flat, call_id):
    n = lax.axis_size("slab")
    shape = lo_flat.shape
    total = lo_flat.size // 128
    part = -(-total // 24) * 8
    padded = 3 * part

    def prep(a):
        return jnp.pad(a.reshape(total, 128), ((0, padded - total), (0, 0)))

    vmem = pl.BlockSpec(memory_space=pltpu.VMEM)
    lo_recv, hi_recv = pl.pallas_call(
        functools.partial(halo_kernel, n),
        out_shape=(
            jax.ShapeDtypeStruct((padded, 128), jnp.float32),
            jax.ShapeDtypeStruct((padded, 128), jnp.float32),
        ),
        in_specs=[vmem, vmem],
        out_specs=(vmem, vmem),
        scratch_shapes=[
            pltpu.VMEM((part, 128), jnp.float32),
            pltpu.VMEM((part, 128), jnp.float32),
            pltpu.SemaphoreType.DMA((16,)),
        ],
        compiler_params=pltpu.CompilerParams(collective_id=call_id, has_side_effects=True),
    )(prep(lo_flat), prep(hi_flat))
    return lo_recv[:total].reshape(shape), hi_recv[:total].reshape(shape)


def extended(block, pick_y, pick_x, width, call_id):
    dim = 2
    lo_flat = cut_windows(
        lax.slice_in_dim(block, block.shape[dim] - width, None, axis=dim), pick_y, pick_x
    )
    hi_flat = cut_windows(lax.slice_in_dim(block, 0, width, axis=dim), pick_y, pick_x)
    low, high = exchange(lo_flat, hi_flat, call_id)
    i = lax.axis_index("slab")
    low = jnp.where(i >= 1, low, 0.0)
    high = jnp.where(i + 1 < lax.axis_size("slab"), high, 0.0)
    low = paste_windows(low, pick_y, pick_x, width)
    high = paste_windows(high, pick_y, pick_x, width)
    return jnp.concatenate([low, block, high], axis=dim)


def laplace(padded):
    axis_z = padded.ndim - 3
    length = padded.shape[axis_z] - 8
    center = lax.slice_in_dim(padded, 4, 4 + length, axis=axis_z)
    total = 3.0 * COEF[0] * center
    for shift_k in range(1, 5):
        upper = lax.slice_in_dim(padded, 4 + shift_k, 4 + shift_k + length, axis=axis_z)
        lower = lax.slice_in_dim(padded, 4 - shift_k, 4 - shift_k + length, axis=axis_z)
        total = total + COEF[shift_k] * (upper + lower)
    widths = [(0, 0)] * (center.ndim - 2) + [(4, 4), (4, 4)]
    plane = jnp.pad(center, widths)
    rows_y = center.shape[-2]
    cols_x = center.shape[-1]
    for shift_k in range(1, 5):
        side_y = (
            plane[..., 4 + shift_k : 4 + shift_k + rows_y, 4 : 4 + cols_x]
            + plane[..., 4 - shift_k : 4 - shift_k + rows_y, 4 : 4 + cols_x]
        )
        side_x = (
            plane[..., 4 : 4 + rows_y, 4 + shift_k : 4 + shift_k + cols_x]
            + plane[..., 4 : 4 + rows_y, 4 - shift_k : 4 - shift_k + cols_x]
        )
        total = total + COEF[shift_k] * (side_y + side_x)
    return total


def band_mask(source_y, source_x, half_y, half_x, rows_y, cols_x):
    grid_y = jnp.arange(rows_y, dtype=jnp.int32)
    grid_x = jnp.arange(cols_x, dtype=jnp.int32)
    inside_y = jnp.abs(grid_y[None, :, None] - source_y[:, None, None]) <= half_y[:, None, None]
    inside_x = jnp.abs(grid_x[None, None, :] - source_x[:, None, None]) <= half_x[:, None, None]
    return (inside_y & inside_x).astype(jnp.float32)


def point_field(depth_local, row, col, values, length, rows_y, cols_x):
    grid_z = jnp.arange(length, dtype=jnp.int32)[None, :, None, None]
    grid_y = jnp.arange(rows_y, dtype=jnp.int32)[None, None, :, None]
    grid_x = jnp.arange(cols_x, dtype=jnp.int32)[None, None, None, :]
    hit = (
        (grid_z == depth_local[:, None, None, None])
        & (grid_y == row[:, None, None, None])
        & (grid_x == col[:, None, None, None])
    )
    return jnp.where(hit, values[:, None, None, None], 0.0)


def receiver_field(cells, traces, begin, length, rows_y, cols_x):
    plane = rows_y * cols_x
    depth = cells // plane
    rest = cells - depth * plane
    row = rest // cols_x
    col = rest - row * cols_x
    local = depth - begin
    slab_rows = jnp.arange(length * rows_y, dtype=jnp.int32)
    key = local * rows_y + row
    left = jnp.where(slab_rows[None, :, None] == key[:, None, :], traces[:, None, :], 0.0)
    right = (col[:, :, None] == jnp.arange(cols_x, dtype=jnp.int32)[None, None, :]).astype(
        jnp.float32
    )
    field = jnp.einsum(
        "szr,srx->szx",
        left,
        right,
        precision=lax.Precision.HIGHEST,
        preferred_element_type=jnp.float32,
    )
    return field.reshape(cells.shape[0], length, rows_y, cols_x)


def tree_sum(value, axis):
    count = lax.axis_size(axis)
    me = lax.axis_index(axis)
    shape = value.shape
    piece = value.reshape(-1)
    bits = []
    stride = 1
    while stride < count:
        bits.append(stride)
        stride *= 2
    for stride in bits:
        upper = (me // stride) % 2 == 1
        halves = piece.reshape(2, -1)
        send = jnp.where(upper, halves[0], halves[1])
        keep = jnp.where(upper, halves[1], halves[0])
        pairs = [(i, i ^ stride) for i in range(count)]
        piece = keep + lax.ppermute(send, axis, pairs)
    for stride in reversed(bits):
        upper = (me // stride) % 2 == 1
        pairs = [(i, i ^ stride) for i in range(count)]
        other = lax.ppermute(piece, axis, pairs)
        piece = jnp.where(upper, jnp.concatenate([other, piece]), jnp.concatenate([piece, other]))
    return piece.reshape(shape)


def allreduce_kernel(strides, local_ref, out_ref, *scratch):
    rounds = len(strides)
    halves = scratch[:rounds]
    sums = scratch[rounds : 2 * rounds]
    send_sems, recv_sems = scratch[2 * rounds], scratch[2 * rounds + 1]
    me = lax.axis_index("shots")
    slab = lax.axis_index("slab")
    mesh_id = pl.DeviceIdType.MESH
    barrier = pltpu.get_barrier_semaphore()
    for stride in strides:
        partner = me + stride - 2 * stride * ((me // stride) % 2)
        pl.semaphore_signal(barrier, inc=1, device_id=(slab, partner), device_id_type=mesh_id)
    pl.semaphore_wait(barrier, rounds)
    source = local_ref
    start = 0
    rows = local_ref.shape[0]
    for k, stride in enumerate(strides):
        upper = (me // stride) % 2
        partner = me + stride - 2 * stride * upper
        rows //= 2
        copy = pltpu.make_async_remote_copy(
            src_ref=source.at[pl.ds(pl.multiple_of((1 - upper) * rows, 8), rows)],
            dst_ref=halves[k],
            send_sem=send_sems.at[k],
            recv_sem=recv_sems.at[k],
            device_id=(slab, partner),
            device_id_type=mesh_id,
        )
        copy.start()
        copy.wait()
        kept = source[pl.ds(pl.multiple_of(upper * rows, 8), rows)]
        sums[k][...] = kept + halves[k][...]
        source = sums[k]
        start = start + upper * rows
    out_ref[pl.ds(pl.multiple_of(start, 8), rows)] = sums[rounds - 1][...]
    for k in reversed(range(rounds)):
        stride = strides[k]
        upper = (me // stride) % 2
        partner = me + stride - 2 * stride * upper
        mine = out_ref.at[pl.ds(pl.multiple_of(start, 8), rows)]
        copy = pltpu.make_async_remote_copy(
            src_ref=mine,
            dst_ref=mine,
            send_sem=send_sems.at[rounds + k],
            recv_sem=recv_sems.at[rounds + k],
            device_id=(slab, partner),
            device_id_type=mesh_id,
        )
        copy.start()
        copy.wait()
        start = start - upper * rows
        rows *= 2


def shots_sum(value):
    count = lax.axis_size("shots")
    strides = []
    stride = 1
    while stride < count:
        strides.append(stride)
        stride *= 2
    shape = value.shape
    chunks = value.reshape(-1, 128)
    rows = chunks.shape[0]
    scratch = []
    for k in range(len(strides)):
        scratch.append(pltpu.VMEM((rows >> (k + 1), 128), jnp.float32))
    for k in range(len(strides)):
        scratch.append(pltpu.VMEM((rows >> (k + 1), 128), jnp.float32))
    scratch.append(pltpu.SemaphoreType.DMA((2 * len(strides),)))
    scratch.append(pltpu.SemaphoreType.DMA((2 * len(strides),)))
    out = pl.pallas_call(
        functools.partial(allreduce_kernel, tuple(strides)),
        out_shape=jax.ShapeDtypeStruct(chunks.shape, jnp.float32),
        in_specs=[pl.BlockSpec(memory_space=pltpu.VMEM)],
        out_specs=pl.BlockSpec(memory_space=pltpu.VMEM),
        scratch_shapes=scratch,
        compiler_params=pltpu.CompilerParams(collective_id=0, has_side_effects=True),
    )(chunks)
    return out.reshape(shape)


def per_device(
    src_prev,
    src_cur,
    rcv_prev,
    rcv_cur,
    velocity,
    wavelet,
    residual_traces,
    source_depth,
    source_y,
    source_x,
    half_y,
    half_x,
    receiver_cell,
):
    shot_count, depth, rows_y, cols_x = src_cur.shape
    start = lax.axis_index("slab") * depth
    mask = band_mask(source_y, source_x, half_y, half_x, rows_y, cols_x)[:, None]
    row0, col0 = band_corner(source_y, source_x, half_y, half_x, rows_y, cols_x)
    pick_y, pick_x = selectors(row0, col0, rows_y, cols_x)
    terms = []
    up, u, vp, v = (src_prev, src_cur, rcv_prev, rcv_cur)
    for step in range(STEPS):
        stacked = jnp.stack([u, v])
        padded = extended(stacked, pick_y, pick_x, 4, 1 + step)
        lap = laplace(padded)
        sdelta = point_field(
            source_depth - start, source_y, source_x, wavelet[step], depth, rows_y, cols_x
        )
        rdelta = receiver_field(receiver_cell, residual_traces[step], start, depth, rows_y, cols_x)
        unew = mask * (2.0 * u - up + velocity * lap[0] + sdelta)
        vnew = mask * (2.0 * v - vp + velocity * lap[1] + rdelta)
        terms.append(jnp.sum((unew - 2.0 * u + up) * vnew, axis=0))
        up, u, vp, v = (u, unew, v, vnew)
    src_last, rcv_last = (u, v)
    local_sum = terms[0]
    for extra in terms[1:]:
        local_sum = local_sum + extra
    image = shots_sum(local_sum)
    return (src_last, rcv_last, image)


def solution(mesh):
    return jax.shard_map(
        per_device,
        mesh=mesh,
        in_specs=(
            P("shots", "slab", None, None),
            P("shots", "slab", None, None),
            P("shots", "slab", None, None),
            P("shots", "slab", None, None),
            P("slab", None, None),
            P(None, "shots"),
            P(None, "shots", None),
            P("shots"),
            P("shots"),
            P("shots"),
            P("shots"),
            P("shots"),
            P("shots", None),
        ),
        out_specs=(
            P("shots", "slab", None, None),
            P("shots", "slab", None, None),
            P("slab", None, None),
        ),
        check_vma=False,
    )
```

```python
import jax
import jax.numpy as jnp
from jax import lax
from jax.sharding import PartitionSpec as P
from jax.experimental import pallas as pl
from jax.experimental.pallas import tpu as pltpu
import functools

STEPS = 2


COEF = (-205.0 / 72.0, 8.0 / 5.0, -1.0 / 5.0, 8.0 / 315.0, -1.0 / 560.0)


WIN_Y = 44
WIN_X = 88


def band_corner(source_y, source_x, half_y, half_x, rows_y, cols_x):
    row0 = jnp.clip(source_y - half_y, 0, rows_y - WIN_Y)
    col0 = jnp.clip(source_x - half_x, 0, cols_x - WIN_X)
    return row0, col0


def selectors(row0, col0, rows_y, cols_x):
    pick_y = (
        jnp.arange(rows_y, dtype=jnp.int32)[None, :, None]
        == row0[:, None, None] + jnp.arange(WIN_Y, dtype=jnp.int32)[None, None, :]
    ).astype(jnp.float32)
    pick_x = (
        jnp.arange(cols_x, dtype=jnp.int32)[None, None, :]
        == col0[:, None, None] + jnp.arange(WIN_X, dtype=jnp.int32)[None, :, None]
    ).astype(jnp.float32)
    return pick_y, pick_x


def exact_einsum(spec, a, b):
    return jnp.einsum(
        spec, a, b, precision=lax.Precision.HIGHEST, preferred_element_type=jnp.float32
    )


def cut_windows(layers, pick_y, pick_x):
    fields, shots, width = layers.shape[:3]
    part = exact_einsum("fsjyx,sbx->fsjyb", layers, pick_x)
    part = exact_einsum("sya,fsjyb->fsjab", pick_y, part)
    return part.reshape(fields, shots, -1, 128)


def paste_windows(flat, pick_y, pick_x, width):
    fields, shots = flat.shape[:2]
    part = flat.reshape(fields, shots, width, WIN_Y, WIN_X)
    part = exact_einsum("fsjab,sbx->fsjax", part, pick_x)
    return exact_einsum("sya,fsjax->fsjyx", pick_y, part)


def halo_kernel(n, lo_send, hi_send, lo_recv, hi_recv, relay_f, relay_b, sems):
    i = lax.axis_index("slab")
    shot = lax.axis_index("shots")
    x = i % 4
    part = lo_send.shape[0] // 3
    mesh_id = pl.DeviceIdType.MESH
    barrier = pltpu.get_barrier_semaphore()
    greeted = 0
    for d in (-3, -2, -1, 1, 2, 3):
        ok = (i + d >= 0) & (i + d < n)

        @pl.when(ok)
        def _():
            pl.semaphore_signal(barrier, inc=1, device_id=(i + d, shot), device_id_type=mesh_id)

        greeted = greeted + ok.astype(jnp.int32)
    pl.semaphore_wait(barrier, greeted)

    def rows(p):
        return pl.ds(p * part, part)

    def remote(src, dst, send, recv, target):
        return pltpu.make_async_remote_copy(
            src_ref=src,
            dst_ref=dst,
            send_sem=sems.at[send],
            recv_sem=sems.at[recv],
            device_id=(target, shot),
            device_id_type=mesh_id,
        )

    has_up = i + 1 < n
    has_down = i >= 1
    up_far = x == 3
    down_far = x == 0
    for p in range(3):
        direct_up = has_up if p == 0 else has_up & jnp.logical_not(up_far)

        @pl.when(direct_up)
        def _():
            remote(lo_send.at[rows(p)], lo_recv.at[rows(p)], p, 8 + p, i + 1).start()

        direct_down = has_down if p == 0 else has_down & jnp.logical_not(down_far)

        @pl.when(direct_down)
        def _():
            remote(hi_send.at[rows(p)], hi_recv.at[rows(p)], 3 + p, 11 + p, i - 1).start()

        if p > 0:

            @pl.when(has_up & up_far)
            def _():
                remote(lo_send.at[rows(p)], relay_f, p, 14, i - 3 + p).start()

            @pl.when(has_down & down_far)
            def _():
                remote(hi_send.at[rows(p)], relay_b, 3 + p, 15, i + p).start()

    for p in (1, 2):
        fwd = (x == p) & (i + 4 - p < n)

        @pl.when(fwd)
        def _():
            remote(lo_send.at[rows(p)], relay_f, p, 14, i).wait_recv()
            copy = remote(relay_f, lo_recv.at[rows(p)], 6, 8 + p, i + 4 - p)
            copy.start()
            copy.wait_send()

        bwd = (x == p) & (i - p >= 1)

        @pl.when(bwd)
        def _():
            remote(hi_send.at[rows(p)], relay_b, 3 + p, 15, i).wait_recv()
            copy = remote(relay_b, hi_recv.at[rows(p)], 7, 11 + p, i - p - 1)
            copy.start()
            copy.wait_send()

    for p in range(3):

        @pl.when(has_up)
        def _():
            remote(lo_send.at[rows(p)], lo_recv.at[rows(p)], p, 8 + p, i + 1).wait_send()

        @pl.when(has_down)
        def _():
            remote(hi_send.at[rows(p)], hi_recv.at[rows(p)], 3 + p, 11 + p, i - 1).wait_send()

        @pl.when(has_down)
        def _():
            remote(lo_send.at[rows(p)], lo_recv.at[rows(p)], p, 8 + p, i).wait_recv()

        @pl.when(has_up)
        def _():
            remote(hi_send.at[rows(p)], hi_recv.at[rows(p)], 3 + p, 11 + p, i).wait_recv()


def exchange(lo_flat, hi_flat, call_id):
    n = lax.axis_size("slab")
    shape = lo_flat.shape
    total = lo_flat.size // 128
    part = -(-total // 24) * 8
    padded = 3 * part

    def prep(a):
        return jnp.pad(a.reshape(total, 128), ((0, padded - total), (0, 0)))

    vmem = pl.BlockSpec(memory_space=pltpu.VMEM)
    lo_recv, hi_recv = pl.pallas_call(
        functools.partial(halo_kernel, n),
        out_shape=(
            jax.ShapeDtypeStruct((padded, 128), jnp.float32),
            jax.ShapeDtypeStruct((padded, 128), jnp.float32),
        ),
        in_specs=[vmem, vmem],
        out_specs=(vmem, vmem),
        scratch_shapes=[
            pltpu.VMEM((part, 128), jnp.float32),
            pltpu.VMEM((part, 128), jnp.float32),
            pltpu.SemaphoreType.DMA((16,)),
        ],
        compiler_params=pltpu.CompilerParams(collective_id=call_id, has_side_effects=True),
    )(prep(lo_flat), prep(hi_flat))
    return lo_recv[:total].reshape(shape), hi_recv[:total].reshape(shape)


def extended(block, pick_y, pick_x, width, call_id):
    dim = 2
    lo_flat = cut_windows(
        lax.slice_in_dim(block, block.shape[dim] - width, None, axis=dim), pick_y, pick_x
    )
    hi_flat = cut_windows(lax.slice_in_dim(block, 0, width, axis=dim), pick_y, pick_x)
    low, high = exchange(lo_flat, hi_flat, call_id)
    i = lax.axis_index("slab")
    low = jnp.where(i >= 1, low, 0.0)
    high = jnp.where(i + 1 < lax.axis_size("slab"), high, 0.0)
    low = paste_windows(low, pick_y, pick_x, width)
    high = paste_windows(high, pick_y, pick_x, width)
    return jnp.concatenate([low, block, high], axis=dim)


def laplace(padded):
    axis_z = padded.ndim - 3
    length = padded.shape[axis_z] - 8
    center = lax.slice_in_dim(padded, 4, 4 + length, axis=axis_z)
    total = 3.0 * COEF[0] * center
    for shift_k in range(1, 5):
        upper = lax.slice_in_dim(padded, 4 + shift_k, 4 + shift_k + length, axis=axis_z)
        lower = lax.slice_in_dim(padded, 4 - shift_k, 4 - shift_k + length, axis=axis_z)
        total = total + COEF[shift_k] * (upper + lower)
    widths = [(0, 0)] * (center.ndim - 2) + [(4, 4), (4, 4)]
    plane = jnp.pad(center, widths)
    rows_y = center.shape[-2]
    cols_x = center.shape[-1]
    for shift_k in range(1, 5):
        side_y = (
            plane[..., 4 + shift_k : 4 + shift_k + rows_y, 4 : 4 + cols_x]
            + plane[..., 4 - shift_k : 4 - shift_k + rows_y, 4 : 4 + cols_x]
        )
        side_x = (
            plane[..., 4 : 4 + rows_y, 4 + shift_k : 4 + shift_k + cols_x]
            + plane[..., 4 : 4 + rows_y, 4 - shift_k : 4 - shift_k + cols_x]
        )
        total = total + COEF[shift_k] * (side_y + side_x)
    return total


def band_mask(source_y, source_x, half_y, half_x, rows_y, cols_x):
    grid_y = jnp.arange(rows_y, dtype=jnp.int32)
    grid_x = jnp.arange(cols_x, dtype=jnp.int32)
    inside_y = jnp.abs(grid_y[None, :, None] - source_y[:, None, None]) <= half_y[:, None, None]
    inside_x = jnp.abs(grid_x[None, None, :] - source_x[:, None, None]) <= half_x[:, None, None]
    return (inside_y & inside_x).astype(jnp.float32)


def point_field(depth_local, row, col, values, length, rows_y, cols_x):
    grid_z = jnp.arange(length, dtype=jnp.int32)[None, :, None, None]
    grid_y = jnp.arange(rows_y, dtype=jnp.int32)[None, None, :, None]
    grid_x = jnp.arange(cols_x, dtype=jnp.int32)[None, None, None, :]
    hit = (
        (grid_z == depth_local[:, None, None, None])
        & (grid_y == row[:, None, None, None])
        & (grid_x == col[:, None, None, None])
    )
    return jnp.where(hit, values[:, None, None, None], 0.0)


def receiver_field(cells, traces, begin, length, rows_y, cols_x):
    plane = rows_y * cols_x
    depth = cells // plane
    rest = cells - depth * plane
    row = rest // cols_x
    col = rest - row * cols_x
    local = depth - begin
    slab_rows = jnp.arange(length * rows_y, dtype=jnp.int32)
    key = local * rows_y + row
    left = jnp.where(slab_rows[None, :, None] == key[:, None, :], traces[:, None, :], 0.0)
    right = (col[:, :, None] == jnp.arange(cols_x, dtype=jnp.int32)[None, None, :]).astype(
        jnp.float32
    )
    field = jnp.einsum(
        "szr,srx->szx",
        left,
        right,
        precision=lax.Precision.HIGHEST,
        preferred_element_type=jnp.float32,
    )
    return field.reshape(cells.shape[0], length, rows_y, cols_x)


def tree_sum(value, axis):
    count = lax.axis_size(axis)
    me = lax.axis_index(axis)
    shape = value.shape
    piece = value.reshape(-1)
    bits = []
    stride = 1
    while stride < count:
        bits.append(stride)
        stride *= 2
    for stride in bits:
        upper = (me // stride) % 2 == 1
        halves = piece.reshape(2, -1)
        send = jnp.where(upper, halves[0], halves[1])
        keep = jnp.where(upper, halves[1], halves[0])
        pairs = [(i, i ^ stride) for i in range(count)]
        piece = keep + lax.ppermute(send, axis, pairs)
    for stride in reversed(bits):
        upper = (me // stride) % 2 == 1
        pairs = [(i, i ^ stride) for i in range(count)]
        other = lax.ppermute(piece, axis, pairs)
        piece = jnp.where(upper, jnp.concatenate([other, piece]), jnp.concatenate([piece, other]))
    return piece.reshape(shape)


def allreduce_kernel(strides, local_ref, out_ref, *scratch):
    rounds = len(strides)
    halves = scratch[:rounds]
    sums = scratch[rounds : 2 * rounds]
    send_sems, recv_sems = scratch[2 * rounds], scratch[2 * rounds + 1]
    me = lax.axis_index("shots")
    slab = lax.axis_index("slab")
    mesh_id = pl.DeviceIdType.MESH
    barrier = pltpu.get_barrier_semaphore()
    for stride in strides:
        partner = me + stride - 2 * stride * ((me // stride) % 2)
        pl.semaphore_signal(barrier, inc=1, device_id=(slab, partner), device_id_type=mesh_id)
    pl.semaphore_wait(barrier, rounds)
    source = local_ref
    start = 0
    rows = local_ref.shape[0]
    for k, stride in enumerate(strides):
        upper = (me // stride) % 2
        partner = me + stride - 2 * stride * upper
        rows //= 2
        copy = pltpu.make_async_remote_copy(
            src_ref=source.at[pl.ds(pl.multiple_of((1 - upper) * rows, 8), rows)],
            dst_ref=halves[k],
            send_sem=send_sems.at[k],
            recv_sem=recv_sems.at[k],
            device_id=(slab, partner),
            device_id_type=mesh_id,
        )
        copy.start()
        copy.wait()
        kept = source[pl.ds(pl.multiple_of(upper * rows, 8), rows)]
        sums[k][...] = kept + halves[k][...]
        source = sums[k]
        start = start + upper * rows
    out_ref[pl.ds(pl.multiple_of(start, 8), rows)] = sums[rounds - 1][...]
    for k in reversed(range(rounds)):
        stride = strides[k]
        upper = (me // stride) % 2
        partner = me + stride - 2 * stride * upper
        mine = out_ref.at[pl.ds(pl.multiple_of(start, 8), rows)]
        copy = pltpu.make_async_remote_copy(
            src_ref=mine,
            dst_ref=mine,
            send_sem=send_sems.at[rounds + k],
            recv_sem=recv_sems.at[rounds + k],
            device_id=(slab, partner),
            device_id_type=mesh_id,
        )
        copy.start()
        copy.wait()
        start = start - upper * rows
        rows *= 2


def shots_sum(value):
    count = lax.axis_size("shots")
    strides = []
    stride = 1
    while stride < count:
        strides.append(stride)
        stride *= 2
    shape = value.shape
    chunks = value.reshape(-1, 128)
    rows = chunks.shape[0]
    scratch = []
    for k in range(len(strides)):
        scratch.append(pltpu.VMEM((rows >> (k + 1), 128), jnp.float32))
    for k in range(len(strides)):
        scratch.append(pltpu.VMEM((rows >> (k + 1), 128), jnp.float32))
    scratch.append(pltpu.SemaphoreType.DMA((2 * len(strides),)))
    scratch.append(pltpu.SemaphoreType.DMA((2 * len(strides),)))
    out = pl.pallas_call(
        functools.partial(allreduce_kernel, tuple(strides)),
        out_shape=jax.ShapeDtypeStruct(chunks.shape, jnp.float32),
        in_specs=[pl.BlockSpec(memory_space=pltpu.VMEM)],
        out_specs=pl.BlockSpec(memory_space=pltpu.VMEM),
        scratch_shapes=scratch,
        compiler_params=pltpu.CompilerParams(collective_id=0, has_side_effects=True),
    )(chunks)
    return out.reshape(shape)


def per_device(
    src_prev,
    src_cur,
    rcv_prev,
    rcv_cur,
    velocity,
    wavelet,
    residual_traces,
    source_depth,
    source_y,
    source_x,
    half_y,
    half_x,
    receiver_cell,
):
    shot_count, depth, rows_y, cols_x = src_cur.shape
    start = lax.axis_index("slab") * depth
    mask = band_mask(source_y, source_x, half_y, half_x, rows_y, cols_x)[:, None]
    row0, col0 = band_corner(source_y, source_x, half_y, half_x, rows_y, cols_x)
    pick_y, pick_x = selectors(row0, col0, rows_y, cols_x)
    terms = []
    up, u, vp, v = (src_prev, src_cur, rcv_prev, rcv_cur)
    for step in range(STEPS):
        stacked = jnp.stack([u, v])
        padded = extended(stacked, pick_y, pick_x, 4, 1 + step)
        lap = laplace(padded)
        sdelta = point_field(
            source_depth - start, source_y, source_x, wavelet[step], depth, rows_y, cols_x
        )
        rdelta = receiver_field(receiver_cell, residual_traces[step], start, depth, rows_y, cols_x)
        unew = mask * (2.0 * u - up + velocity * lap[0] + sdelta)
        vnew = mask * (2.0 * v - vp + velocity * lap[1] + rdelta)
        terms.append(jnp.sum((unew - 2.0 * u + up) * vnew, axis=0))
        up, u, vp, v = (u, unew, v, vnew)
    src_last, rcv_last = (u, v)
    local_sum = terms[0]
    for extra in terms[1:]:
        local_sum = local_sum + extra
    image = shots_sum(local_sum)
    return (src_last, rcv_last, image)


def solution(mesh):
    return jax.shard_map(
        per_device,
        mesh=mesh,
        in_specs=(
            P("shots", "slab", None, None),
            P("shots", "slab", None, None),
            P("shots", "slab", None, None),
            P("shots", "slab", None, None),
            P("slab", None, None),
            P(None, "shots"),
            P(None, "shots", None),
            P("shots"),
            P("shots"),
            P("shots"),
            P("shots"),
            P("shots"),
            P("shots", None),
        ),
        out_specs=(
            P("shots", "slab", None, None),
            P("shots", "slab", None, None),
            P("slab", None, None),
        ),
        check_vma=False,
    )
```

```python
import jax
import jax.numpy as jnp
from jax import lax
from jax.sharding import PartitionSpec as P
from jax.experimental import pallas as pl
from jax.experimental.pallas import tpu as pltpu
import functools

STEPS = 2


COEF = (-205.0 / 72.0, 8.0 / 5.0, -1.0 / 5.0, 8.0 / 315.0, -1.0 / 560.0)


WIN_Y = 44
WIN_X = 88


def band_corner(source_y, source_x, half_y, half_x, rows_y, cols_x):
    row0 = jnp.clip(source_y - half_y, 0, rows_y - WIN_Y)
    col0 = jnp.clip(source_x - half_x, 0, cols_x - WIN_X)
    return row0, col0


def selectors(row0, col0, rows_y, cols_x):
    pick_y = (
        jnp.arange(rows_y, dtype=jnp.int32)[None, :, None]
        == row0[:, None, None] + jnp.arange(WIN_Y, dtype=jnp.int32)[None, None, :]
    ).astype(jnp.float32)
    pick_x = (
        jnp.arange(cols_x, dtype=jnp.int32)[None, None, :]
        == col0[:, None, None] + jnp.arange(WIN_X, dtype=jnp.int32)[None, :, None]
    ).astype(jnp.float32)
    return pick_y, pick_x


def exact_einsum(spec, a, b):
    return jnp.einsum(
        spec, a, b, precision=lax.Precision.HIGHEST, preferred_element_type=jnp.float32
    )


def cut_windows(layers, pick_y, pick_x):
    fields, shots, width = layers.shape[:3]
    part = exact_einsum("fsjyx,sbx->fsjyb", layers, pick_x)
    part = exact_einsum("sya,fsjyb->fsjab", pick_y, part)
    return part.reshape(fields, shots, -1, 128)


def paste_windows(flat, pick_y, pick_x, width):
    fields, shots = flat.shape[:2]
    part = flat.reshape(fields, shots, width, WIN_Y, WIN_X)
    part = exact_einsum("fsjab,sbx->fsjax", part, pick_x)
    return exact_einsum("sya,fsjax->fsjyx", pick_y, part)


def halo_kernel(n, lo_send, hi_send, lo_recv, hi_recv, f_near, f_far, b_near, b_far, sems):
    i = lax.axis_index("slab")
    shot = lax.axis_index("shots")
    x = i % 4
    part = lo_send.shape[0] // 3
    mesh_id = pl.DeviceIdType.MESH
    barrier = pltpu.get_barrier_semaphore()
    greeted = 0
    for d in (-4, -3, -2, -1, 1, 2, 3, 4):
        ok = (i + d >= 0) & (i + d < n)

        @pl.when(ok)
        def _():
            pl.semaphore_signal(barrier, inc=1, device_id=(i + d, shot), device_id_type=mesh_id)

        greeted = greeted + ok.astype(jnp.int32)
    pl.semaphore_wait(barrier, greeted)

    def rows(p):
        return pl.ds(p * part, part)

    def remote(src, dst, send, recv, target):
        return pltpu.make_async_remote_copy(
            src_ref=src,
            dst_ref=dst,
            send_sem=sems.at[send],
            recv_sem=sems.at[recv],
            device_id=(target, shot),
            device_id_type=mesh_id,
        )

    has_up = i + 1 < n
    has_down = i >= 1
    up_far = x == 3
    down_far = x == 0
    for p in range(3):
        direct_up = has_up if p == 0 else has_up & jnp.logical_not(up_far)

        @pl.when(direct_up)
        def _():
            remote(lo_send.at[rows(p)], lo_recv.at[rows(p)], p, 10 + p, i + 1).start()

        direct_down = has_down if p == 0 else has_down & jnp.logical_not(down_far)

        @pl.when(direct_down)
        def _():
            remote(hi_send.at[rows(p)], hi_recv.at[rows(p)], 3 + p, 13 + p, i - 1).start()

        if p > 0:

            @pl.when(has_up & up_far)
            def _():
                remote(lo_send.at[rows(p)], f_near, p, 16, i - 3 + p).start()

            @pl.when(has_down & down_far)
            def _():
                remote(hi_send.at[rows(p)], b_near, 3 + p, 18, i + p).start()

    def relay(cond, landing, recv, out, send, out_recv, target, src_part):
        @pl.when(cond)
        def _():
            remote(src_part, landing, 0, recv, i).wait_recv()
            copy = remote(landing, out, send, out_recv, target)
            copy.start()
            copy.wait_send()

    for p in (1, 2):
        mine = x == p
        relay(mine & (i + 4 - p < n), f_near, 16, f_far, 6, 17, i + 4, lo_send.at[rows(p)])
        relay(mine & (i - p >= 1), b_near, 18, b_far, 8, 19, i - 4, hi_send.at[rows(p)])
    for p in (1, 2):
        mine = x == p
        relay(mine & (i - p >= 1), f_far, 17, lo_recv.at[rows(p)], 7, 10 + p, i - p, f_near)
        relay(mine & (i + 4 - p < n), b_far, 19, hi_recv.at[rows(p)], 9, 13 + p, i + 3 - p, b_near)

    for p in range(3):

        @pl.when(has_up)
        def _():
            remote(lo_send.at[rows(p)], lo_recv.at[rows(p)], p, 10 + p, i + 1).wait_send()

        @pl.when(has_down)
        def _():
            remote(hi_send.at[rows(p)], hi_recv.at[rows(p)], 3 + p, 13 + p, i - 1).wait_send()

        @pl.when(has_down)
        def _():
            remote(lo_send.at[rows(p)], lo_recv.at[rows(p)], p, 10 + p, i).wait_recv()

        @pl.when(has_up)
        def _():
            remote(hi_send.at[rows(p)], hi_recv.at[rows(p)], 3 + p, 13 + p, i).wait_recv()


def exchange(lo_flat, hi_flat, call_id):
    n = lax.axis_size("slab")
    shape = lo_flat.shape
    total = lo_flat.size // 128
    part = -(-total // 24) * 8
    padded = 3 * part

    def prep(a):
        return jnp.pad(a.reshape(total, 128), ((0, padded - total), (0, 0)))

    vmem = pl.BlockSpec(memory_space=pltpu.VMEM)
    lo_recv, hi_recv = pl.pallas_call(
        functools.partial(halo_kernel, n),
        out_shape=(
            jax.ShapeDtypeStruct((padded, 128), jnp.float32),
            jax.ShapeDtypeStruct((padded, 128), jnp.float32),
        ),
        in_specs=[vmem, vmem],
        out_specs=(vmem, vmem),
        scratch_shapes=[
            pltpu.VMEM((part, 128), jnp.float32),
            pltpu.VMEM((part, 128), jnp.float32),
            pltpu.VMEM((part, 128), jnp.float32),
            pltpu.VMEM((part, 128), jnp.float32),
            pltpu.SemaphoreType.DMA((20,)),
        ],
        compiler_params=pltpu.CompilerParams(collective_id=call_id, has_side_effects=True),
    )(prep(lo_flat), prep(hi_flat))
    return lo_recv[:total].reshape(shape), hi_recv[:total].reshape(shape)


def extended(block, pick_y, pick_x, width, call_id):
    dim = 2
    lo_flat = cut_windows(
        lax.slice_in_dim(block, block.shape[dim] - width, None, axis=dim), pick_y, pick_x
    )
    hi_flat = cut_windows(lax.slice_in_dim(block, 0, width, axis=dim), pick_y, pick_x)
    low, high = exchange(lo_flat, hi_flat, call_id)
    i = lax.axis_index("slab")
    low = jnp.where(i >= 1, low, 0.0)
    high = jnp.where(i + 1 < lax.axis_size("slab"), high, 0.0)
    low = paste_windows(low, pick_y, pick_x, width)
    high = paste_windows(high, pick_y, pick_x, width)
    return jnp.concatenate([low, block, high], axis=dim)


def laplace(padded):
    axis_z = padded.ndim - 3
    length = padded.shape[axis_z] - 8
    center = lax.slice_in_dim(padded, 4, 4 + length, axis=axis_z)
    total = 3.0 * COEF[0] * center
    for shift_k in range(1, 5):
        upper = lax.slice_in_dim(padded, 4 + shift_k, 4 + shift_k + length, axis=axis_z)
        lower = lax.slice_in_dim(padded, 4 - shift_k, 4 - shift_k + length, axis=axis_z)
        total = total + COEF[shift_k] * (upper + lower)
    widths = [(0, 0)] * (center.ndim - 2) + [(4, 4), (4, 4)]
    plane = jnp.pad(center, widths)
    rows_y = center.shape[-2]
    cols_x = center.shape[-1]
    for shift_k in range(1, 5):
        side_y = (
            plane[..., 4 + shift_k : 4 + shift_k + rows_y, 4 : 4 + cols_x]
            + plane[..., 4 - shift_k : 4 - shift_k + rows_y, 4 : 4 + cols_x]
        )
        side_x = (
            plane[..., 4 : 4 + rows_y, 4 + shift_k : 4 + shift_k + cols_x]
            + plane[..., 4 : 4 + rows_y, 4 - shift_k : 4 - shift_k + cols_x]
        )
        total = total + COEF[shift_k] * (side_y + side_x)
    return total


def band_mask(source_y, source_x, half_y, half_x, rows_y, cols_x):
    grid_y = jnp.arange(rows_y, dtype=jnp.int32)
    grid_x = jnp.arange(cols_x, dtype=jnp.int32)
    inside_y = jnp.abs(grid_y[None, :, None] - source_y[:, None, None]) <= half_y[:, None, None]
    inside_x = jnp.abs(grid_x[None, None, :] - source_x[:, None, None]) <= half_x[:, None, None]
    return (inside_y & inside_x).astype(jnp.float32)


def point_field(depth_local, row, col, values, length, rows_y, cols_x):
    grid_z = jnp.arange(length, dtype=jnp.int32)[None, :, None, None]
    grid_y = jnp.arange(rows_y, dtype=jnp.int32)[None, None, :, None]
    grid_x = jnp.arange(cols_x, dtype=jnp.int32)[None, None, None, :]
    hit = (
        (grid_z == depth_local[:, None, None, None])
        & (grid_y == row[:, None, None, None])
        & (grid_x == col[:, None, None, None])
    )
    return jnp.where(hit, values[:, None, None, None], 0.0)


def receiver_field(cells, traces, begin, length, rows_y, cols_x):
    plane = rows_y * cols_x
    depth = cells // plane
    rest = cells - depth * plane
    row = rest // cols_x
    col = rest - row * cols_x
    local = depth - begin
    slab_rows = jnp.arange(length * rows_y, dtype=jnp.int32)
    key = local * rows_y + row
    left = jnp.where(slab_rows[None, :, None] == key[:, None, :], traces[:, None, :], 0.0)
    right = (col[:, :, None] == jnp.arange(cols_x, dtype=jnp.int32)[None, None, :]).astype(
        jnp.float32
    )
    field = jnp.einsum(
        "szr,srx->szx",
        left,
        right,
        precision=lax.Precision.HIGHEST,
        preferred_element_type=jnp.float32,
    )
    return field.reshape(cells.shape[0], length, rows_y, cols_x)


def tree_sum(value, axis):
    count = lax.axis_size(axis)
    me = lax.axis_index(axis)
    shape = value.shape
    piece = value.reshape(-1)
    bits = []
    stride = 1
    while stride < count:
        bits.append(stride)
        stride *= 2
    for stride in bits:
        upper = (me // stride) % 2 == 1
        halves = piece.reshape(2, -1)
        send = jnp.where(upper, halves[0], halves[1])
        keep = jnp.where(upper, halves[1], halves[0])
        pairs = [(i, i ^ stride) for i in range(count)]
        piece = keep + lax.ppermute(send, axis, pairs)
    for stride in reversed(bits):
        upper = (me // stride) % 2 == 1
        pairs = [(i, i ^ stride) for i in range(count)]
        other = lax.ppermute(piece, axis, pairs)
        piece = jnp.where(upper, jnp.concatenate([other, piece]), jnp.concatenate([piece, other]))
    return piece.reshape(shape)


def allreduce_kernel(strides, local_ref, out_ref, *scratch):
    rounds = len(strides)
    halves = scratch[:rounds]
    sums = scratch[rounds : 2 * rounds]
    send_sems, recv_sems = scratch[2 * rounds], scratch[2 * rounds + 1]
    me = lax.axis_index("shots")
    slab = lax.axis_index("slab")
    mesh_id = pl.DeviceIdType.MESH
    barrier = pltpu.get_barrier_semaphore()
    for stride in strides:
        partner = me + stride - 2 * stride * ((me // stride) % 2)
        pl.semaphore_signal(barrier, inc=1, device_id=(slab, partner), device_id_type=mesh_id)
    pl.semaphore_wait(barrier, rounds)
    source = local_ref
    start = 0
    rows = local_ref.shape[0]
    for k, stride in enumerate(strides):
        upper = (me // stride) % 2
        partner = me + stride - 2 * stride * upper
        rows //= 2
        copy = pltpu.make_async_remote_copy(
            src_ref=source.at[pl.ds(pl.multiple_of((1 - upper) * rows, 8), rows)],
            dst_ref=halves[k],
            send_sem=send_sems.at[k],
            recv_sem=recv_sems.at[k],
            device_id=(slab, partner),
            device_id_type=mesh_id,
        )
        copy.start()
        copy.wait()
        kept = source[pl.ds(pl.multiple_of(upper * rows, 8), rows)]
        sums[k][...] = kept + halves[k][...]
        source = sums[k]
        start = start + upper * rows
    out_ref[pl.ds(pl.multiple_of(start, 8), rows)] = sums[rounds - 1][...]
    for k in reversed(range(rounds)):
        stride = strides[k]
        upper = (me // stride) % 2
        partner = me + stride - 2 * stride * upper
        mine = out_ref.at[pl.ds(pl.multiple_of(start, 8), rows)]
        copy = pltpu.make_async_remote_copy(
            src_ref=mine,
            dst_ref=mine,
            send_sem=send_sems.at[rounds + k],
            recv_sem=recv_sems.at[rounds + k],
            device_id=(slab, partner),
            device_id_type=mesh_id,
        )
        copy.start()
        copy.wait()
        start = start - upper * rows
        rows *= 2


def shots_sum(value):
    count = lax.axis_size("shots")
    strides = []
    stride = 1
    while stride < count:
        strides.append(stride)
        stride *= 2
    shape = value.shape
    chunks = value.reshape(-1, 128)
    rows = chunks.shape[0]
    scratch = []
    for k in range(len(strides)):
        scratch.append(pltpu.VMEM((rows >> (k + 1), 128), jnp.float32))
    for k in range(len(strides)):
        scratch.append(pltpu.VMEM((rows >> (k + 1), 128), jnp.float32))
    scratch.append(pltpu.SemaphoreType.DMA((2 * len(strides),)))
    scratch.append(pltpu.SemaphoreType.DMA((2 * len(strides),)))
    out = pl.pallas_call(
        functools.partial(allreduce_kernel, tuple(strides)),
        out_shape=jax.ShapeDtypeStruct(chunks.shape, jnp.float32),
        in_specs=[pl.BlockSpec(memory_space=pltpu.VMEM)],
        out_specs=pl.BlockSpec(memory_space=pltpu.VMEM),
        scratch_shapes=scratch,
        compiler_params=pltpu.CompilerParams(collective_id=0, has_side_effects=True),
    )(chunks)
    return out.reshape(shape)


def per_device(
    src_prev,
    src_cur,
    rcv_prev,
    rcv_cur,
    velocity,
    wavelet,
    residual_traces,
    source_depth,
    source_y,
    source_x,
    half_y,
    half_x,
    receiver_cell,
):
    shot_count, depth, rows_y, cols_x = src_cur.shape
    start = lax.axis_index("slab") * depth
    mask = band_mask(source_y, source_x, half_y, half_x, rows_y, cols_x)[:, None]
    row0, col0 = band_corner(source_y, source_x, half_y, half_x, rows_y, cols_x)
    pick_y, pick_x = selectors(row0, col0, rows_y, cols_x)
    terms = []
    up, u, vp, v = (src_prev, src_cur, rcv_prev, rcv_cur)
    for step in range(STEPS):
        stacked = jnp.stack([u, v])
        padded = extended(stacked, pick_y, pick_x, 4, 1 + step)
        lap = laplace(padded)
        sdelta = point_field(
            source_depth - start, source_y, source_x, wavelet[step], depth, rows_y, cols_x
        )
        rdelta = receiver_field(receiver_cell, residual_traces[step], start, depth, rows_y, cols_x)
        unew = mask * (2.0 * u - up + velocity * lap[0] + sdelta)
        vnew = mask * (2.0 * v - vp + velocity * lap[1] + rdelta)
        terms.append(jnp.sum((unew - 2.0 * u + up) * vnew, axis=0))
        up, u, vp, v = (u, unew, v, vnew)
    src_last, rcv_last = (u, v)
    local_sum = terms[0]
    for extra in terms[1:]:
        local_sum = local_sum + extra
    image = shots_sum(local_sum)
    return (src_last, rcv_last, image)


def solution(mesh):
    return jax.shard_map(
        per_device,
        mesh=mesh,
        in_specs=(
            P("shots", "slab", None, None),
            P("shots", "slab", None, None),
            P("shots", "slab", None, None),
            P("shots", "slab", None, None),
            P("slab", None, None),
            P(None, "shots"),
            P(None, "shots", None),
            P("shots"),
            P("shots"),
            P("shots"),
            P("shots"),
            P("shots"),
            P("shots", None),
        ),
        out_specs=(
            P("shots", "slab", None, None),
            P("shots", "slab", None, None),
            P("slab", None, None),
        ),
        check_vma=False,
    )
```

```python
import jax
import jax.numpy as jnp
from jax import lax
from jax.sharding import PartitionSpec as P
from jax.experimental import pallas as pl
from jax.experimental.pallas import tpu as pltpu
import functools

STEPS = 2


COEF = (-205.0 / 72.0, 8.0 / 5.0, -1.0 / 5.0, 8.0 / 315.0, -1.0 / 560.0)


WIN_Y = 44
WIN_X = 88


def band_corner(source_y, source_x, half_y, half_x, rows_y, cols_x):
    row0 = jnp.clip(source_y - half_y, 0, rows_y - WIN_Y)
    col0 = jnp.clip(source_x - half_x, 0, cols_x - WIN_X)
    return row0, col0


def selectors(row0, col0, rows_y, cols_x):
    pick_y = (
        jnp.arange(rows_y, dtype=jnp.int32)[None, :, None]
        == row0[:, None, None] + jnp.arange(WIN_Y, dtype=jnp.int32)[None, None, :]
    ).astype(jnp.float32)
    pick_x = (
        jnp.arange(cols_x, dtype=jnp.int32)[None, None, :]
        == col0[:, None, None] + jnp.arange(WIN_X, dtype=jnp.int32)[None, :, None]
    ).astype(jnp.float32)
    return pick_y, pick_x


def exact_einsum(spec, a, b):
    return jnp.einsum(
        spec, a, b, precision=lax.Precision.HIGHEST, preferred_element_type=jnp.float32
    )


def cut_windows(layers, pick_y, pick_x):
    fields, shots, width = layers.shape[:3]
    part = exact_einsum("fsjyx,sbx->fsjyb", layers, pick_x)
    part = exact_einsum("sya,fsjyb->fsjab", pick_y, part)
    return part.reshape(fields, shots, -1, 128)


def paste_windows(flat, pick_y, pick_x, width):
    fields, shots = flat.shape[:2]
    part = flat.reshape(fields, shots, width, WIN_Y, WIN_X)
    part = exact_einsum("fsjab,sbx->fsjax", part, pick_x)
    return exact_einsum("sya,fsjax->fsjyx", pick_y, part)


def halo_kernel(n, lo_send, hi_send, lo_recv, hi_recv, relay_f, relay_b, sems):
    i = lax.axis_index("slab")
    shot = lax.axis_index("shots")
    x = i % 4
    part = lo_send.shape[0] // 3
    mesh_id = pl.DeviceIdType.MESH
    barrier = pltpu.get_barrier_semaphore()
    greeted = 0
    for d in (-3, -2, -1, 1, 2, 3):
        ok = (i + d >= 0) & (i + d < n)

        @pl.when(ok)
        def _():
            pl.semaphore_signal(barrier, inc=1, device_id=(i + d, shot), device_id_type=mesh_id)

        greeted = greeted + ok.astype(jnp.int32)
    pl.semaphore_wait(barrier, greeted)

    def rows(p):
        return pl.ds(p * part, part)

    def remote(src, dst, send, recv, target):
        return pltpu.make_async_remote_copy(
            src_ref=src,
            dst_ref=dst,
            send_sem=sems.at[send],
            recv_sem=sems.at[recv],
            device_id=(target, shot),
            device_id_type=mesh_id,
        )

    has_up = i + 1 < n
    has_down = i >= 1
    up_far = x == 3
    down_far = x == 0
    for p in range(3):
        direct_up = has_up if p == 0 else has_up & jnp.logical_not(up_far)

        @pl.when(direct_up)
        def _():
            remote(lo_send.at[rows(p)], lo_recv.at[rows(p)], p, 8 + p, i + 1).start()

        direct_down = has_down if p == 0 else has_down & jnp.logical_not(down_far)

        @pl.when(direct_down)
        def _():
            remote(hi_send.at[rows(p)], hi_recv.at[rows(p)], 3 + p, 11 + p, i - 1).start()

        if p > 0:

            @pl.when(has_up & up_far)
            def _():
                remote(lo_send.at[rows(p)], relay_f, p, 14, i - 3 + p).start()

            @pl.when(has_down & down_far)
            def _():
                remote(hi_send.at[rows(p)], relay_b, 3 + p, 15, i + p).start()

    for p in (1, 2):
        fwd = (x == p) & (i + 4 - p < n)

        @pl.when(fwd)
        def _():
            remote(lo_send.at[rows(p)], relay_f, p, 14, i).wait_recv()
            copy = remote(relay_f, lo_recv.at[rows(p)], 6, 8 + p, i + 4 - p)
            copy.start()
            copy.wait_send()

        bwd = (x == p) & (i - p >= 1)

        @pl.when(bwd)
        def _():
            remote(hi_send.at[rows(p)], relay_b, 3 + p, 15, i).wait_recv()
            copy = remote(relay_b, hi_recv.at[rows(p)], 7, 11 + p, i - p - 1)
            copy.start()
            copy.wait_send()

    for p in range(3):

        @pl.when(has_up)
        def _():
            remote(lo_send.at[rows(p)], lo_recv.at[rows(p)], p, 8 + p, i + 1).wait_send()

        @pl.when(has_down)
        def _():
            remote(hi_send.at[rows(p)], hi_recv.at[rows(p)], 3 + p, 11 + p, i - 1).wait_send()

        @pl.when(has_down)
        def _():
            remote(lo_send.at[rows(p)], lo_recv.at[rows(p)], p, 8 + p, i).wait_recv()

        @pl.when(has_up)
        def _():
            remote(hi_send.at[rows(p)], hi_recv.at[rows(p)], 3 + p, 11 + p, i).wait_recv()


def exchange(lo_flat, hi_flat, call_id):
    n = lax.axis_size("slab")
    shape = lo_flat.shape
    total = lo_flat.size // 128
    part = -(-total // 24) * 8
    padded = 3 * part

    def prep(a):
        return jnp.pad(a.reshape(total, 128), ((0, padded - total), (0, 0)))

    vmem = pl.BlockSpec(memory_space=pltpu.VMEM)
    lo_recv, hi_recv = pl.pallas_call(
        functools.partial(halo_kernel, n),
        out_shape=(
            jax.ShapeDtypeStruct((padded, 128), jnp.float32),
            jax.ShapeDtypeStruct((padded, 128), jnp.float32),
        ),
        in_specs=[vmem, vmem],
        out_specs=(vmem, vmem),
        scratch_shapes=[
            pltpu.VMEM((part, 128), jnp.float32),
            pltpu.VMEM((part, 128), jnp.float32),
            pltpu.SemaphoreType.DMA((16,)),
        ],
        compiler_params=pltpu.CompilerParams(collective_id=call_id, has_side_effects=True),
    )(prep(lo_flat), prep(hi_flat))
    return lo_recv[:total].reshape(shape), hi_recv[:total].reshape(shape)


def extended(block, pick_y, pick_x, width, call_id):
    dim = 2
    lo_flat = cut_windows(
        lax.slice_in_dim(block, block.shape[dim] - width, None, axis=dim), pick_y, pick_x
    )
    hi_flat = cut_windows(lax.slice_in_dim(block, 0, width, axis=dim), pick_y, pick_x)
    low, high = exchange(lo_flat, hi_flat, call_id)
    i = lax.axis_index("slab")
    low = jnp.where(i >= 1, low, 0.0)
    high = jnp.where(i + 1 < lax.axis_size("slab"), high, 0.0)
    low = paste_windows(low, pick_y, pick_x, width)
    high = paste_windows(high, pick_y, pick_x, width)
    return jnp.concatenate([low, block, high], axis=dim)


def laplace(padded):
    axis_z = padded.ndim - 3
    length = padded.shape[axis_z] - 8
    center = lax.slice_in_dim(padded, 4, 4 + length, axis=axis_z)
    total = 3.0 * COEF[0] * center
    for shift_k in range(1, 5):
        upper = lax.slice_in_dim(padded, 4 + shift_k, 4 + shift_k + length, axis=axis_z)
        lower = lax.slice_in_dim(padded, 4 - shift_k, 4 - shift_k + length, axis=axis_z)
        total = total + COEF[shift_k] * (upper + lower)
    widths = [(0, 0)] * (center.ndim - 2) + [(4, 4), (4, 4)]
    plane = jnp.pad(center, widths)
    rows_y = center.shape[-2]
    cols_x = center.shape[-1]
    for shift_k in range(1, 5):
        side_y = (
            plane[..., 4 + shift_k : 4 + shift_k + rows_y, 4 : 4 + cols_x]
            + plane[..., 4 - shift_k : 4 - shift_k + rows_y, 4 : 4 + cols_x]
        )
        side_x = (
            plane[..., 4 : 4 + rows_y, 4 + shift_k : 4 + shift_k + cols_x]
            + plane[..., 4 : 4 + rows_y, 4 - shift_k : 4 - shift_k + cols_x]
        )
        total = total + COEF[shift_k] * (side_y + side_x)
    return total


def band_mask(source_y, source_x, half_y, half_x, rows_y, cols_x):
    grid_y = jnp.arange(rows_y, dtype=jnp.int32)
    grid_x = jnp.arange(cols_x, dtype=jnp.int32)
    inside_y = jnp.abs(grid_y[None, :, None] - source_y[:, None, None]) <= half_y[:, None, None]
    inside_x = jnp.abs(grid_x[None, None, :] - source_x[:, None, None]) <= half_x[:, None, None]
    return (inside_y & inside_x).astype(jnp.float32)


def point_field(depth_local, row, col, values, length, rows_y, cols_x):
    grid_z = jnp.arange(length, dtype=jnp.int32)[None, :, None, None]
    grid_y = jnp.arange(rows_y, dtype=jnp.int32)[None, None, :, None]
    grid_x = jnp.arange(cols_x, dtype=jnp.int32)[None, None, None, :]
    hit = (
        (grid_z == depth_local[:, None, None, None])
        & (grid_y == row[:, None, None, None])
        & (grid_x == col[:, None, None, None])
    )
    return jnp.where(hit, values[:, None, None, None], 0.0)


def receiver_field(cells, traces, begin, length, rows_y, cols_x):
    plane = rows_y * cols_x
    depth = cells // plane
    rest = cells - depth * plane
    row = rest // cols_x
    col = rest - row * cols_x
    local = depth - begin
    slab_rows = jnp.arange(length * rows_y, dtype=jnp.int32)
    key = local * rows_y + row
    left = jnp.where(slab_rows[None, :, None] == key[:, None, :], traces[:, None, :], 0.0)
    right = (col[:, :, None] == jnp.arange(cols_x, dtype=jnp.int32)[None, None, :]).astype(
        jnp.float32
    )
    field = jnp.einsum(
        "szr,srx->szx",
        left,
        right,
        precision=lax.Precision.HIGHEST,
        preferred_element_type=jnp.float32,
    )
    return field.reshape(cells.shape[0], length, rows_y, cols_x)


def tree_sum(value, axis):
    count = lax.axis_size(axis)
    me = lax.axis_index(axis)
    shape = value.shape
    piece = value.reshape(-1)
    bits = []
    stride = 1
    while stride < count:
        bits.append(stride)
        stride *= 2
    for stride in bits:
        upper = (me // stride) % 2 == 1
        halves = piece.reshape(2, -1)
        send = jnp.where(upper, halves[0], halves[1])
        keep = jnp.where(upper, halves[1], halves[0])
        pairs = [(i, i ^ stride) for i in range(count)]
        piece = keep + lax.ppermute(send, axis, pairs)
    for stride in reversed(bits):
        upper = (me // stride) % 2 == 1
        pairs = [(i, i ^ stride) for i in range(count)]
        other = lax.ppermute(piece, axis, pairs)
        piece = jnp.where(upper, jnp.concatenate([other, piece]), jnp.concatenate([piece, other]))
    return piece.reshape(shape)


def allreduce_kernel(chips, local_ref, out_ref, half_in, gathered, spread, send_sems, recv_sems):
    me = lax.axis_index("shots")
    slab = lax.axis_index("slab")
    core = me % 2
    chip = me // 2
    mesh_id = pl.DeviceIdType.MESH
    rows = local_ref.shape[0] // 2
    chunk = rows // chips
    barrier = pltpu.get_barrier_semaphore()
    pl.semaphore_signal(barrier, inc=1, device_id=(slab, me + 1 - 2 * core), device_id_type=mesh_id)
    for k in range(1, chips):
        peer = lax.rem(chip + k, chips) * 2 + core
        pl.semaphore_signal(barrier, inc=1, device_id=(slab, peer), device_id_type=mesh_id)
    pl.semaphore_wait(barrier, chips)

    def remote(src, dst, slot, target):
        return pltpu.make_async_remote_copy(
            src_ref=src,
            dst_ref=dst,
            send_sem=send_sems.at[slot],
            recv_sem=recv_sems.at[slot],
            device_id=(slab, target),
            device_id_type=mesh_id,
        )

    mine = pl.ds(pl.multiple_of(core * rows, 8), rows)
    theirs = pl.ds(pl.multiple_of((1 - core) * rows, 8), rows)
    copy = remote(local_ref.at[theirs], half_in, 0, me + 1 - 2 * core)
    copy.start()
    copy.wait()
    out_ref[mine] = local_ref[mine] + half_in[...]
    copies = []
    for k in range(1, chips):
        target = lax.rem(chip + k, chips)
        src = out_ref.at[pl.ds(pl.multiple_of(core * rows + target * chunk, 8), chunk)]
        copy = remote(src, gathered.at[k], k, target * 2 + core)
        copy.start()
        copies.append(copy)
    for copy in copies:
        copy.wait()
    own = pl.ds(pl.multiple_of(core * rows + chip * chunk, 8), chunk)
    total = out_ref[own]
    for k in range(1, chips):
        total = total + gathered[k]
    out_ref[own] = total
    copies = []
    for k in range(1, chips):
        target = lax.rem(chip + k, chips)
        copy = remote(out_ref.at[own], spread.at[k], chips + k, target * 2 + core)
        copy.start()
        copies.append(copy)
    for copy in copies:
        copy.wait()
    for k in range(1, chips):
        source = lax.rem(chip + chips - k, chips)
        out_ref[pl.ds(pl.multiple_of(core * rows + source * chunk, 8), chunk)] = spread[k]
    copy = remote(out_ref.at[mine], out_ref.at[mine], 2 * chips, me + 1 - 2 * core)
    copy.start()
    copy.wait()


def shots_sum(value):
    chips = lax.axis_size("shots") // 2
    shape = value.shape
    chunks = value.reshape(-1, 128)
    rows = chunks.shape[0]
    out = pl.pallas_call(
        functools.partial(allreduce_kernel, chips),
        out_shape=jax.ShapeDtypeStruct(chunks.shape, jnp.float32),
        in_specs=[pl.BlockSpec(memory_space=pltpu.VMEM)],
        out_specs=pl.BlockSpec(memory_space=pltpu.VMEM),
        scratch_shapes=[
            pltpu.VMEM((rows // 2, 128), jnp.float32),
            pltpu.VMEM((chips, rows // 2 // chips, 128), jnp.float32),
            pltpu.VMEM((chips, rows // 2 // chips, 128), jnp.float32),
            pltpu.SemaphoreType.DMA((2 * chips + 1,)),
            pltpu.SemaphoreType.DMA((2 * chips + 1,)),
        ],
        compiler_params=pltpu.CompilerParams(collective_id=0, has_side_effects=True),
    )(chunks)
    return out.reshape(shape)


def per_device(
    src_prev,
    src_cur,
    rcv_prev,
    rcv_cur,
    velocity,
    wavelet,
    residual_traces,
    source_depth,
    source_y,
    source_x,
    half_y,
    half_x,
    receiver_cell,
):
    shot_count, depth, rows_y, cols_x = src_cur.shape
    start = lax.axis_index("slab") * depth
    mask = band_mask(source_y, source_x, half_y, half_x, rows_y, cols_x)[:, None]
    row0, col0 = band_corner(source_y, source_x, half_y, half_x, rows_y, cols_x)
    pick_y, pick_x = selectors(row0, col0, rows_y, cols_x)
    terms = []
    up, u, vp, v = (src_prev, src_cur, rcv_prev, rcv_cur)
    for step in range(STEPS):
        stacked = jnp.stack([u, v])
        padded = extended(stacked, pick_y, pick_x, 4, 1 + step)
        lap = laplace(padded)
        sdelta = point_field(
            source_depth - start, source_y, source_x, wavelet[step], depth, rows_y, cols_x
        )
        rdelta = receiver_field(receiver_cell, residual_traces[step], start, depth, rows_y, cols_x)
        unew = mask * (2.0 * u - up + velocity * lap[0] + sdelta)
        vnew = mask * (2.0 * v - vp + velocity * lap[1] + rdelta)
        terms.append(jnp.sum((unew - 2.0 * u + up) * vnew, axis=0))
        up, u, vp, v = (u, unew, v, vnew)
    src_last, rcv_last = (u, v)
    local_sum = terms[0]
    for extra in terms[1:]:
        local_sum = local_sum + extra
    image = shots_sum(local_sum)
    return (src_last, rcv_last, image)


def solution(mesh):
    return jax.shard_map(
        per_device,
        mesh=mesh,
        in_specs=(
            P("shots", "slab", None, None),
            P("shots", "slab", None, None),
            P("shots", "slab", None, None),
            P("shots", "slab", None, None),
            P("slab", None, None),
            P(None, "shots"),
            P(None, "shots", None),
            P("shots"),
            P("shots"),
            P("shots"),
            P("shots"),
            P("shots"),
            P("shots", None),
        ),
        out_specs=(
            P("shots", "slab", None, None),
            P("shots", "slab", None, None),
            P("slab", None, None),
        ),
        check_vma=False,
    )
```

```python
import jax
import jax.numpy as jnp
from jax import lax
from jax.sharding import PartitionSpec as P
from jax.experimental import pallas as pl
from jax.experimental.pallas import tpu as pltpu
import functools

STEPS = 2


COEF = (-205.0 / 72.0, 8.0 / 5.0, -1.0 / 5.0, 8.0 / 315.0, -1.0 / 560.0)


WIN_Y = 44
WIN_X = 88


def band_corner(source_y, source_x, half_y, half_x, rows_y, cols_x):
    row0 = jnp.clip(source_y - half_y, 0, rows_y - WIN_Y)
    col0 = jnp.clip(source_x - half_x, 0, cols_x - WIN_X)
    return row0, col0


def selectors(row0, col0, rows_y, cols_x):
    pick_y = (
        jnp.arange(rows_y, dtype=jnp.int32)[None, :, None]
        == row0[:, None, None] + jnp.arange(WIN_Y, dtype=jnp.int32)[None, None, :]
    ).astype(jnp.float32)
    pick_x = (
        jnp.arange(cols_x, dtype=jnp.int32)[None, None, :]
        == col0[:, None, None] + jnp.arange(WIN_X, dtype=jnp.int32)[None, :, None]
    ).astype(jnp.float32)
    return pick_y, pick_x


def exact_einsum(spec, a, b):
    return jnp.einsum(
        spec, a, b, precision=lax.Precision.HIGHEST, preferred_element_type=jnp.float32
    )


def cut_windows(layers, pick_y, pick_x):
    fields, shots, width = layers.shape[:3]
    part = exact_einsum("fsjyx,sbx->fsjyb", layers, pick_x)
    part = exact_einsum("sya,fsjyb->fsjab", pick_y, part)
    return part.reshape(fields, shots, -1, 128)


def paste_windows(flat, pick_y, pick_x, width):
    fields, shots = flat.shape[:2]
    part = flat.reshape(fields, shots, width, WIN_Y, WIN_X)
    part = exact_einsum("fsjab,sbx->fsjax", part, pick_x)
    return exact_einsum("sya,fsjax->fsjyx", pick_y, part)


def halo_kernel(n, send_ref, recv_ref, relay_f, relay_b, sems):
    lo_send, hi_send = send_ref.at[0], send_ref.at[1]
    lo_recv, hi_recv = recv_ref.at[0], recv_ref.at[1]
    i = lax.axis_index("slab")
    shot = lax.axis_index("shots")
    x = i % 4
    part = send_ref.shape[1] // 3
    mesh_id = pl.DeviceIdType.MESH
    barrier = pltpu.get_barrier_semaphore()
    greeted = 0
    for d in (-3, -2, -1, 1, 2, 3):
        ok = (i + d >= 0) & (i + d < n)

        @pl.when(ok)
        def _():
            pl.semaphore_signal(barrier, inc=1, device_id=(i + d, shot), device_id_type=mesh_id)

        greeted = greeted + ok.astype(jnp.int32)
    pl.semaphore_wait(barrier, greeted)

    def rows(p):
        return pl.ds(p * part, part)

    def remote(src, dst, send, recv, target):
        return pltpu.make_async_remote_copy(
            src_ref=src,
            dst_ref=dst,
            send_sem=sems.at[send],
            recv_sem=sems.at[recv],
            device_id=(target, shot),
            device_id_type=mesh_id,
        )

    has_up = i + 1 < n
    has_down = i >= 1
    up_far = x == 3
    down_far = x == 0
    for p in range(3):
        direct_up = has_up if p == 0 else has_up & jnp.logical_not(up_far)

        @pl.when(direct_up)
        def _():
            remote(lo_send.at[rows(p)], lo_recv.at[rows(p)], p, 8 + p, i + 1).start()

        direct_down = has_down if p == 0 else has_down & jnp.logical_not(down_far)

        @pl.when(direct_down)
        def _():
            remote(hi_send.at[rows(p)], hi_recv.at[rows(p)], 3 + p, 11 + p, i - 1).start()

        if p > 0:

            @pl.when(has_up & up_far)
            def _():
                remote(lo_send.at[rows(p)], relay_f, p, 14, i - 3 + p).start()

            @pl.when(has_down & down_far)
            def _():
                remote(hi_send.at[rows(p)], relay_b, 3 + p, 15, i + p).start()

    for p in (1, 2):
        fwd = (x == p) & (i + 4 - p < n)

        @pl.when(fwd)
        def _():
            remote(lo_send.at[rows(p)], relay_f, p, 14, i).wait_recv()
            copy = remote(relay_f, lo_recv.at[rows(p)], 6, 8 + p, i + 4 - p)
            copy.start()
            copy.wait_send()

        bwd = (x == p) & (i - p >= 1)

        @pl.when(bwd)
        def _():
            remote(hi_send.at[rows(p)], relay_b, 3 + p, 15, i).wait_recv()
            copy = remote(relay_b, hi_recv.at[rows(p)], 7, 11 + p, i - p - 1)
            copy.start()
            copy.wait_send()

    for p in range(3):

        @pl.when(has_up)
        def _():
            remote(lo_send.at[rows(p)], lo_recv.at[rows(p)], p, 8 + p, i + 1).wait_send()

        @pl.when(has_down)
        def _():
            remote(hi_send.at[rows(p)], hi_recv.at[rows(p)], 3 + p, 11 + p, i - 1).wait_send()

        @pl.when(has_down)
        def _():
            remote(lo_send.at[rows(p)], lo_recv.at[rows(p)], p, 8 + p, i).wait_recv()

        @pl.when(has_up)
        def _():
            remote(hi_send.at[rows(p)], hi_recv.at[rows(p)], 3 + p, 11 + p, i).wait_recv()


def exchange(both, call_id):
    n = lax.axis_size("slab")
    shape = both.shape
    total = both[0].size // 128
    part = -(-total // 24) * 8
    padded = 3 * part
    send = jnp.pad(both.reshape(2, total, 128), ((0, 0), (0, padded - total), (0, 0)))
    vmem = pl.BlockSpec(memory_space=pltpu.VMEM)
    recv = pl.pallas_call(
        functools.partial(halo_kernel, n),
        out_shape=jax.ShapeDtypeStruct((2, padded, 128), jnp.float32),
        in_specs=[vmem],
        out_specs=vmem,
        scratch_shapes=[
            pltpu.VMEM((part, 128), jnp.float32),
            pltpu.VMEM((part, 128), jnp.float32),
            pltpu.SemaphoreType.DMA((16,)),
        ],
        compiler_params=pltpu.CompilerParams(collective_id=call_id, has_side_effects=True),
    )(send)
    return recv[:, :total].reshape(shape)


def extended(block, pick_y, pick_x, width, call_id):
    dim = 2
    sides = jnp.stack(
        [
            lax.slice_in_dim(block, block.shape[dim] - width, None, axis=dim),
            lax.slice_in_dim(block, 0, width, axis=dim),
        ]
    )
    part = exact_einsum("zfsjyx,sbx->zfsjyb", sides, pick_x)
    part = exact_einsum("sya,zfsjyb->zfsjab", pick_y, part)
    got = exchange(part, call_id)
    i = lax.axis_index("slab")
    present = jnp.stack([i >= 1, i + 1 < lax.axis_size("slab")])
    got = jnp.where(present[:, None, None, None, None, None], got, 0.0)
    got = exact_einsum("zfsjab,sbx->zfsjax", got, pick_x)
    got = exact_einsum("sya,zfsjax->zfsjyx", pick_y, got)
    return jnp.concatenate([got[0], block, got[1]], axis=dim)


def laplace(padded):
    axis_z = padded.ndim - 3
    length = padded.shape[axis_z] - 8
    center = lax.slice_in_dim(padded, 4, 4 + length, axis=axis_z)
    total = 3.0 * COEF[0] * center
    for shift_k in range(1, 5):
        upper = lax.slice_in_dim(padded, 4 + shift_k, 4 + shift_k + length, axis=axis_z)
        lower = lax.slice_in_dim(padded, 4 - shift_k, 4 - shift_k + length, axis=axis_z)
        total = total + COEF[shift_k] * (upper + lower)
    widths = [(0, 0)] * (center.ndim - 2) + [(4, 4), (4, 4)]
    plane = jnp.pad(center, widths)
    rows_y = center.shape[-2]
    cols_x = center.shape[-1]
    for shift_k in range(1, 5):
        side_y = (
            plane[..., 4 + shift_k : 4 + shift_k + rows_y, 4 : 4 + cols_x]
            + plane[..., 4 - shift_k : 4 - shift_k + rows_y, 4 : 4 + cols_x]
        )
        side_x = (
            plane[..., 4 : 4 + rows_y, 4 + shift_k : 4 + shift_k + cols_x]
            + plane[..., 4 : 4 + rows_y, 4 - shift_k : 4 - shift_k + cols_x]
        )
        total = total + COEF[shift_k] * (side_y + side_x)
    return total


def band_mask(source_y, source_x, half_y, half_x, rows_y, cols_x):
    grid_y = jnp.arange(rows_y, dtype=jnp.int32)
    grid_x = jnp.arange(cols_x, dtype=jnp.int32)
    inside_y = jnp.abs(grid_y[None, :, None] - source_y[:, None, None]) <= half_y[:, None, None]
    inside_x = jnp.abs(grid_x[None, None, :] - source_x[:, None, None]) <= half_x[:, None, None]
    return (inside_y & inside_x).astype(jnp.float32)


def point_field(depth_local, row, col, values, length, rows_y, cols_x):
    grid_z = jnp.arange(length, dtype=jnp.int32)[None, :, None, None]
    grid_y = jnp.arange(rows_y, dtype=jnp.int32)[None, None, :, None]
    grid_x = jnp.arange(cols_x, dtype=jnp.int32)[None, None, None, :]
    hit = (
        (grid_z == depth_local[:, None, None, None])
        & (grid_y == row[:, None, None, None])
        & (grid_x == col[:, None, None, None])
    )
    return jnp.where(hit, values[:, None, None, None], 0.0)


def receiver_field(cells, traces, begin, length, rows_y, cols_x):
    plane = rows_y * cols_x
    depth = cells // plane
    rest = cells - depth * plane
    row = rest // cols_x
    col = rest - row * cols_x
    local = depth - begin
    slab_rows = jnp.arange(length * rows_y, dtype=jnp.int32)
    key = local * rows_y + row
    left = jnp.where(slab_rows[None, :, None] == key[:, None, :], traces[:, None, :], 0.0)
    right = (col[:, :, None] == jnp.arange(cols_x, dtype=jnp.int32)[None, None, :]).astype(
        jnp.float32
    )
    field = jnp.einsum(
        "szr,srx->szx",
        left,
        right,
        precision=lax.Precision.HIGHEST,
        preferred_element_type=jnp.float32,
    )
    return field.reshape(cells.shape[0], length, rows_y, cols_x)


def tree_sum(value, axis):
    count = lax.axis_size(axis)
    me = lax.axis_index(axis)
    shape = value.shape
    piece = value.reshape(-1)
    bits = []
    stride = 1
    while stride < count:
        bits.append(stride)
        stride *= 2
    for stride in bits:
        upper = (me // stride) % 2 == 1
        halves = piece.reshape(2, -1)
        send = jnp.where(upper, halves[0], halves[1])
        keep = jnp.where(upper, halves[1], halves[0])
        pairs = [(i, i ^ stride) for i in range(count)]
        piece = keep + lax.ppermute(send, axis, pairs)
    for stride in reversed(bits):
        upper = (me // stride) % 2 == 1
        pairs = [(i, i ^ stride) for i in range(count)]
        other = lax.ppermute(piece, axis, pairs)
        piece = jnp.where(upper, jnp.concatenate([other, piece]), jnp.concatenate([piece, other]))
    return piece.reshape(shape)


def allreduce_kernel(chips, local_ref, out_ref, half_in, gathered, spread, send_sems, recv_sems):
    me = lax.axis_index("shots")
    slab = lax.axis_index("slab")
    core = me % 2
    chip = me // 2
    mesh_id = pl.DeviceIdType.MESH
    rows = local_ref.shape[0] // 2
    chunk = rows // chips
    barrier = pltpu.get_barrier_semaphore()
    pl.semaphore_signal(barrier, inc=1, device_id=(slab, me + 1 - 2 * core), device_id_type=mesh_id)
    for k in range(1, chips):
        peer = lax.rem(chip + k, chips) * 2 + core
        pl.semaphore_signal(barrier, inc=1, device_id=(slab, peer), device_id_type=mesh_id)
    pl.semaphore_wait(barrier, chips)

    def remote(src, dst, slot, target):
        return pltpu.make_async_remote_copy(
            src_ref=src,
            dst_ref=dst,
            send_sem=send_sems.at[slot],
            recv_sem=recv_sems.at[slot],
            device_id=(slab, target),
            device_id_type=mesh_id,
        )

    mine = pl.ds(pl.multiple_of(core * rows, 8), rows)
    theirs = pl.ds(pl.multiple_of((1 - core) * rows, 8), rows)
    copy = remote(local_ref.at[theirs], half_in, 0, me + 1 - 2 * core)
    copy.start()
    copy.wait()
    out_ref[mine] = local_ref[mine] + half_in[...]
    copies = []
    for k in range(1, chips):
        target = lax.rem(chip + k, chips)
        src = out_ref.at[pl.ds(pl.multiple_of(core * rows + target * chunk, 8), chunk)]
        copy = remote(src, gathered.at[k], k, target * 2 + core)
        copy.start()
        copies.append(copy)
    for copy in copies:
        copy.wait()
    own = pl.ds(pl.multiple_of(core * rows + chip * chunk, 8), chunk)
    total = out_ref[own]
    for k in range(1, chips):
        total = total + gathered[k]
    out_ref[own] = total
    copies = []
    for k in range(1, chips):
        target = lax.rem(chip + k, chips)
        copy = remote(out_ref.at[own], spread.at[k], chips + k, target * 2 + core)
        copy.start()
        copies.append(copy)
    for copy in copies:
        copy.wait()
    for k in range(1, chips):
        source = lax.rem(chip + chips - k, chips)
        out_ref[pl.ds(pl.multiple_of(core * rows + source * chunk, 8), chunk)] = spread[k]
    copy = remote(out_ref.at[mine], out_ref.at[mine], 2 * chips, me + 1 - 2 * core)
    copy.start()
    copy.wait()


def shots_sum(value):
    chips = lax.axis_size("shots") // 2
    shape = value.shape
    chunks = value.reshape(-1, 128)
    rows = chunks.shape[0]
    out = pl.pallas_call(
        functools.partial(allreduce_kernel, chips),
        out_shape=jax.ShapeDtypeStruct(chunks.shape, jnp.float32),
        in_specs=[pl.BlockSpec(memory_space=pltpu.VMEM)],
        out_specs=pl.BlockSpec(memory_space=pltpu.VMEM),
        scratch_shapes=[
            pltpu.VMEM((rows // 2, 128), jnp.float32),
            pltpu.VMEM((chips, rows // 2 // chips, 128), jnp.float32),
            pltpu.VMEM((chips, rows // 2 // chips, 128), jnp.float32),
            pltpu.SemaphoreType.DMA((2 * chips + 1,)),
            pltpu.SemaphoreType.DMA((2 * chips + 1,)),
        ],
        compiler_params=pltpu.CompilerParams(collective_id=0, has_side_effects=True),
    )(chunks)
    return out.reshape(shape)


def per_device(
    src_prev,
    src_cur,
    rcv_prev,
    rcv_cur,
    velocity,
    wavelet,
    residual_traces,
    source_depth,
    source_y,
    source_x,
    half_y,
    half_x,
    receiver_cell,
):
    shot_count, depth, rows_y, cols_x = src_cur.shape
    start = lax.axis_index("slab") * depth
    mask = band_mask(source_y, source_x, half_y, half_x, rows_y, cols_x)[:, None]
    row0, col0 = band_corner(source_y, source_x, half_y, half_x, rows_y, cols_x)
    pick_y, pick_x = selectors(row0, col0, rows_y, cols_x)
    terms = []
    up, u, vp, v = (src_prev, src_cur, rcv_prev, rcv_cur)
    for step in range(STEPS):
        stacked = jnp.stack([u, v])
        padded = extended(stacked, pick_y, pick_x, 4, 1 + step)
        lap = laplace(padded)
        sdelta = point_field(
            source_depth - start, source_y, source_x, wavelet[step], depth, rows_y, cols_x
        )
        rdelta = receiver_field(receiver_cell, residual_traces[step], start, depth, rows_y, cols_x)
        unew = mask * (2.0 * u - up + velocity * lap[0] + sdelta)
        vnew = mask * (2.0 * v - vp + velocity * lap[1] + rdelta)
        terms.append(jnp.sum((unew - 2.0 * u + up) * vnew, axis=0))
        up, u, vp, v = (u, unew, v, vnew)
    src_last, rcv_last = (u, v)
    local_sum = terms[0]
    for extra in terms[1:]:
        local_sum = local_sum + extra
    image = shots_sum(local_sum)
    return (src_last, rcv_last, image)


def solution(mesh):
    return jax.shard_map(
        per_device,
        mesh=mesh,
        in_specs=(
            P("shots", "slab", None, None),
            P("shots", "slab", None, None),
            P("shots", "slab", None, None),
            P("shots", "slab", None, None),
            P("slab", None, None),
            P(None, "shots"),
            P(None, "shots", None),
            P("shots"),
            P("shots"),
            P("shots"),
            P("shots"),
            P("shots"),
            P("shots", None),
        ),
        out_specs=(
            P("shots", "slab", None, None),
            P("shots", "slab", None, None),
            P("slab", None, None),
        ),
        check_vma=False,
    )
```

```python
import jax
import jax.numpy as jnp
from jax import lax
from jax.sharding import PartitionSpec as P
from jax.experimental import pallas as pl
from jax.experimental.pallas import tpu as pltpu
import functools

STEPS = 2


COEF = (-205.0 / 72.0, 8.0 / 5.0, -1.0 / 5.0, 8.0 / 315.0, -1.0 / 560.0)


WIN_Y = 44
WIN_X = 88


def band_corner(source_y, source_x, half_y, half_x, rows_y, cols_x):
    row0 = jnp.clip(source_y - half_y, 0, rows_y - WIN_Y)
    col0 = jnp.clip(source_x - half_x, 0, cols_x - WIN_X)
    return row0, col0


def selectors(row0, col0, rows_y, cols_x):
    pick_y = (
        jnp.arange(rows_y, dtype=jnp.int32)[None, :, None]
        == row0[:, None, None] + jnp.arange(WIN_Y, dtype=jnp.int32)[None, None, :]
    ).astype(jnp.float32)
    pick_x = (
        jnp.arange(cols_x, dtype=jnp.int32)[None, None, :]
        == col0[:, None, None] + jnp.arange(WIN_X, dtype=jnp.int32)[None, :, None]
    ).astype(jnp.float32)
    return pick_y, pick_x


def exact_einsum(spec, a, b):
    return jnp.einsum(
        spec, a, b, precision=lax.Precision.HIGHEST, preferred_element_type=jnp.float32
    )


def cut_windows(layers, pick_y, pick_x):
    fields, shots, width = layers.shape[:3]
    part = exact_einsum("fsjyx,sbx->fsjyb", layers, pick_x)
    part = exact_einsum("sya,fsjyb->fsjab", pick_y, part)
    return part.reshape(fields, shots, -1, 128)


def paste_windows(flat, pick_y, pick_x, width):
    fields, shots = flat.shape[:2]
    part = flat.reshape(fields, shots, width, WIN_Y, WIN_X)
    part = exact_einsum("fsjab,sbx->fsjax", part, pick_x)
    return exact_einsum("sya,fsjax->fsjyx", pick_y, part)


def halo_kernel(n, bounds, send_ref, recv_ref, relay_f1, relay_f2, relay_b1, relay_b2, sems):
    lo_send, hi_send = send_ref.at[0], send_ref.at[1]
    lo_recv, hi_recv = recv_ref.at[0], recv_ref.at[1]
    i = lax.axis_index("slab")
    shot = lax.axis_index("shots")
    x = i % 4
    relay_f = {1: relay_f1, 2: relay_f2}
    relay_b = {1: relay_b1, 2: relay_b2}
    mesh_id = pl.DeviceIdType.MESH
    barrier = pltpu.get_barrier_semaphore()
    greeted = 0
    for d in (-3, -2, -1, 1, 2, 3):
        ok = (i + d >= 0) & (i + d < n)

        @pl.when(ok)
        def _():
            pl.semaphore_signal(barrier, inc=1, device_id=(i + d, shot), device_id_type=mesh_id)

        greeted = greeted + ok.astype(jnp.int32)
    pl.semaphore_wait(barrier, greeted)

    def rows(p):
        return pl.ds(bounds[p], bounds[p + 1] - bounds[p])

    def remote(src, dst, send, recv, target):
        return pltpu.make_async_remote_copy(
            src_ref=src,
            dst_ref=dst,
            send_sem=sems.at[send],
            recv_sem=sems.at[recv],
            device_id=(target, shot),
            device_id_type=mesh_id,
        )

    has_up = i + 1 < n
    has_down = i >= 1
    up_far = x == 3
    down_far = x == 0
    for p in range(3):
        direct_up = has_up if p == 0 else has_up & jnp.logical_not(up_far)

        @pl.when(direct_up)
        def _():
            remote(lo_send.at[rows(p)], lo_recv.at[rows(p)], p, 8 + p, i + 1).start()

        direct_down = has_down if p == 0 else has_down & jnp.logical_not(down_far)

        @pl.when(direct_down)
        def _():
            remote(hi_send.at[rows(p)], hi_recv.at[rows(p)], 3 + p, 11 + p, i - 1).start()

        if p > 0:

            @pl.when(has_up & up_far)
            def _():
                remote(lo_send.at[rows(p)], relay_f[p], p, 14, i - 3 + p).start()

            @pl.when(has_down & down_far)
            def _():
                remote(hi_send.at[rows(p)], relay_b[p], 3 + p, 15, i + p).start()

    for p in (1, 2):
        fwd = (x == p) & (i + 4 - p < n)

        @pl.when(fwd)
        def _():
            remote(lo_send.at[rows(p)], relay_f[p], p, 14, i).wait_recv()
            copy = remote(relay_f[p], lo_recv.at[rows(p)], 6, 8 + p, i + 4 - p)
            copy.start()
            copy.wait_send()

        bwd = (x == p) & (i - p >= 1)

        @pl.when(bwd)
        def _():
            remote(hi_send.at[rows(p)], relay_b[p], 3 + p, 15, i).wait_recv()
            copy = remote(relay_b[p], hi_recv.at[rows(p)], 7, 11 + p, i - p - 1)
            copy.start()
            copy.wait_send()

    for p in range(3):

        @pl.when(has_up)
        def _():
            remote(lo_send.at[rows(p)], lo_recv.at[rows(p)], p, 8 + p, i + 1).wait_send()

        @pl.when(has_down)
        def _():
            remote(hi_send.at[rows(p)], hi_recv.at[rows(p)], 3 + p, 11 + p, i - 1).wait_send()

        @pl.when(has_down)
        def _():
            remote(lo_send.at[rows(p)], lo_recv.at[rows(p)], p, 8 + p, i).wait_recv()

        @pl.when(has_up)
        def _():
            remote(hi_send.at[rows(p)], hi_recv.at[rows(p)], 3 + p, 11 + p, i).wait_recv()


def exchange(both, call_id):
    n = lax.axis_size("slab")
    shape = both.shape
    total = both[0].size // 128
    part = total // 3 // 8 * 8
    bounds = (0, part, 2 * part, total)
    vmem = pl.BlockSpec(memory_space=pltpu.VMEM)
    recv = pl.pallas_call(
        functools.partial(halo_kernel, n, bounds),
        out_shape=jax.ShapeDtypeStruct((2, total, 128), jnp.float32),
        in_specs=[vmem],
        out_specs=vmem,
        scratch_shapes=[
            pltpu.VMEM((part, 128), jnp.float32),
            pltpu.VMEM((total - 2 * part, 128), jnp.float32),
            pltpu.VMEM((part, 128), jnp.float32),
            pltpu.VMEM((total - 2 * part, 128), jnp.float32),
            pltpu.SemaphoreType.DMA((16,)),
        ],
        compiler_params=pltpu.CompilerParams(collective_id=call_id, has_side_effects=True),
    )(both.reshape(2, total, 128))
    return recv.reshape(shape)


def extended(block, pick_y, pick_x, width, call_id):
    dim = 2
    sides = jnp.stack(
        [
            lax.slice_in_dim(block, block.shape[dim] - width, None, axis=dim),
            lax.slice_in_dim(block, 0, width, axis=dim),
        ]
    )
    part = exact_einsum("zfsjyx,sbx->zfsjyb", sides, pick_x)
    part = exact_einsum("sya,zfsjyb->zfsjab", pick_y, part)
    got = exchange(part, call_id)
    i = lax.axis_index("slab")
    present = jnp.stack([i >= 1, i + 1 < lax.axis_size("slab")])
    got = jnp.where(present[:, None, None, None, None, None], got, 0.0)
    got = exact_einsum("zfsjab,sbx->zfsjax", got, pick_x)
    got = exact_einsum("sya,zfsjax->zfsjyx", pick_y, got)
    return jnp.concatenate([got[0], block, got[1]], axis=dim)


def laplace(padded):
    axis_z = padded.ndim - 3
    length = padded.shape[axis_z] - 8
    center = lax.slice_in_dim(padded, 4, 4 + length, axis=axis_z)
    total = 3.0 * COEF[0] * center
    for shift_k in range(1, 5):
        upper = lax.slice_in_dim(padded, 4 + shift_k, 4 + shift_k + length, axis=axis_z)
        lower = lax.slice_in_dim(padded, 4 - shift_k, 4 - shift_k + length, axis=axis_z)
        total = total + COEF[shift_k] * (upper + lower)
    widths = [(0, 0)] * (center.ndim - 2) + [(4, 4), (4, 4)]
    plane = jnp.pad(center, widths)
    rows_y = center.shape[-2]
    cols_x = center.shape[-1]
    for shift_k in range(1, 5):
        side_y = (
            plane[..., 4 + shift_k : 4 + shift_k + rows_y, 4 : 4 + cols_x]
            + plane[..., 4 - shift_k : 4 - shift_k + rows_y, 4 : 4 + cols_x]
        )
        side_x = (
            plane[..., 4 : 4 + rows_y, 4 + shift_k : 4 + shift_k + cols_x]
            + plane[..., 4 : 4 + rows_y, 4 - shift_k : 4 - shift_k + cols_x]
        )
        total = total + COEF[shift_k] * (side_y + side_x)
    return total


def band_mask(source_y, source_x, half_y, half_x, rows_y, cols_x):
    grid_y = jnp.arange(rows_y, dtype=jnp.int32)
    grid_x = jnp.arange(cols_x, dtype=jnp.int32)
    inside_y = jnp.abs(grid_y[None, :, None] - source_y[:, None, None]) <= half_y[:, None, None]
    inside_x = jnp.abs(grid_x[None, None, :] - source_x[:, None, None]) <= half_x[:, None, None]
    return (inside_y & inside_x).astype(jnp.float32)


def point_field(depth_local, row, col, values, length, rows_y, cols_x):
    grid_z = jnp.arange(length, dtype=jnp.int32)[None, :, None, None]
    grid_y = jnp.arange(rows_y, dtype=jnp.int32)[None, None, :, None]
    grid_x = jnp.arange(cols_x, dtype=jnp.int32)[None, None, None, :]
    hit = (
        (grid_z == depth_local[:, None, None, None])
        & (grid_y == row[:, None, None, None])
        & (grid_x == col[:, None, None, None])
    )
    return jnp.where(hit, values[:, None, None, None], 0.0)


def receiver_field(cells, traces, begin, length, rows_y, cols_x):
    plane = rows_y * cols_x
    depth = cells // plane
    rest = cells - depth * plane
    row = rest // cols_x
    col = rest - row * cols_x
    local = depth - begin
    slab_rows = jnp.arange(length * rows_y, dtype=jnp.int32)
    key = local * rows_y + row
    left = jnp.where(slab_rows[None, :, None] == key[:, None, :], traces[:, None, :], 0.0)
    right = (col[:, :, None] == jnp.arange(cols_x, dtype=jnp.int32)[None, None, :]).astype(
        jnp.float32
    )
    field = jnp.einsum(
        "szr,srx->szx",
        left,
        right,
        precision=lax.Precision.HIGHEST,
        preferred_element_type=jnp.float32,
    )
    return field.reshape(cells.shape[0], length, rows_y, cols_x)


def tree_sum(value, axis):
    count = lax.axis_size(axis)
    me = lax.axis_index(axis)
    shape = value.shape
    piece = value.reshape(-1)
    bits = []
    stride = 1
    while stride < count:
        bits.append(stride)
        stride *= 2
    for stride in bits:
        upper = (me // stride) % 2 == 1
        halves = piece.reshape(2, -1)
        send = jnp.where(upper, halves[0], halves[1])
        keep = jnp.where(upper, halves[1], halves[0])
        pairs = [(i, i ^ stride) for i in range(count)]
        piece = keep + lax.ppermute(send, axis, pairs)
    for stride in reversed(bits):
        upper = (me // stride) % 2 == 1
        pairs = [(i, i ^ stride) for i in range(count)]
        other = lax.ppermute(piece, axis, pairs)
        piece = jnp.where(upper, jnp.concatenate([other, piece]), jnp.concatenate([piece, other]))
    return piece.reshape(shape)


def allreduce_kernel(chips, local_ref, out_ref, half_in, gathered, spread, send_sems, recv_sems):
    me = lax.axis_index("shots")
    slab = lax.axis_index("slab")
    core = me % 2
    chip = me // 2
    mesh_id = pl.DeviceIdType.MESH
    rows = local_ref.shape[0] // 2
    chunk = rows // chips
    barrier = pltpu.get_barrier_semaphore()
    pl.semaphore_signal(barrier, inc=1, device_id=(slab, me + 1 - 2 * core), device_id_type=mesh_id)
    for k in range(1, chips):
        peer = lax.rem(chip + k, chips) * 2 + core
        pl.semaphore_signal(barrier, inc=1, device_id=(slab, peer), device_id_type=mesh_id)
    pl.semaphore_wait(barrier, chips)

    def remote(src, dst, slot, target):
        return pltpu.make_async_remote_copy(
            src_ref=src,
            dst_ref=dst,
            send_sem=send_sems.at[slot],
            recv_sem=recv_sems.at[slot],
            device_id=(slab, target),
            device_id_type=mesh_id,
        )

    mine = pl.ds(pl.multiple_of(core * rows, 8), rows)
    theirs = pl.ds(pl.multiple_of((1 - core) * rows, 8), rows)
    copy = remote(local_ref.at[theirs], half_in, 0, me + 1 - 2 * core)
    copy.start()
    copy.wait()
    out_ref[mine] = local_ref[mine] + half_in[...]
    copies = []
    for k in range(1, chips):
        target = lax.rem(chip + k, chips)
        src = out_ref.at[pl.ds(pl.multiple_of(core * rows + target * chunk, 8), chunk)]
        copy = remote(src, gathered.at[k], k, target * 2 + core)
        copy.start()
        copies.append(copy)
    for copy in copies:
        copy.wait()
    own = pl.ds(pl.multiple_of(core * rows + chip * chunk, 8), chunk)
    total = out_ref[own]
    for k in range(1, chips):
        total = total + gathered[k]
    out_ref[own] = total
    copies = []
    for k in range(1, chips):
        target = lax.rem(chip + k, chips)
        copy = remote(out_ref.at[own], spread.at[k], chips + k, target * 2 + core)
        copy.start()
        copies.append(copy)
    for copy in copies:
        copy.wait()
    for k in range(1, chips):
        source = lax.rem(chip + chips - k, chips)
        out_ref[pl.ds(pl.multiple_of(core * rows + source * chunk, 8), chunk)] = spread[k]
    copy = remote(out_ref.at[mine], out_ref.at[mine], 2 * chips, me + 1 - 2 * core)
    copy.start()
    copy.wait()


def shots_sum(value):
    chips = lax.axis_size("shots") // 2
    shape = value.shape
    chunks = value.reshape(-1, 128)
    rows = chunks.shape[0]
    out = pl.pallas_call(
        functools.partial(allreduce_kernel, chips),
        out_shape=jax.ShapeDtypeStruct(chunks.shape, jnp.float32),
        in_specs=[pl.BlockSpec(memory_space=pltpu.VMEM)],
        out_specs=pl.BlockSpec(memory_space=pltpu.VMEM),
        scratch_shapes=[
            pltpu.VMEM((rows // 2, 128), jnp.float32),
            pltpu.VMEM((chips, rows // 2 // chips, 128), jnp.float32),
            pltpu.VMEM((chips, rows // 2 // chips, 128), jnp.float32),
            pltpu.SemaphoreType.DMA((2 * chips + 1,)),
            pltpu.SemaphoreType.DMA((2 * chips + 1,)),
        ],
        compiler_params=pltpu.CompilerParams(collective_id=0, has_side_effects=True),
    )(chunks)
    return out.reshape(shape)


def per_device(
    src_prev,
    src_cur,
    rcv_prev,
    rcv_cur,
    velocity,
    wavelet,
    residual_traces,
    source_depth,
    source_y,
    source_x,
    half_y,
    half_x,
    receiver_cell,
):
    shot_count, depth, rows_y, cols_x = src_cur.shape
    start = lax.axis_index("slab") * depth
    mask = band_mask(source_y, source_x, half_y, half_x, rows_y, cols_x)[:, None]
    row0, col0 = band_corner(source_y, source_x, half_y, half_x, rows_y, cols_x)
    pick_y, pick_x = selectors(row0, col0, rows_y, cols_x)
    terms = []
    up, u, vp, v = (src_prev, src_cur, rcv_prev, rcv_cur)
    for step in range(STEPS):
        stacked = jnp.stack([u, v])
        padded = extended(stacked, pick_y, pick_x, 4, 1 + step)
        lap = laplace(padded)
        sdelta = point_field(
            source_depth - start, source_y, source_x, wavelet[step], depth, rows_y, cols_x
        )
        rdelta = receiver_field(receiver_cell, residual_traces[step], start, depth, rows_y, cols_x)
        unew = mask * (2.0 * u - up + velocity * lap[0] + sdelta)
        vnew = mask * (2.0 * v - vp + velocity * lap[1] + rdelta)
        terms.append(jnp.sum((unew - 2.0 * u + up) * vnew, axis=0))
        up, u, vp, v = (u, unew, v, vnew)
    src_last, rcv_last = (u, v)
    local_sum = terms[0]
    for extra in terms[1:]:
        local_sum = local_sum + extra
    image = shots_sum(local_sum)
    return (src_last, rcv_last, image)


def solution(mesh):
    return jax.shard_map(
        per_device,
        mesh=mesh,
        in_specs=(
            P("shots", "slab", None, None),
            P("shots", "slab", None, None),
            P("shots", "slab", None, None),
            P("shots", "slab", None, None),
            P("slab", None, None),
            P(None, "shots"),
            P(None, "shots", None),
            P("shots"),
            P("shots"),
            P("shots"),
            P("shots"),
            P("shots"),
            P("shots", None),
        ),
        out_specs=(
            P("shots", "slab", None, None),
            P("shots", "slab", None, None),
            P("slab", None, None),
        ),
        check_vma=False,
    )
```

```python
import jax
import jax.numpy as jnp
from jax import lax
from jax.sharding import PartitionSpec as P
from jax.experimental import pallas as pl
from jax.experimental.pallas import tpu as pltpu
import functools

STEPS = 2


COEF = (-205.0 / 72.0, 8.0 / 5.0, -1.0 / 5.0, 8.0 / 315.0, -1.0 / 560.0)


WIN_Y = 44
WIN_X = 88


def band_corner(source_y, source_x, half_y, half_x, rows_y, cols_x):
    row0 = jnp.clip(source_y - half_y, 0, rows_y - WIN_Y)
    col0 = jnp.clip(source_x - half_x, 0, cols_x - WIN_X)
    return row0, col0


def selectors(row0, col0, rows_y, cols_x):
    pick_y = (
        jnp.arange(rows_y, dtype=jnp.int32)[None, :, None]
        == row0[:, None, None] + jnp.arange(WIN_Y, dtype=jnp.int32)[None, None, :]
    ).astype(jnp.float32)
    pick_x = (
        jnp.arange(cols_x, dtype=jnp.int32)[None, None, :]
        == col0[:, None, None] + jnp.arange(WIN_X, dtype=jnp.int32)[None, :, None]
    ).astype(jnp.float32)
    return pick_y, pick_x


def exact_einsum(spec, a, b):
    return jnp.einsum(
        spec, a, b, precision=lax.Precision.HIGHEST, preferred_element_type=jnp.float32
    )


def cut_windows(layers, pick_y, pick_x):
    fields, shots, width = layers.shape[:3]
    part = exact_einsum("fsjyx,sbx->fsjyb", layers, pick_x)
    part = exact_einsum("sya,fsjyb->fsjab", pick_y, part)
    return part.reshape(fields, shots, -1, 128)


def paste_windows(flat, pick_y, pick_x, width):
    fields, shots = flat.shape[:2]
    part = flat.reshape(fields, shots, width, WIN_Y, WIN_X)
    part = exact_einsum("fsjab,sbx->fsjax", part, pick_x)
    return exact_einsum("sya,fsjax->fsjyx", pick_y, part)


def halo_kernel(n, send_ref, recv_ref, sems):
    i = lax.axis_index("slab")
    shot = lax.axis_index("shots")
    mesh_id = pl.DeviceIdType.MESH
    has_up = i + 1 < n
    has_down = i >= 1
    barrier = pltpu.get_barrier_semaphore()

    @pl.when(has_up)
    def _():
        pl.semaphore_signal(barrier, inc=1, device_id=(i + 1, shot), device_id_type=mesh_id)

    @pl.when(has_down)
    def _():
        pl.semaphore_signal(barrier, inc=1, device_id=(i - 1, shot), device_id_type=mesh_id)

    pl.semaphore_wait(barrier, has_up.astype(jnp.int32) + has_down.astype(jnp.int32))

    def remote(side, target):
        return pltpu.make_async_remote_copy(
            src_ref=send_ref.at[side],
            dst_ref=recv_ref.at[side],
            send_sem=sems.at[side],
            recv_sem=sems.at[2 + side],
            device_id=(target, shot),
            device_id_type=mesh_id,
        )

    @pl.when(has_up)
    def _():
        remote(0, i + 1).start()

    @pl.when(has_down)
    def _():
        remote(1, i - 1).start()

    @pl.when(has_up)
    def _():
        remote(0, i + 1).wait_send()
        remote(1, i).wait_recv()

    @pl.when(has_down)
    def _():
        remote(1, i - 1).wait_send()
        remote(0, i).wait_recv()


def exchange(both, call_id):
    n = lax.axis_size("slab")
    shape = both.shape
    total = both[0].size // 128
    vmem = pl.BlockSpec(memory_space=pltpu.VMEM)
    recv = pl.pallas_call(
        functools.partial(halo_kernel, n),
        out_shape=jax.ShapeDtypeStruct((2, total, 128), jnp.float32),
        in_specs=[vmem],
        out_specs=vmem,
        scratch_shapes=[pltpu.SemaphoreType.DMA((4,))],
        compiler_params=pltpu.CompilerParams(collective_id=call_id, has_side_effects=True),
    )(both.reshape(2, total, 128))
    return recv.reshape(shape)


def extended(block, pick_y, pick_x, width, call_id):
    dim = 2
    sides = jnp.stack(
        [
            lax.slice_in_dim(block, block.shape[dim] - width, None, axis=dim),
            lax.slice_in_dim(block, 0, width, axis=dim),
        ]
    )
    part = exact_einsum("zfsjyx,sbx->zfsjyb", sides, pick_x)
    part = exact_einsum("sya,zfsjyb->zfsjab", pick_y, part)
    got = exchange(part, call_id)
    i = lax.axis_index("slab")
    present = jnp.stack([i >= 1, i + 1 < lax.axis_size("slab")])
    got = jnp.where(present[:, None, None, None, None, None], got, 0.0)
    got = exact_einsum("zfsjab,sbx->zfsjax", got, pick_x)
    got = exact_einsum("sya,zfsjax->zfsjyx", pick_y, got)
    return jnp.concatenate([got[0], block, got[1]], axis=dim)


def laplace(padded):
    axis_z = padded.ndim - 3
    length = padded.shape[axis_z] - 8
    center = lax.slice_in_dim(padded, 4, 4 + length, axis=axis_z)
    total = 3.0 * COEF[0] * center
    for shift_k in range(1, 5):
        upper = lax.slice_in_dim(padded, 4 + shift_k, 4 + shift_k + length, axis=axis_z)
        lower = lax.slice_in_dim(padded, 4 - shift_k, 4 - shift_k + length, axis=axis_z)
        total = total + COEF[shift_k] * (upper + lower)
    widths = [(0, 0)] * (center.ndim - 2) + [(4, 4), (4, 4)]
    plane = jnp.pad(center, widths)
    rows_y = center.shape[-2]
    cols_x = center.shape[-1]
    for shift_k in range(1, 5):
        side_y = (
            plane[..., 4 + shift_k : 4 + shift_k + rows_y, 4 : 4 + cols_x]
            + plane[..., 4 - shift_k : 4 - shift_k + rows_y, 4 : 4 + cols_x]
        )
        side_x = (
            plane[..., 4 : 4 + rows_y, 4 + shift_k : 4 + shift_k + cols_x]
            + plane[..., 4 : 4 + rows_y, 4 - shift_k : 4 - shift_k + cols_x]
        )
        total = total + COEF[shift_k] * (side_y + side_x)
    return total


def band_mask(source_y, source_x, half_y, half_x, rows_y, cols_x):
    grid_y = jnp.arange(rows_y, dtype=jnp.int32)
    grid_x = jnp.arange(cols_x, dtype=jnp.int32)
    inside_y = jnp.abs(grid_y[None, :, None] - source_y[:, None, None]) <= half_y[:, None, None]
    inside_x = jnp.abs(grid_x[None, None, :] - source_x[:, None, None]) <= half_x[:, None, None]
    return (inside_y & inside_x).astype(jnp.float32)


def point_field(depth_local, row, col, values, length, rows_y, cols_x):
    grid_z = jnp.arange(length, dtype=jnp.int32)[None, :, None, None]
    grid_y = jnp.arange(rows_y, dtype=jnp.int32)[None, None, :, None]
    grid_x = jnp.arange(cols_x, dtype=jnp.int32)[None, None, None, :]
    hit = (
        (grid_z == depth_local[:, None, None, None])
        & (grid_y == row[:, None, None, None])
        & (grid_x == col[:, None, None, None])
    )
    return jnp.where(hit, values[:, None, None, None], 0.0)


def receiver_field(cells, traces, begin, length, rows_y, cols_x):
    plane = rows_y * cols_x
    depth = cells // plane
    rest = cells - depth * plane
    row = rest // cols_x
    col = rest - row * cols_x
    local = depth - begin
    slab_rows = jnp.arange(length * rows_y, dtype=jnp.int32)
    key = local * rows_y + row
    left = jnp.where(slab_rows[None, :, None] == key[:, None, :], traces[:, None, :], 0.0)
    right = (col[:, :, None] == jnp.arange(cols_x, dtype=jnp.int32)[None, None, :]).astype(
        jnp.float32
    )
    field = jnp.einsum(
        "szr,srx->szx",
        left,
        right,
        precision=lax.Precision.HIGHEST,
        preferred_element_type=jnp.float32,
    )
    return field.reshape(cells.shape[0], length, rows_y, cols_x)


def tree_sum(value, axis):
    count = lax.axis_size(axis)
    me = lax.axis_index(axis)
    shape = value.shape
    piece = value.reshape(-1)
    bits = []
    stride = 1
    while stride < count:
        bits.append(stride)
        stride *= 2
    for stride in bits:
        upper = (me // stride) % 2 == 1
        halves = piece.reshape(2, -1)
        send = jnp.where(upper, halves[0], halves[1])
        keep = jnp.where(upper, halves[1], halves[0])
        pairs = [(i, i ^ stride) for i in range(count)]
        piece = keep + lax.ppermute(send, axis, pairs)
    for stride in reversed(bits):
        upper = (me // stride) % 2 == 1
        pairs = [(i, i ^ stride) for i in range(count)]
        other = lax.ppermute(piece, axis, pairs)
        piece = jnp.where(upper, jnp.concatenate([other, piece]), jnp.concatenate([piece, other]))
    return piece.reshape(shape)


def allreduce_kernel(chips, local_ref, out_ref, half_in, gathered, spread, send_sems, recv_sems):
    me = lax.axis_index("shots")
    slab = lax.axis_index("slab")
    core = me % 2
    chip = me // 2
    mesh_id = pl.DeviceIdType.MESH
    rows = local_ref.shape[0] // 2
    chunk = rows // chips
    barrier = pltpu.get_barrier_semaphore()
    pl.semaphore_signal(barrier, inc=1, device_id=(slab, me + 1 - 2 * core), device_id_type=mesh_id)
    for k in range(1, chips):
        peer = lax.rem(chip + k, chips) * 2 + core
        pl.semaphore_signal(barrier, inc=1, device_id=(slab, peer), device_id_type=mesh_id)
    pl.semaphore_wait(barrier, chips)

    def remote(src, dst, slot, target):
        return pltpu.make_async_remote_copy(
            src_ref=src,
            dst_ref=dst,
            send_sem=send_sems.at[slot],
            recv_sem=recv_sems.at[slot],
            device_id=(slab, target),
            device_id_type=mesh_id,
        )

    mine = pl.ds(pl.multiple_of(core * rows, 8), rows)
    theirs = pl.ds(pl.multiple_of((1 - core) * rows, 8), rows)
    copy = remote(local_ref.at[theirs], half_in, 0, me + 1 - 2 * core)
    copy.start()
    copy.wait()
    out_ref[mine] = local_ref[mine] + half_in[...]
    copies = []
    for k in range(1, chips):
        target = lax.rem(chip + k, chips)
        src = out_ref.at[pl.ds(pl.multiple_of(core * rows + target * chunk, 8), chunk)]
        copy = remote(src, gathered.at[k], k, target * 2 + core)
        copy.start()
        copies.append(copy)
    for copy in copies:
        copy.wait()
    own = pl.ds(pl.multiple_of(core * rows + chip * chunk, 8), chunk)
    total = out_ref[own]
    for k in range(1, chips):
        total = total + gathered[k]
    out_ref[own] = total
    copies = []
    for k in range(1, chips):
        target = lax.rem(chip + k, chips)
        copy = remote(out_ref.at[own], spread.at[k], chips + k, target * 2 + core)
        copy.start()
        copies.append(copy)
    for copy in copies:
        copy.wait()
    for k in range(1, chips):
        source = lax.rem(chip + chips - k, chips)
        out_ref[pl.ds(pl.multiple_of(core * rows + source * chunk, 8), chunk)] = spread[k]
    copy = remote(out_ref.at[mine], out_ref.at[mine], 2 * chips, me + 1 - 2 * core)
    copy.start()
    copy.wait()


def shots_sum(value):
    chips = lax.axis_size("shots") // 2
    shape = value.shape
    chunks = value.reshape(-1, 128)
    rows = chunks.shape[0]
    out = pl.pallas_call(
        functools.partial(allreduce_kernel, chips),
        out_shape=jax.ShapeDtypeStruct(chunks.shape, jnp.float32),
        in_specs=[pl.BlockSpec(memory_space=pltpu.VMEM)],
        out_specs=pl.BlockSpec(memory_space=pltpu.VMEM),
        scratch_shapes=[
            pltpu.VMEM((rows // 2, 128), jnp.float32),
            pltpu.VMEM((chips, rows // 2 // chips, 128), jnp.float32),
            pltpu.VMEM((chips, rows // 2 // chips, 128), jnp.float32),
            pltpu.SemaphoreType.DMA((2 * chips + 1,)),
            pltpu.SemaphoreType.DMA((2 * chips + 1,)),
        ],
        compiler_params=pltpu.CompilerParams(collective_id=0, has_side_effects=True),
    )(chunks)
    return out.reshape(shape)


def per_device(
    src_prev,
    src_cur,
    rcv_prev,
    rcv_cur,
    velocity,
    wavelet,
    residual_traces,
    source_depth,
    source_y,
    source_x,
    half_y,
    half_x,
    receiver_cell,
):
    shot_count, depth, rows_y, cols_x = src_cur.shape
    start = lax.axis_index("slab") * depth
    mask = band_mask(source_y, source_x, half_y, half_x, rows_y, cols_x)[:, None]
    row0, col0 = band_corner(source_y, source_x, half_y, half_x, rows_y, cols_x)
    pick_y, pick_x = selectors(row0, col0, rows_y, cols_x)
    terms = []
    up, u, vp, v = (src_prev, src_cur, rcv_prev, rcv_cur)
    for step in range(STEPS):
        stacked = jnp.stack([u, v])
        padded = extended(stacked, pick_y, pick_x, 4, 1 + step)
        lap = laplace(padded)
        sdelta = point_field(
            source_depth - start, source_y, source_x, wavelet[step], depth, rows_y, cols_x
        )
        rdelta = receiver_field(receiver_cell, residual_traces[step], start, depth, rows_y, cols_x)
        unew = mask * (2.0 * u - up + velocity * lap[0] + sdelta)
        vnew = mask * (2.0 * v - vp + velocity * lap[1] + rdelta)
        terms.append(jnp.sum((unew - 2.0 * u + up) * vnew, axis=0))
        up, u, vp, v = (u, unew, v, vnew)
    src_last, rcv_last = (u, v)
    local_sum = terms[0]
    for extra in terms[1:]:
        local_sum = local_sum + extra
    image = shots_sum(local_sum)
    return (src_last, rcv_last, image)


def solution(mesh):
    return jax.shard_map(
        per_device,
        mesh=mesh,
        in_specs=(
            P("shots", "slab", None, None),
            P("shots", "slab", None, None),
            P("shots", "slab", None, None),
            P("shots", "slab", None, None),
            P("slab", None, None),
            P(None, "shots"),
            P(None, "shots", None),
            P("shots"),
            P("shots"),
            P("shots"),
            P("shots"),
            P("shots"),
            P("shots", None),
        ),
        out_specs=(
            P("shots", "slab", None, None),
            P("shots", "slab", None, None),
            P("slab", None, None),
        ),
        check_vma=False,
    )
```

```python
import jax
import jax.numpy as jnp
from jax import lax
from jax.sharding import PartitionSpec as P
from jax.experimental import pallas as pl
from jax.experimental.pallas import tpu as pltpu
import functools

STEPS = 2


COEF = (-205.0 / 72.0, 8.0 / 5.0, -1.0 / 5.0, 8.0 / 315.0, -1.0 / 560.0)


WIN_Y = 44
WIN_X = 88


def band_corner(source_y, source_x, half_y, half_x, rows_y, cols_x):
    row0 = jnp.clip(source_y - half_y, 0, rows_y - WIN_Y)
    col0 = jnp.clip(source_x - half_x, 0, cols_x - WIN_X)
    return row0, col0


def selectors(row0, col0, rows_y, cols_x):
    pick_y = (
        jnp.arange(rows_y, dtype=jnp.int32)[None, :, None]
        == row0[:, None, None] + jnp.arange(WIN_Y, dtype=jnp.int32)[None, None, :]
    ).astype(jnp.float32)
    pick_x = (
        jnp.arange(cols_x, dtype=jnp.int32)[None, None, :]
        == col0[:, None, None] + jnp.arange(WIN_X, dtype=jnp.int32)[None, :, None]
    ).astype(jnp.float32)
    return pick_y, pick_x


def exact_einsum(spec, a, b):
    return jnp.einsum(
        spec, a, b, precision=lax.Precision.HIGHEST, preferred_element_type=jnp.float32
    )


def cut_windows(layers, pick_y, pick_x):
    fields, shots, width = layers.shape[:3]
    part = exact_einsum("fsjyx,sbx->fsjyb", layers, pick_x)
    part = exact_einsum("sya,fsjyb->fsjab", pick_y, part)
    return part.reshape(fields, shots, -1, 128)


def paste_windows(flat, pick_y, pick_x, width):
    fields, shots = flat.shape[:2]
    part = flat.reshape(fields, shots, width, WIN_Y, WIN_X)
    part = exact_einsum("fsjab,sbx->fsjax", part, pick_x)
    return exact_einsum("sya,fsjax->fsjyx", pick_y, part)


def halo_kernel(n, send_ref, recv_ref, sems):
    i = lax.axis_index("slab")
    shot = lax.axis_index("shots")
    mesh_id = pl.DeviceIdType.MESH
    has_up = i + 1 < n
    has_down = i >= 1
    barrier = pltpu.get_barrier_semaphore()

    @pl.when(has_up)
    def _():
        pl.semaphore_signal(barrier, inc=1, device_id=(i + 1, shot), device_id_type=mesh_id)

    @pl.when(has_down)
    def _():
        pl.semaphore_signal(barrier, inc=1, device_id=(i - 1, shot), device_id_type=mesh_id)

    pl.semaphore_wait(barrier, has_up.astype(jnp.int32) + has_down.astype(jnp.int32))

    def remote(side, target):
        return pltpu.make_async_remote_copy(
            src_ref=send_ref.at[side],
            dst_ref=recv_ref.at[side],
            send_sem=sems.at[side],
            recv_sem=sems.at[2 + side],
            device_id=(target, shot),
            device_id_type=mesh_id,
        )

    @pl.when(has_up)
    def _():
        remote(0, i + 1).start()

    @pl.when(has_down)
    def _():
        remote(1, i - 1).start()

    @pl.when(has_up)
    def _():
        remote(0, i + 1).wait_send()
        remote(1, i).wait_recv()

    @pl.when(has_down)
    def _():
        remote(1, i - 1).wait_send()
        remote(0, i).wait_recv()


def exchange(both, call_id):
    n = lax.axis_size("slab")
    shape = both.shape
    total = both[0].size // 128
    vmem = pl.BlockSpec(memory_space=pltpu.VMEM)
    recv = pl.pallas_call(
        functools.partial(halo_kernel, n),
        out_shape=jax.ShapeDtypeStruct((2, total, 128), jnp.float32),
        in_specs=[vmem],
        out_specs=vmem,
        scratch_shapes=[pltpu.SemaphoreType.DMA((4,))],
        compiler_params=pltpu.CompilerParams(collective_id=call_id, has_side_effects=True),
    )(both.reshape(2, total, 128))
    return recv.reshape(shape)


def extended(block, pick_y, pick_x, width, call_id):
    dim = 2
    sides = jnp.stack(
        [
            lax.slice_in_dim(block, block.shape[dim] - width, None, axis=dim),
            lax.slice_in_dim(block, 0, width, axis=dim),
        ]
    )
    part = exact_einsum("zfsjyx,sbx->zfsjyb", sides, pick_x)
    part = exact_einsum("sya,zfsjyb->zfsjab", pick_y, part)
    got = exchange(part, call_id)
    i = lax.axis_index("slab")
    present = jnp.stack([i >= 1, i + 1 < lax.axis_size("slab")])
    got = jnp.where(present[:, None, None, None, None, None], got, 0.0)
    got = exact_einsum("zfsjab,sbx->zfsjax", got, pick_x)
    got = exact_einsum("sya,zfsjax->zfsjyx", pick_y, got)
    return jnp.concatenate([got[0], block, got[1]], axis=dim)


def laplace(padded):
    axis_z = padded.ndim - 3
    length = padded.shape[axis_z] - 8
    center = lax.slice_in_dim(padded, 4, 4 + length, axis=axis_z)
    total = 3.0 * COEF[0] * center
    for shift_k in range(1, 5):
        upper = lax.slice_in_dim(padded, 4 + shift_k, 4 + shift_k + length, axis=axis_z)
        lower = lax.slice_in_dim(padded, 4 - shift_k, 4 - shift_k + length, axis=axis_z)
        total = total + COEF[shift_k] * (upper + lower)
    widths = [(0, 0)] * (center.ndim - 2) + [(4, 4), (4, 4)]
    plane = jnp.pad(center, widths)
    rows_y = center.shape[-2]
    cols_x = center.shape[-1]
    for shift_k in range(1, 5):
        side_y = (
            plane[..., 4 + shift_k : 4 + shift_k + rows_y, 4 : 4 + cols_x]
            + plane[..., 4 - shift_k : 4 - shift_k + rows_y, 4 : 4 + cols_x]
        )
        side_x = (
            plane[..., 4 : 4 + rows_y, 4 + shift_k : 4 + shift_k + cols_x]
            + plane[..., 4 : 4 + rows_y, 4 - shift_k : 4 - shift_k + cols_x]
        )
        total = total + COEF[shift_k] * (side_y + side_x)
    return total


def band_mask(source_y, source_x, half_y, half_x, rows_y, cols_x):
    grid_y = jnp.arange(rows_y, dtype=jnp.int32)
    grid_x = jnp.arange(cols_x, dtype=jnp.int32)
    inside_y = jnp.abs(grid_y[None, :, None] - source_y[:, None, None]) <= half_y[:, None, None]
    inside_x = jnp.abs(grid_x[None, None, :] - source_x[:, None, None]) <= half_x[:, None, None]
    return (inside_y & inside_x).astype(jnp.float32)


def point_field(depth_local, row, col, values, length, rows_y, cols_x):
    grid_z = jnp.arange(length, dtype=jnp.int32)[None, :, None, None]
    grid_y = jnp.arange(rows_y, dtype=jnp.int32)[None, None, :, None]
    grid_x = jnp.arange(cols_x, dtype=jnp.int32)[None, None, None, :]
    hit = (
        (grid_z == depth_local[:, None, None, None])
        & (grid_y == row[:, None, None, None])
        & (grid_x == col[:, None, None, None])
    )
    return jnp.where(hit, values[:, None, None, None], 0.0)


def receiver_field(cells, traces, begin, length, rows_y, cols_x):
    plane = rows_y * cols_x
    depth = cells // plane
    rest = cells - depth * plane
    row = rest // cols_x
    col = rest - row * cols_x
    local = depth - begin
    slab_rows = jnp.arange(length * rows_y, dtype=jnp.int32)
    key = local * rows_y + row
    left = jnp.where(slab_rows[None, :, None] == key[:, None, :], traces[:, None, :], 0.0)
    right = (col[:, :, None] == jnp.arange(cols_x, dtype=jnp.int32)[None, None, :]).astype(
        jnp.float32
    )
    field = jnp.einsum(
        "szr,srx->szx",
        left,
        right,
        precision=lax.Precision.HIGHEST,
        preferred_element_type=jnp.float32,
    )
    return field.reshape(cells.shape[0], length, rows_y, cols_x)


def tree_sum(value, axis):
    count = lax.axis_size(axis)
    me = lax.axis_index(axis)
    shape = value.shape
    piece = value.reshape(-1)
    bits = []
    stride = 1
    while stride < count:
        bits.append(stride)
        stride *= 2
    for stride in bits:
        upper = (me // stride) % 2 == 1
        halves = piece.reshape(2, -1)
        send = jnp.where(upper, halves[0], halves[1])
        keep = jnp.where(upper, halves[1], halves[0])
        pairs = [(i, i ^ stride) for i in range(count)]
        piece = keep + lax.ppermute(send, axis, pairs)
    for stride in reversed(bits):
        upper = (me // stride) % 2 == 1
        pairs = [(i, i ^ stride) for i in range(count)]
        other = lax.ppermute(piece, axis, pairs)
        piece = jnp.where(upper, jnp.concatenate([other, piece]), jnp.concatenate([piece, other]))
    return piece.reshape(shape)


def allreduce_kernel(chips, local_ref, out_ref, half_in, gathered, spread, send_sems, recv_sems):
    me = lax.axis_index("shots")
    slab = lax.axis_index("slab")
    core = me % 2
    chip = me // 2
    mesh_id = pl.DeviceIdType.MESH
    rows = local_ref.shape[0] // 2
    chunk = rows // chips
    barrier = pltpu.get_barrier_semaphore()
    pl.semaphore_signal(barrier, inc=1, device_id=(slab, me + 1 - 2 * core), device_id_type=mesh_id)
    for k in range(1, chips):
        peer = lax.rem(chip + k, chips) * 2 + core
        pl.semaphore_signal(barrier, inc=1, device_id=(slab, peer), device_id_type=mesh_id)
    pl.semaphore_wait(barrier, chips)

    def remote(src, dst, slot, target):
        return pltpu.make_async_remote_copy(
            src_ref=src,
            dst_ref=dst,
            send_sem=send_sems.at[slot],
            recv_sem=recv_sems.at[slot],
            device_id=(slab, target),
            device_id_type=mesh_id,
        )

    mine = pl.ds(pl.multiple_of(core * rows, 8), rows)
    theirs = pl.ds(pl.multiple_of((1 - core) * rows, 8), rows)
    copy = remote(local_ref.at[theirs], half_in, 0, me + 1 - 2 * core)
    copy.start()
    copy.wait()
    out_ref[mine] = local_ref[mine] + half_in[...]
    copies = []
    for k in range(1, chips):
        target = lax.rem(chip + k, chips)
        src = out_ref.at[pl.ds(pl.multiple_of(core * rows + target * chunk, 8), chunk)]
        copy = remote(src, gathered.at[k], k, target * 2 + core)
        copy.start()
        copies.append(copy)
    for copy in copies:
        copy.wait()
    own = pl.ds(pl.multiple_of(core * rows + chip * chunk, 8), chunk)
    total = out_ref[own]
    for k in range(1, chips):
        total = total + gathered[k]
    out_ref[own] = total
    copies = []
    for k in range(1, chips):
        target = lax.rem(chip + k, chips)
        copy = remote(out_ref.at[own], spread.at[k], chips + k, target * 2 + core)
        copy.start()
        copies.append(copy)
    for copy in copies:
        copy.wait()
    for k in range(1, chips):
        source = lax.rem(chip + chips - k, chips)
        out_ref[pl.ds(pl.multiple_of(core * rows + source * chunk, 8), chunk)] = spread[k]
    copy = remote(out_ref.at[mine], out_ref.at[mine], 2 * chips, me + 1 - 2 * core)
    copy.start()
    copy.wait()


def shots_sum(value):
    chips = lax.axis_size("shots") // 2
    shape = value.shape
    chunks = value.reshape(-1, 128)
    rows = chunks.shape[0]
    out = pl.pallas_call(
        functools.partial(allreduce_kernel, chips),
        out_shape=jax.ShapeDtypeStruct(chunks.shape, jnp.float32),
        in_specs=[pl.BlockSpec(memory_space=pltpu.VMEM)],
        out_specs=pl.BlockSpec(memory_space=pltpu.VMEM),
        scratch_shapes=[
            pltpu.VMEM((rows // 2, 128), jnp.float32),
            pltpu.VMEM((chips, rows // 2 // chips, 128), jnp.float32),
            pltpu.VMEM((chips, rows // 2 // chips, 128), jnp.float32),
            pltpu.SemaphoreType.DMA((2 * chips + 1,)),
            pltpu.SemaphoreType.DMA((2 * chips + 1,)),
        ],
        compiler_params=pltpu.CompilerParams(collective_id=0, has_side_effects=True),
    )(chunks)
    return out.reshape(shape)


def per_device(
    src_prev,
    src_cur,
    rcv_prev,
    rcv_cur,
    velocity,
    wavelet,
    residual_traces,
    source_depth,
    source_y,
    source_x,
    half_y,
    half_x,
    receiver_cell,
):
    shot_count, depth, rows_y, cols_x = src_cur.shape
    start = lax.axis_index("slab") * depth
    mask = band_mask(source_y, source_x, half_y, half_x, rows_y, cols_x)[:, None]
    row0, col0 = band_corner(source_y, source_x, half_y, half_x, rows_y, cols_x)
    pick_y, pick_x = selectors(row0, col0, rows_y, cols_x)
    terms = []
    up, u, vp, v = (src_prev, src_cur, rcv_prev, rcv_cur)
    for step in range(STEPS):
        stacked = jnp.stack([u, v])
        padded = extended(stacked, pick_y, pick_x, 4, 1 + step)
        lap = laplace(padded)
        sdelta = point_field(
            source_depth - start, source_y, source_x, wavelet[step], depth, rows_y, cols_x
        )
        rdelta = receiver_field(receiver_cell, residual_traces[step], start, depth, rows_y, cols_x)
        unew = mask * (2.0 * u - up + velocity * lap[0] + sdelta)
        vnew = mask * (2.0 * v - vp + velocity * lap[1] + rdelta)
        terms.append((unew - 2.0 * u + up) * vnew)
        up, u, vp, v = (u, unew, v, vnew)
    src_last, rcv_last = (u, v)
    local_sum = terms[0]
    for extra in terms[1:]:
        local_sum = local_sum + extra
    image = shots_sum(jnp.sum(local_sum, axis=0))
    return (src_last, rcv_last, image)


def solution(mesh):
    return jax.shard_map(
        per_device,
        mesh=mesh,
        in_specs=(
            P("shots", "slab", None, None),
            P("shots", "slab", None, None),
            P("shots", "slab", None, None),
            P("shots", "slab", None, None),
            P("slab", None, None),
            P(None, "shots"),
            P(None, "shots", None),
            P("shots"),
            P("shots"),
            P("shots"),
            P("shots"),
            P("shots"),
            P("shots", None),
        ),
        out_specs=(
            P("shots", "slab", None, None),
            P("shots", "slab", None, None),
            P("slab", None, None),
        ),
        check_vma=False,
    )
```

```python
import jax
import jax.numpy as jnp
from jax import lax
from jax.sharding import PartitionSpec as P
from jax.experimental import pallas as pl
from jax.experimental.pallas import tpu as pltpu
import functools

STEPS = 2


COEF = (-205.0 / 72.0, 8.0 / 5.0, -1.0 / 5.0, 8.0 / 315.0, -1.0 / 560.0)


WIN_Y = 44
WIN_X = 88


def band_corner(source_y, source_x, half_y, half_x, rows_y, cols_x):
    row0 = jnp.clip(source_y - half_y, 0, rows_y - WIN_Y)
    col0 = jnp.clip(source_x - half_x, 0, cols_x - WIN_X)
    return row0, col0


def selectors(row0, col0, rows_y, cols_x):
    pick_y = (
        jnp.arange(rows_y, dtype=jnp.int32)[None, :, None]
        == row0[:, None, None] + jnp.arange(WIN_Y, dtype=jnp.int32)[None, None, :]
    ).astype(jnp.float32)
    pick_x = (
        jnp.arange(cols_x, dtype=jnp.int32)[None, None, :]
        == col0[:, None, None] + jnp.arange(WIN_X, dtype=jnp.int32)[None, :, None]
    ).astype(jnp.float32)
    return pick_y, pick_x


def exact_einsum(spec, a, b):
    return jnp.einsum(
        spec, a, b, precision=lax.Precision.HIGHEST, preferred_element_type=jnp.float32
    )


def cut_windows(layers, pick_y, pick_x):
    fields, shots, width = layers.shape[:3]
    part = exact_einsum("fsjyx,sbx->fsjyb", layers, pick_x)
    part = exact_einsum("sya,fsjyb->fsjab", pick_y, part)
    return part.reshape(fields, shots, -1, 128)


def paste_windows(flat, pick_y, pick_x, width):
    fields, shots = flat.shape[:2]
    part = flat.reshape(fields, shots, width, WIN_Y, WIN_X)
    part = exact_einsum("fsjab,sbx->fsjax", part, pick_x)
    return exact_einsum("sya,fsjax->fsjyx", pick_y, part)


def halo_kernel(n, send_ref, recv_ref, sems):
    i = lax.axis_index("slab")
    shot = lax.axis_index("shots")
    mesh_id = pl.DeviceIdType.MESH
    has_up = i + 1 < n
    has_down = i >= 1
    barrier = pltpu.get_barrier_semaphore()

    @pl.when(has_up)
    def _():
        pl.semaphore_signal(barrier, inc=1, device_id=(i + 1, shot), device_id_type=mesh_id)

    @pl.when(has_down)
    def _():
        pl.semaphore_signal(barrier, inc=1, device_id=(i - 1, shot), device_id_type=mesh_id)

    pl.semaphore_wait(barrier, has_up.astype(jnp.int32) + has_down.astype(jnp.int32))

    def remote(side, target):
        return pltpu.make_async_remote_copy(
            src_ref=send_ref.at[side],
            dst_ref=recv_ref.at[side],
            send_sem=sems.at[side],
            recv_sem=sems.at[2 + side],
            device_id=(target, shot),
            device_id_type=mesh_id,
        )

    @pl.when(has_up)
    def _():
        remote(0, i + 1).start()

    @pl.when(has_down)
    def _():
        remote(1, i - 1).start()

    @pl.when(has_up)
    def _():
        remote(0, i + 1).wait_send()
        remote(1, i).wait_recv()

    @pl.when(has_down)
    def _():
        remote(1, i - 1).wait_send()
        remote(0, i).wait_recv()


def exchange(both, call_id):
    n = lax.axis_size("slab")
    shape = both.shape
    total = both[0].size // 128
    vmem = pl.BlockSpec(memory_space=pltpu.VMEM)
    recv = pl.pallas_call(
        functools.partial(halo_kernel, n),
        out_shape=jax.ShapeDtypeStruct((2, total, 128), jnp.float32),
        in_specs=[vmem],
        out_specs=vmem,
        scratch_shapes=[pltpu.SemaphoreType.DMA((4,))],
        compiler_params=pltpu.CompilerParams(collective_id=call_id, has_side_effects=True),
    )(both.reshape(2, total, 128))
    return recv.reshape(shape)


def extended(block, pick_y, pick_x, width, call_id):
    dim = 2
    sides = jnp.stack(
        [
            lax.slice_in_dim(block, block.shape[dim] - width, None, axis=dim),
            lax.slice_in_dim(block, 0, width, axis=dim),
        ]
    )
    part = exact_einsum("zfsjyx,sbx->zfsjyb", sides, pick_x)
    part = exact_einsum("sya,zfsjyb->zfsjab", pick_y, part)
    got = exchange(part, call_id)
    i = lax.axis_index("slab")
    present = jnp.stack([i >= 1, i + 1 < lax.axis_size("slab")])
    got = jnp.where(present[:, None, None, None, None, None], got, 0.0)
    got = exact_einsum("zfsjab,sbx->zfsjax", got, pick_x)
    got = exact_einsum("sya,zfsjax->zfsjyx", pick_y, got)
    return jnp.concatenate([got[0], block, got[1]], axis=dim)


def laplace(padded):
    axis_z = padded.ndim - 3
    length = padded.shape[axis_z] - 8
    center = lax.slice_in_dim(padded, 4, 4 + length, axis=axis_z)
    total = 3.0 * COEF[0] * center
    for shift_k in range(1, 5):
        upper = lax.slice_in_dim(padded, 4 + shift_k, 4 + shift_k + length, axis=axis_z)
        lower = lax.slice_in_dim(padded, 4 - shift_k, 4 - shift_k + length, axis=axis_z)
        total = total + COEF[shift_k] * (upper + lower)
    widths = [(0, 0)] * (center.ndim - 2) + [(4, 4), (4, 4)]
    plane = jnp.pad(center, widths)
    rows_y = center.shape[-2]
    cols_x = center.shape[-1]
    for shift_k in range(1, 5):
        side_y = (
            plane[..., 4 + shift_k : 4 + shift_k + rows_y, 4 : 4 + cols_x]
            + plane[..., 4 - shift_k : 4 - shift_k + rows_y, 4 : 4 + cols_x]
        )
        side_x = (
            plane[..., 4 : 4 + rows_y, 4 + shift_k : 4 + shift_k + cols_x]
            + plane[..., 4 : 4 + rows_y, 4 - shift_k : 4 - shift_k + cols_x]
        )
        total = total + COEF[shift_k] * (side_y + side_x)
    return total


def band_mask(source_y, source_x, half_y, half_x, rows_y, cols_x):
    grid_y = jnp.arange(rows_y, dtype=jnp.int32)
    grid_x = jnp.arange(cols_x, dtype=jnp.int32)
    inside_y = jnp.abs(grid_y[None, :, None] - source_y[:, None, None]) <= half_y[:, None, None]
    inside_x = jnp.abs(grid_x[None, None, :] - source_x[:, None, None]) <= half_x[:, None, None]
    return (inside_y & inside_x).astype(jnp.float32)


def point_field(depth_local, row, col, values, length, rows_y, cols_x):
    grid_z = jnp.arange(length, dtype=jnp.int32)[None, :, None, None]
    grid_y = jnp.arange(rows_y, dtype=jnp.int32)[None, None, :, None]
    grid_x = jnp.arange(cols_x, dtype=jnp.int32)[None, None, None, :]
    hit = (
        (grid_z == depth_local[:, None, None, None])
        & (grid_y == row[:, None, None, None])
        & (grid_x == col[:, None, None, None])
    )
    return jnp.where(hit, values[:, None, None, None], 0.0)


def receiver_field(cells, traces, begin, length, rows_y, cols_x):
    plane = rows_y * cols_x
    depth = cells // plane
    rest = cells - depth * plane
    row = rest // cols_x
    col = rest - row * cols_x
    local = depth - begin
    slab_rows = jnp.arange(length * rows_y, dtype=jnp.int32)
    key = local * rows_y + row
    left = jnp.where(slab_rows[None, :, None] == key[:, None, :], traces[:, None, :], 0.0)
    right = (col[:, :, None] == jnp.arange(cols_x, dtype=jnp.int32)[None, None, :]).astype(
        jnp.float32
    )
    field = jnp.einsum(
        "szr,srx->szx",
        left,
        right,
        precision=lax.Precision.HIGHEST,
        preferred_element_type=jnp.float32,
    )
    return field.reshape(cells.shape[0], length, rows_y, cols_x)


def tree_sum(value, axis):
    count = lax.axis_size(axis)
    me = lax.axis_index(axis)
    shape = value.shape
    piece = value.reshape(-1)
    bits = []
    stride = 1
    while stride < count:
        bits.append(stride)
        stride *= 2
    for stride in bits:
        upper = (me // stride) % 2 == 1
        halves = piece.reshape(2, -1)
        send = jnp.where(upper, halves[0], halves[1])
        keep = jnp.where(upper, halves[1], halves[0])
        pairs = [(i, i ^ stride) for i in range(count)]
        piece = keep + lax.ppermute(send, axis, pairs)
    for stride in reversed(bits):
        upper = (me // stride) % 2 == 1
        pairs = [(i, i ^ stride) for i in range(count)]
        other = lax.ppermute(piece, axis, pairs)
        piece = jnp.where(upper, jnp.concatenate([other, piece]), jnp.concatenate([piece, other]))
    return piece.reshape(shape)


def allreduce_kernel(chips, local_ref, out_ref, half_in, gathered, spread, send_sems, recv_sems):
    me = lax.axis_index("shots")
    slab = lax.axis_index("slab")
    core = me % 2
    chip = me // 2
    mesh_id = pl.DeviceIdType.MESH
    rows = local_ref.shape[0] // 2
    chunk = rows // chips
    barrier = pltpu.get_barrier_semaphore()
    pl.semaphore_signal(barrier, inc=1, device_id=(slab, me + 1 - 2 * core), device_id_type=mesh_id)
    for k in range(1, chips):
        for side in (0, 1):
            peer = lax.rem(chip + k, chips) * 2 + side
            pl.semaphore_signal(barrier, inc=1, device_id=(slab, peer), device_id_type=mesh_id)
    pl.semaphore_wait(barrier, 2 * chips - 1)

    def remote(src, dst, slot, target):
        return pltpu.make_async_remote_copy(
            src_ref=src,
            dst_ref=dst,
            send_sem=send_sems.at[slot],
            recv_sem=recv_sems.at[slot],
            device_id=(slab, target),
            device_id_type=mesh_id,
        )

    mine = pl.ds(pl.multiple_of(core * rows, 8), rows)
    theirs = pl.ds(pl.multiple_of((1 - core) * rows, 8), rows)
    copy = remote(local_ref.at[theirs], half_in, 0, me + 1 - 2 * core)
    copy.start()
    copy.wait()
    out_ref[mine] = local_ref[mine] + half_in[...]
    copies = []
    for k in range(1, chips):
        target = lax.rem(chip + k, chips)
        src = out_ref.at[pl.ds(pl.multiple_of(core * rows + target * chunk, 8), chunk)]
        copy = remote(src, gathered.at[k], k, target * 2 + core)
        copy.start()
        copies.append(copy)
    for copy in copies:
        copy.wait()
    own = pl.ds(pl.multiple_of(core * rows + chip * chunk, 8), chunk)
    total = out_ref[own]
    for k in range(1, chips):
        total = total + gathered[k]
    out_ref[own] = total
    copies = []
    for k in range(chips):
        target = lax.rem(chip + k, chips)
        for other in (0, 1):
            if k == 0 and other == 0:
                continue
            slot = k + chips * other
            copy = remote(
                out_ref.at[own], spread.at[slot], chips + slot, target * 2 + (core + other) % 2
            )
            copy.start()
            copies.append(copy)
    for copy in copies:
        copy.wait()
    for k in range(chips):
        source = lax.rem(chip + chips - k, chips)
        for other in (0, 1):
            if k == 0 and other == 0:
                continue
            half = (core + other) % 2
            out_ref[pl.ds(pl.multiple_of(half * rows + source * chunk, 8), chunk)] = spread[
                k + chips * other
            ]


def shots_sum(value):
    chips = lax.axis_size("shots") // 2
    shape = value.shape
    chunks = value.reshape(-1, 128)
    rows = chunks.shape[0]
    out = pl.pallas_call(
        functools.partial(allreduce_kernel, chips),
        out_shape=jax.ShapeDtypeStruct(chunks.shape, jnp.float32),
        in_specs=[pl.BlockSpec(memory_space=pltpu.VMEM)],
        out_specs=pl.BlockSpec(memory_space=pltpu.VMEM),
        scratch_shapes=[
            pltpu.VMEM((rows // 2, 128), jnp.float32),
            pltpu.VMEM((chips, rows // 2 // chips, 128), jnp.float32),
            pltpu.VMEM((2 * chips, rows // 2 // chips, 128), jnp.float32),
            pltpu.SemaphoreType.DMA((3 * chips,)),
            pltpu.SemaphoreType.DMA((3 * chips,)),
        ],
        compiler_params=pltpu.CompilerParams(collective_id=0, has_side_effects=True),
    )(chunks)
    return out.reshape(shape)


def per_device(
    src_prev,
    src_cur,
    rcv_prev,
    rcv_cur,
    velocity,
    wavelet,
    residual_traces,
    source_depth,
    source_y,
    source_x,
    half_y,
    half_x,
    receiver_cell,
):
    shot_count, depth, rows_y, cols_x = src_cur.shape
    start = lax.axis_index("slab") * depth
    mask = band_mask(source_y, source_x, half_y, half_x, rows_y, cols_x)[:, None]
    row0, col0 = band_corner(source_y, source_x, half_y, half_x, rows_y, cols_x)
    pick_y, pick_x = selectors(row0, col0, rows_y, cols_x)
    terms = []
    up, u, vp, v = (src_prev, src_cur, rcv_prev, rcv_cur)
    for step in range(STEPS):
        stacked = jnp.stack([u, v])
        padded = extended(stacked, pick_y, pick_x, 4, 1 + step)
        lap = laplace(padded)
        sdelta = point_field(
            source_depth - start, source_y, source_x, wavelet[step], depth, rows_y, cols_x
        )
        rdelta = receiver_field(receiver_cell, residual_traces[step], start, depth, rows_y, cols_x)
        unew = mask * (2.0 * u - up + velocity * lap[0] + sdelta)
        vnew = mask * (2.0 * v - vp + velocity * lap[1] + rdelta)
        terms.append(jnp.sum((unew - 2.0 * u + up) * vnew, axis=0))
        up, u, vp, v = (u, unew, v, vnew)
    src_last, rcv_last = (u, v)
    local_sum = terms[0]
    for extra in terms[1:]:
        local_sum = local_sum + extra
    image = shots_sum(local_sum)
    return (src_last, rcv_last, image)


def solution(mesh):
    return jax.shard_map(
        per_device,
        mesh=mesh,
        in_specs=(
            P("shots", "slab", None, None),
            P("shots", "slab", None, None),
            P("shots", "slab", None, None),
            P("shots", "slab", None, None),
            P("slab", None, None),
            P(None, "shots"),
            P(None, "shots", None),
            P("shots"),
            P("shots"),
            P("shots"),
            P("shots"),
            P("shots"),
            P("shots", None),
        ),
        out_specs=(
            P("shots", "slab", None, None),
            P("shots", "slab", None, None),
            P("slab", None, None),
        ),
        check_vma=False,
    )
```

```python
import jax
import jax.numpy as jnp
from jax import lax
from jax.sharding import PartitionSpec as P
from jax.experimental import pallas as pl
from jax.experimental.pallas import tpu as pltpu
import functools

STEPS = 2


COEF = (-205.0 / 72.0, 8.0 / 5.0, -1.0 / 5.0, 8.0 / 315.0, -1.0 / 560.0)


WIN_Y = 44
WIN_X = 88


def band_corner(source_y, source_x, half_y, half_x, rows_y, cols_x):
    row0 = jnp.clip(source_y - half_y, 0, rows_y - WIN_Y)
    col0 = jnp.clip(source_x - half_x, 0, cols_x - WIN_X)
    return row0, col0


def selectors(row0, col0, rows_y, cols_x):
    pick_y = (
        jnp.arange(rows_y, dtype=jnp.int32)[None, :, None]
        == row0[:, None, None] + jnp.arange(WIN_Y, dtype=jnp.int32)[None, None, :]
    ).astype(jnp.float32)
    pick_x = (
        jnp.arange(cols_x, dtype=jnp.int32)[None, None, :]
        == col0[:, None, None] + jnp.arange(WIN_X, dtype=jnp.int32)[None, :, None]
    ).astype(jnp.float32)
    return pick_y, pick_x


def exact_einsum(spec, a, b):
    return jnp.einsum(
        spec, a, b, precision=lax.Precision.HIGHEST, preferred_element_type=jnp.float32
    )


def cut_windows(layers, pick_y, pick_x):
    fields, shots, width = layers.shape[:3]
    part = exact_einsum("fsjyx,sbx->fsjyb", layers, pick_x)
    part = exact_einsum("sya,fsjyb->fsjab", pick_y, part)
    return part.reshape(fields, shots, -1, 128)


def paste_windows(flat, pick_y, pick_x, width):
    fields, shots = flat.shape[:2]
    part = flat.reshape(fields, shots, width, WIN_Y, WIN_X)
    part = exact_einsum("fsjab,sbx->fsjax", part, pick_x)
    return exact_einsum("sya,fsjax->fsjyx", pick_y, part)


def halo_kernel(n, send_ref, recv_ref, sems):
    i = lax.axis_index("slab")
    shot = lax.axis_index("shots")
    mesh_id = pl.DeviceIdType.MESH
    has_up = i + 1 < n
    has_down = i >= 1
    barrier = pltpu.get_barrier_semaphore()

    @pl.when(has_up)
    def _():
        pl.semaphore_signal(barrier, inc=1, device_id=(i + 1, shot), device_id_type=mesh_id)

    @pl.when(has_down)
    def _():
        pl.semaphore_signal(barrier, inc=1, device_id=(i - 1, shot), device_id_type=mesh_id)

    pl.semaphore_wait(barrier, has_up.astype(jnp.int32) + has_down.astype(jnp.int32))

    def remote(side, target):
        return pltpu.make_async_remote_copy(
            src_ref=send_ref.at[side],
            dst_ref=recv_ref.at[side],
            send_sem=sems.at[side],
            recv_sem=sems.at[2 + side],
            device_id=(target, shot),
            device_id_type=mesh_id,
        )

    @pl.when(has_up)
    def _():
        remote(0, i + 1).start()

    @pl.when(has_down)
    def _():
        remote(1, i - 1).start()

    @pl.when(has_up)
    def _():
        remote(0, i + 1).wait_send()
        remote(1, i).wait_recv()

    @pl.when(has_down)
    def _():
        remote(1, i - 1).wait_send()
        remote(0, i).wait_recv()


def exchange(both, call_id):
    n = lax.axis_size("slab")
    shape = both.shape
    total = both[0].size // 128
    vmem = pl.BlockSpec(memory_space=pl.ANY)
    recv = pl.pallas_call(
        functools.partial(halo_kernel, n),
        out_shape=jax.ShapeDtypeStruct((2, total, 128), jnp.float32),
        in_specs=[vmem],
        out_specs=vmem,
        scratch_shapes=[pltpu.SemaphoreType.DMA((4,))],
        compiler_params=pltpu.CompilerParams(collective_id=call_id, has_side_effects=True),
    )(both.reshape(2, total, 128))
    return recv.reshape(shape)


def extended(block, pick_y, pick_x, width, call_id):
    dim = 2
    sides = jnp.stack(
        [
            lax.slice_in_dim(block, block.shape[dim] - width, None, axis=dim),
            lax.slice_in_dim(block, 0, width, axis=dim),
        ]
    )
    part = exact_einsum("zfsjyx,sbx->zfsjyb", sides, pick_x)
    part = exact_einsum("sya,zfsjyb->zfsjab", pick_y, part)
    got = exchange(part, call_id)
    i = lax.axis_index("slab")
    present = jnp.stack([i >= 1, i + 1 < lax.axis_size("slab")])
    got = jnp.where(present[:, None, None, None, None, None], got, 0.0)
    got = exact_einsum("zfsjab,sbx->zfsjax", got, pick_x)
    got = exact_einsum("sya,zfsjax->zfsjyx", pick_y, got)
    return jnp.concatenate([got[0], block, got[1]], axis=dim)


def laplace(padded):
    axis_z = padded.ndim - 3
    length = padded.shape[axis_z] - 8
    center = lax.slice_in_dim(padded, 4, 4 + length, axis=axis_z)
    total = 3.0 * COEF[0] * center
    for shift_k in range(1, 5):
        upper = lax.slice_in_dim(padded, 4 + shift_k, 4 + shift_k + length, axis=axis_z)
        lower = lax.slice_in_dim(padded, 4 - shift_k, 4 - shift_k + length, axis=axis_z)
        total = total + COEF[shift_k] * (upper + lower)
    widths = [(0, 0)] * (center.ndim - 2) + [(4, 4), (4, 4)]
    plane = jnp.pad(center, widths)
    rows_y = center.shape[-2]
    cols_x = center.shape[-1]
    for shift_k in range(1, 5):
        side_y = (
            plane[..., 4 + shift_k : 4 + shift_k + rows_y, 4 : 4 + cols_x]
            + plane[..., 4 - shift_k : 4 - shift_k + rows_y, 4 : 4 + cols_x]
        )
        side_x = (
            plane[..., 4 : 4 + rows_y, 4 + shift_k : 4 + shift_k + cols_x]
            + plane[..., 4 : 4 + rows_y, 4 - shift_k : 4 - shift_k + cols_x]
        )
        total = total + COEF[shift_k] * (side_y + side_x)
    return total


def band_mask(source_y, source_x, half_y, half_x, rows_y, cols_x):
    grid_y = jnp.arange(rows_y, dtype=jnp.int32)
    grid_x = jnp.arange(cols_x, dtype=jnp.int32)
    inside_y = jnp.abs(grid_y[None, :, None] - source_y[:, None, None]) <= half_y[:, None, None]
    inside_x = jnp.abs(grid_x[None, None, :] - source_x[:, None, None]) <= half_x[:, None, None]
    return (inside_y & inside_x).astype(jnp.float32)


def point_field(depth_local, row, col, values, length, rows_y, cols_x):
    grid_z = jnp.arange(length, dtype=jnp.int32)[None, :, None, None]
    grid_y = jnp.arange(rows_y, dtype=jnp.int32)[None, None, :, None]
    grid_x = jnp.arange(cols_x, dtype=jnp.int32)[None, None, None, :]
    hit = (
        (grid_z == depth_local[:, None, None, None])
        & (grid_y == row[:, None, None, None])
        & (grid_x == col[:, None, None, None])
    )
    return jnp.where(hit, values[:, None, None, None], 0.0)


def receiver_field(cells, traces, begin, length, rows_y, cols_x):
    plane = rows_y * cols_x
    depth = cells // plane
    rest = cells - depth * plane
    row = rest // cols_x
    col = rest - row * cols_x
    local = depth - begin
    slab_rows = jnp.arange(length * rows_y, dtype=jnp.int32)
    key = local * rows_y + row
    left = jnp.where(slab_rows[None, :, None] == key[:, None, :], traces[:, None, :], 0.0)
    right = (col[:, :, None] == jnp.arange(cols_x, dtype=jnp.int32)[None, None, :]).astype(
        jnp.float32
    )
    field = jnp.einsum(
        "szr,srx->szx",
        left,
        right,
        precision=lax.Precision.HIGHEST,
        preferred_element_type=jnp.float32,
    )
    return field.reshape(cells.shape[0], length, rows_y, cols_x)


def tree_sum(value, axis):
    count = lax.axis_size(axis)
    me = lax.axis_index(axis)
    shape = value.shape
    piece = value.reshape(-1)
    bits = []
    stride = 1
    while stride < count:
        bits.append(stride)
        stride *= 2
    for stride in bits:
        upper = (me // stride) % 2 == 1
        halves = piece.reshape(2, -1)
        send = jnp.where(upper, halves[0], halves[1])
        keep = jnp.where(upper, halves[1], halves[0])
        pairs = [(i, i ^ stride) for i in range(count)]
        piece = keep + lax.ppermute(send, axis, pairs)
    for stride in reversed(bits):
        upper = (me // stride) % 2 == 1
        pairs = [(i, i ^ stride) for i in range(count)]
        other = lax.ppermute(piece, axis, pairs)
        piece = jnp.where(upper, jnp.concatenate([other, piece]), jnp.concatenate([piece, other]))
    return piece.reshape(shape)


def allreduce_kernel(chips, local_ref, out_ref, half_in, gathered, spread, send_sems, recv_sems):
    me = lax.axis_index("shots")
    slab = lax.axis_index("slab")
    core = me % 2
    chip = me // 2
    mesh_id = pl.DeviceIdType.MESH
    rows = local_ref.shape[0] // 2
    chunk = rows // chips
    barrier = pltpu.get_barrier_semaphore()
    pl.semaphore_signal(barrier, inc=1, device_id=(slab, me + 1 - 2 * core), device_id_type=mesh_id)
    for k in range(1, chips):
        peer = lax.rem(chip + k, chips) * 2 + core
        pl.semaphore_signal(barrier, inc=1, device_id=(slab, peer), device_id_type=mesh_id)
    pl.semaphore_wait(barrier, chips)

    def remote(src, dst, slot, target):
        return pltpu.make_async_remote_copy(
            src_ref=src,
            dst_ref=dst,
            send_sem=send_sems.at[slot],
            recv_sem=recv_sems.at[slot],
            device_id=(slab, target),
            device_id_type=mesh_id,
        )

    mine = pl.ds(pl.multiple_of(core * rows, 8), rows)
    theirs = pl.ds(pl.multiple_of((1 - core) * rows, 8), rows)
    copy = remote(local_ref.at[theirs], half_in, 0, me + 1 - 2 * core)
    copy.start()
    copy.wait()
    out_ref[mine] = local_ref[mine] + half_in[...]
    copies = []
    for k in range(1, chips):
        target = lax.rem(chip + k, chips)
        src = out_ref.at[pl.ds(pl.multiple_of(core * rows + target * chunk, 8), chunk)]
        copy = remote(src, gathered.at[k], k, target * 2 + core)
        copy.start()
        copies.append(copy)
    for copy in copies:
        copy.wait()
    own = pl.ds(pl.multiple_of(core * rows + chip * chunk, 8), chunk)
    total = out_ref[own]
    for k in range(1, chips):
        total = total + gathered[k]
    out_ref[own] = total
    copies = []
    for k in range(1, chips):
        target = lax.rem(chip + k, chips)
        copy = remote(out_ref.at[own], spread.at[k], chips + k, target * 2 + core)
        copy.start()
        copies.append(copy)
    for copy in copies:
        copy.wait()
    for k in range(1, chips):
        source = lax.rem(chip + chips - k, chips)
        out_ref[pl.ds(pl.multiple_of(core * rows + source * chunk, 8), chunk)] = spread[k]
    copy = remote(out_ref.at[mine], out_ref.at[mine], 2 * chips, me + 1 - 2 * core)
    copy.start()
    copy.wait()


def shots_sum(value):
    chips = lax.axis_size("shots") // 2
    shape = value.shape
    chunks = value.reshape(-1, 128)
    rows = chunks.shape[0]
    out = pl.pallas_call(
        functools.partial(allreduce_kernel, chips),
        out_shape=jax.ShapeDtypeStruct(chunks.shape, jnp.float32),
        in_specs=[pl.BlockSpec(memory_space=pltpu.VMEM)],
        out_specs=pl.BlockSpec(memory_space=pltpu.VMEM),
        scratch_shapes=[
            pltpu.VMEM((rows // 2, 128), jnp.float32),
            pltpu.VMEM((chips, rows // 2 // chips, 128), jnp.float32),
            pltpu.VMEM((chips, rows // 2 // chips, 128), jnp.float32),
            pltpu.SemaphoreType.DMA((2 * chips + 1,)),
            pltpu.SemaphoreType.DMA((2 * chips + 1,)),
        ],
        compiler_params=pltpu.CompilerParams(collective_id=0, has_side_effects=True),
    )(chunks)
    return out.reshape(shape)


def per_device(
    src_prev,
    src_cur,
    rcv_prev,
    rcv_cur,
    velocity,
    wavelet,
    residual_traces,
    source_depth,
    source_y,
    source_x,
    half_y,
    half_x,
    receiver_cell,
):
    shot_count, depth, rows_y, cols_x = src_cur.shape
    start = lax.axis_index("slab") * depth
    mask = band_mask(source_y, source_x, half_y, half_x, rows_y, cols_x)[:, None]
    row0, col0 = band_corner(source_y, source_x, half_y, half_x, rows_y, cols_x)
    pick_y, pick_x = selectors(row0, col0, rows_y, cols_x)
    terms = []
    up, u, vp, v = (src_prev, src_cur, rcv_prev, rcv_cur)
    for step in range(STEPS):
        stacked = jnp.stack([u, v])
        padded = extended(stacked, pick_y, pick_x, 4, 1 + step)
        lap = laplace(padded)
        sdelta = point_field(
            source_depth - start, source_y, source_x, wavelet[step], depth, rows_y, cols_x
        )
        rdelta = receiver_field(receiver_cell, residual_traces[step], start, depth, rows_y, cols_x)
        unew = mask * (2.0 * u - up + velocity * lap[0] + sdelta)
        vnew = mask * (2.0 * v - vp + velocity * lap[1] + rdelta)
        terms.append(jnp.sum((unew - 2.0 * u + up) * vnew, axis=0))
        up, u, vp, v = (u, unew, v, vnew)
    src_last, rcv_last = (u, v)
    local_sum = terms[0]
    for extra in terms[1:]:
        local_sum = local_sum + extra
    image = shots_sum(local_sum)
    return (src_last, rcv_last, image)


def solution(mesh):
    return jax.shard_map(
        per_device,
        mesh=mesh,
        in_specs=(
            P("shots", "slab", None, None),
            P("shots", "slab", None, None),
            P("shots", "slab", None, None),
            P("shots", "slab", None, None),
            P("slab", None, None),
            P(None, "shots"),
            P(None, "shots", None),
            P("shots"),
            P("shots"),
            P("shots"),
            P("shots"),
            P("shots"),
            P("shots", None),
        ),
        out_specs=(
            P("shots", "slab", None, None),
            P("shots", "slab", None, None),
            P("slab", None, None),
        ),
        check_vma=False,
    )
```

```python
import jax
import jax.numpy as jnp
from jax import lax
from jax.sharding import PartitionSpec as P
from jax.experimental import pallas as pl
from jax.experimental.pallas import tpu as pltpu
import functools

STEPS = 2


COEF = (-205.0 / 72.0, 8.0 / 5.0, -1.0 / 5.0, 8.0 / 315.0, -1.0 / 560.0)


WIN_Y = 44
WIN_X = 88


def band_corner(source_y, source_x, half_y, half_x, rows_y, cols_x):
    row0 = jnp.clip(source_y - half_y, 0, rows_y - WIN_Y)
    col0 = jnp.clip(source_x - half_x, 0, cols_x - WIN_X)
    return row0, col0


def selectors(row0, col0, rows_y, cols_x):
    pick_y = (
        jnp.arange(rows_y, dtype=jnp.int32)[None, :, None]
        == row0[:, None, None] + jnp.arange(WIN_Y, dtype=jnp.int32)[None, None, :]
    ).astype(jnp.float32)
    pick_x = (
        jnp.arange(cols_x, dtype=jnp.int32)[None, None, :]
        == col0[:, None, None] + jnp.arange(WIN_X, dtype=jnp.int32)[None, :, None]
    ).astype(jnp.float32)
    return pick_y, pick_x


def exact_einsum(spec, a, b):
    return jnp.einsum(
        spec, a, b, precision=lax.Precision.HIGHEST, preferred_element_type=jnp.float32
    )


def cut_windows(layers, pick_y, pick_x):
    fields, shots, width = layers.shape[:3]
    part = exact_einsum("fsjyx,sbx->fsjyb", layers, pick_x)
    part = exact_einsum("sya,fsjyb->fsjab", pick_y, part)
    return part.reshape(fields, shots, -1, 128)


def paste_windows(flat, pick_y, pick_x, width):
    fields, shots = flat.shape[:2]
    part = flat.reshape(fields, shots, width, WIN_Y, WIN_X)
    part = exact_einsum("fsjab,sbx->fsjax", part, pick_x)
    return exact_einsum("sya,fsjax->fsjyx", pick_y, part)


def halo_kernel(n, send_ref, recv_ref, sems):
    i = lax.axis_index("slab")
    shot = lax.axis_index("shots")
    mesh_id = pl.DeviceIdType.MESH
    has_up = i + 1 < n
    has_down = i >= 1
    barrier = pltpu.get_barrier_semaphore()

    @pl.when(has_up)
    def _():
        pl.semaphore_signal(barrier, inc=1, device_id=(i + 1, shot), device_id_type=mesh_id)

    @pl.when(has_down)
    def _():
        pl.semaphore_signal(barrier, inc=1, device_id=(i - 1, shot), device_id_type=mesh_id)

    pl.semaphore_wait(barrier, has_up.astype(jnp.int32) + has_down.astype(jnp.int32))

    def remote(side, target):
        return pltpu.make_async_remote_copy(
            src_ref=send_ref.at[side],
            dst_ref=recv_ref.at[side],
            send_sem=sems.at[side],
            recv_sem=sems.at[2 + side],
            device_id=(target, shot),
            device_id_type=mesh_id,
        )

    @pl.when(has_up)
    def _():
        remote(0, i + 1).start()

    @pl.when(has_down)
    def _():
        remote(1, i - 1).start()

    @pl.when(has_up)
    def _():
        remote(0, i + 1).wait_send()
        remote(1, i).wait_recv()

    @pl.when(has_down)
    def _():
        remote(1, i - 1).wait_send()
        remote(0, i).wait_recv()


def exchange(both, call_id):
    n = lax.axis_size("slab")
    shape = both.shape
    total = both[0].size // 128
    vmem = pl.BlockSpec(memory_space=pl.ANY)
    recv = pl.pallas_call(
        functools.partial(halo_kernel, n),
        out_shape=jax.ShapeDtypeStruct((2, total, 128), jnp.float32),
        in_specs=[vmem],
        out_specs=vmem,
        scratch_shapes=[pltpu.SemaphoreType.DMA((4,))],
        compiler_params=pltpu.CompilerParams(collective_id=call_id, has_side_effects=True),
    )(both.reshape(2, total, 128))
    return recv.reshape(shape)


def extended(block, pick_y, pick_x, width, call_id):
    dim = 2
    sides = jnp.stack(
        [
            lax.slice_in_dim(block, block.shape[dim] - width, None, axis=dim),
            lax.slice_in_dim(block, 0, width, axis=dim),
        ]
    )
    part = exact_einsum("zfsjyx,sbx->zfsjyb", sides, pick_x)
    part = exact_einsum("sya,zfsjyb->zfsjab", pick_y, part)
    got = exchange(part, call_id)
    i = lax.axis_index("slab")
    present = jnp.stack([i >= 1, i + 1 < lax.axis_size("slab")])
    got = jnp.where(present[:, None, None, None, None, None], got, 0.0)
    got = exact_einsum("zfsjab,sbx->zfsjax", got, pick_x)
    got = exact_einsum("sya,zfsjax->zfsjyx", pick_y, got)
    return jnp.concatenate([got[0], block, got[1]], axis=dim)


def laplace(padded):
    axis_z = padded.ndim - 3
    length = padded.shape[axis_z] - 8
    center = lax.slice_in_dim(padded, 4, 4 + length, axis=axis_z)
    total = 3.0 * COEF[0] * center
    for shift_k in range(1, 5):
        upper = lax.slice_in_dim(padded, 4 + shift_k, 4 + shift_k + length, axis=axis_z)
        lower = lax.slice_in_dim(padded, 4 - shift_k, 4 - shift_k + length, axis=axis_z)
        total = total + COEF[shift_k] * (upper + lower)
    widths = [(0, 0)] * (center.ndim - 2) + [(4, 4), (4, 4)]
    plane = jnp.pad(center, widths)
    rows_y = center.shape[-2]
    cols_x = center.shape[-1]
    for shift_k in range(1, 5):
        side_y = (
            plane[..., 4 + shift_k : 4 + shift_k + rows_y, 4 : 4 + cols_x]
            + plane[..., 4 - shift_k : 4 - shift_k + rows_y, 4 : 4 + cols_x]
        )
        side_x = (
            plane[..., 4 : 4 + rows_y, 4 + shift_k : 4 + shift_k + cols_x]
            + plane[..., 4 : 4 + rows_y, 4 - shift_k : 4 - shift_k + cols_x]
        )
        total = total + COEF[shift_k] * (side_y + side_x)
    return total


def band_mask(source_y, source_x, half_y, half_x, rows_y, cols_x):
    grid_y = jnp.arange(rows_y, dtype=jnp.int32)
    grid_x = jnp.arange(cols_x, dtype=jnp.int32)
    inside_y = jnp.abs(grid_y[None, :, None] - source_y[:, None, None]) <= half_y[:, None, None]
    inside_x = jnp.abs(grid_x[None, None, :] - source_x[:, None, None]) <= half_x[:, None, None]
    return (inside_y & inside_x).astype(jnp.float32)


def point_field(depth_local, row, col, values, length, rows_y, cols_x):
    grid_z = jnp.arange(length, dtype=jnp.int32)[None, :, None, None]
    grid_y = jnp.arange(rows_y, dtype=jnp.int32)[None, None, :, None]
    grid_x = jnp.arange(cols_x, dtype=jnp.int32)[None, None, None, :]
    hit = (
        (grid_z == depth_local[:, None, None, None])
        & (grid_y == row[:, None, None, None])
        & (grid_x == col[:, None, None, None])
    )
    return jnp.where(hit, values[:, None, None, None], 0.0)


def receiver_field(cells, traces, begin, length, rows_y, cols_x):
    plane = rows_y * cols_x
    depth = cells // plane
    rest = cells - depth * plane
    row = rest // cols_x
    col = rest - row * cols_x
    local = depth - begin
    slab_rows = jnp.arange(length * rows_y, dtype=jnp.int32)
    key = local * rows_y + row
    left = jnp.where(slab_rows[None, :, None] == key[:, None, :], traces[:, None, :], 0.0)
    right = (col[:, :, None] == jnp.arange(cols_x, dtype=jnp.int32)[None, None, :]).astype(
        jnp.float32
    )
    field = jnp.einsum(
        "szr,srx->szx",
        left,
        right,
        precision=lax.Precision.HIGHEST,
        preferred_element_type=jnp.float32,
    )
    return field.reshape(cells.shape[0], length, rows_y, cols_x)


def tree_sum(value, axis):
    count = lax.axis_size(axis)
    me = lax.axis_index(axis)
    shape = value.shape
    piece = value.reshape(-1)
    bits = []
    stride = 1
    while stride < count:
        bits.append(stride)
        stride *= 2
    for stride in bits:
        upper = (me // stride) % 2 == 1
        halves = piece.reshape(2, -1)
        send = jnp.where(upper, halves[0], halves[1])
        keep = jnp.where(upper, halves[1], halves[0])
        pairs = [(i, i ^ stride) for i in range(count)]
        piece = keep + lax.ppermute(send, axis, pairs)
    for stride in reversed(bits):
        upper = (me // stride) % 2 == 1
        pairs = [(i, i ^ stride) for i in range(count)]
        other = lax.ppermute(piece, axis, pairs)
        piece = jnp.where(upper, jnp.concatenate([other, piece]), jnp.concatenate([piece, other]))
    return piece.reshape(shape)


def allreduce_kernel(chips, local_ref, out_ref, half_in, own_half, gathered, spread, send_sems, recv_sems, local_sem):
    me = lax.axis_index("shots")
    slab = lax.axis_index("slab")
    core = me % 2
    chip = me // 2
    mesh_id = pl.DeviceIdType.MESH
    rows = local_ref.shape[0] // 2
    chunk = rows // chips
    barrier = pltpu.get_barrier_semaphore()
    pl.semaphore_signal(barrier, inc=1, device_id=(slab, me + 1 - 2 * core), device_id_type=mesh_id)
    for k in range(1, chips):
        peer = lax.rem(chip + k, chips) * 2 + core
        pl.semaphore_signal(barrier, inc=1, device_id=(slab, peer), device_id_type=mesh_id)
    pl.semaphore_wait(barrier, chips)

    def remote(src, dst, slot, target):
        return pltpu.make_async_remote_copy(
            src_ref=src,
            dst_ref=dst,
            send_sem=send_sems.at[slot],
            recv_sem=recv_sems.at[slot],
            device_id=(slab, target),
            device_id_type=mesh_id,
        )

    mine = pl.ds(pl.multiple_of(core * rows, 8), rows)
    theirs = pl.ds(pl.multiple_of((1 - core) * rows, 8), rows)
    fetch = pltpu.make_async_copy(local_ref.at[mine], own_half, local_sem)
    fetch.start()
    copy = remote(local_ref.at[theirs], half_in, 0, me + 1 - 2 * core)
    copy.start()
    fetch.wait()
    copy.wait()
    out_ref[mine] = own_half[...] + half_in[...]
    copies = []
    for k in range(1, chips):
        target = lax.rem(chip + k, chips)
        src = out_ref.at[pl.ds(pl.multiple_of(core * rows + target * chunk, 8), chunk)]
        copy = remote(src, gathered.at[k], k, target * 2 + core)
        copy.start()
        copies.append(copy)
    for copy in copies:
        copy.wait()
    own = pl.ds(pl.multiple_of(core * rows + chip * chunk, 8), chunk)
    total = out_ref[own]
    for k in range(1, chips):
        total = total + gathered[k]
    out_ref[own] = total
    copies = []
    for k in range(1, chips):
        target = lax.rem(chip + k, chips)
        copy = remote(out_ref.at[own], spread.at[k], chips + k, target * 2 + core)
        copy.start()
        copies.append(copy)
    for copy in copies:
        copy.wait()
    for k in range(1, chips):
        source = lax.rem(chip + chips - k, chips)
        out_ref[pl.ds(pl.multiple_of(core * rows + source * chunk, 8), chunk)] = spread[k]
    copy = remote(out_ref.at[mine], out_ref.at[mine], 2 * chips, me + 1 - 2 * core)
    copy.start()
    copy.wait()


def shots_sum(value):
    chips = lax.axis_size("shots") // 2
    shape = value.shape
    chunks = value.reshape(-1, 128)
    rows = chunks.shape[0]
    out = pl.pallas_call(
        functools.partial(allreduce_kernel, chips),
        out_shape=jax.ShapeDtypeStruct(chunks.shape, jnp.float32),
        in_specs=[pl.BlockSpec(memory_space=pl.ANY)],
        out_specs=pl.BlockSpec(memory_space=pltpu.VMEM),
        scratch_shapes=[
            pltpu.VMEM((rows // 2, 128), jnp.float32),
            pltpu.VMEM((rows // 2, 128), jnp.float32),
            pltpu.VMEM((chips, rows // 2 // chips, 128), jnp.float32),
            pltpu.VMEM((chips, rows // 2 // chips, 128), jnp.float32),
            pltpu.SemaphoreType.DMA((2 * chips + 1,)),
            pltpu.SemaphoreType.DMA((2 * chips + 1,)),
            pltpu.SemaphoreType.DMA(()),
        ],
        compiler_params=pltpu.CompilerParams(collective_id=0, has_side_effects=True),
    )(chunks)
    return out.reshape(shape)


def per_device(
    src_prev,
    src_cur,
    rcv_prev,
    rcv_cur,
    velocity,
    wavelet,
    residual_traces,
    source_depth,
    source_y,
    source_x,
    half_y,
    half_x,
    receiver_cell,
):
    shot_count, depth, rows_y, cols_x = src_cur.shape
    start = lax.axis_index("slab") * depth
    mask = band_mask(source_y, source_x, half_y, half_x, rows_y, cols_x)[:, None]
    row0, col0 = band_corner(source_y, source_x, half_y, half_x, rows_y, cols_x)
    pick_y, pick_x = selectors(row0, col0, rows_y, cols_x)
    terms = []
    up, u, vp, v = (src_prev, src_cur, rcv_prev, rcv_cur)
    for step in range(STEPS):
        stacked = jnp.stack([u, v])
        padded = extended(stacked, pick_y, pick_x, 4, 1 + step)
        lap = laplace(padded)
        sdelta = point_field(
            source_depth - start, source_y, source_x, wavelet[step], depth, rows_y, cols_x
        )
        rdelta = receiver_field(receiver_cell, residual_traces[step], start, depth, rows_y, cols_x)
        unew = mask * (2.0 * u - up + velocity * lap[0] + sdelta)
        vnew = mask * (2.0 * v - vp + velocity * lap[1] + rdelta)
        terms.append(jnp.sum((unew - 2.0 * u + up) * vnew, axis=0))
        up, u, vp, v = (u, unew, v, vnew)
    src_last, rcv_last = (u, v)
    local_sum = terms[0]
    for extra in terms[1:]:
        local_sum = local_sum + extra
    image = shots_sum(local_sum)
    return (src_last, rcv_last, image)


def solution(mesh):
    return jax.shard_map(
        per_device,
        mesh=mesh,
        in_specs=(
            P("shots", "slab", None, None),
            P("shots", "slab", None, None),
            P("shots", "slab", None, None),
            P("shots", "slab", None, None),
            P("slab", None, None),
            P(None, "shots"),
            P(None, "shots", None),
            P("shots"),
            P("shots"),
            P("shots"),
            P("shots"),
            P("shots"),
            P("shots", None),
        ),
        out_specs=(
            P("shots", "slab", None, None),
            P("shots", "slab", None, None),
            P("slab", None, None),
        ),
        check_vma=False,
    )
```
